128 devices in a mesh: seq: 128 (over x, y, z, core).
Axes of the slice: x: 4, y: 4, z: 4, core: 2. Of those that a mesh axis runs over, the one named last changes fastest.
Arguments:
- inputs: bfloat16 [2, 32768, 1536], P(None, 'seq'), may hold values from -8 to 8
- ln_gain: float32 [1536], replicated, may hold values from 0.25 to 1.75
- w_in: bfloat16 [1536, 3072], replicated, may hold values from -0.15625 to 0.15625
- kernel: float32 [32, 1536], replicated, may hold values from -1 to 1
- bn_gain: float32 [1536], replicated, may hold values from 0.25 to 1.75
- bn_bias: float32 [1536], replicated, may hold values from -0.6 to 0.6
- w_out: bfloat16 [1536, 1536], replicated, may hold values from -0.15625 to 0.15625
- cotangent: bfloat16 [2, 32768, 1536], P(None, 'seq'), may hold values from -24 to 24
Outputs:
- outputs: bfloat16 [2, 32768, 1536], P(None, 'seq')
- d_inputs: bfloat16 [2, 32768, 1536], P(None, 'seq')
- d_w_out: float32 [1536, 1536], P('seq')
- d_kernel: float32 [32, 1536], replicated
- d_bn_gain: float32 [1536], replicated
- d_bn_bias: float32 [1536], replicated
The draws below stay inside these ranges and needn't reach their ends.
All inputs are finite; a program needn't handle non-finite values.
Results may differ from the reference program's by a relative error of at most 0.0075.
Values may be sent and summed in bfloat16 or wider, within the bound.
A program may use at most 128 MiB of HBM per device.

```python
import math
import jax
import jax.numpy as jnp
from jax import lax

D = 1536
K = 32
UTT = 2
FRAMES = 32768


def draw_inputs(key, part):
    noise_key = jax.random.fold_in(key, 11)
    along_key = jax.random.fold_in(key, 23)
    position = jnp.arange(FRAMES, dtype=jnp.float32) / FRAMES
    direction = jax.random.normal(along_key, (UTT, 1, D), jnp.float32)
    noise = jax.random.normal(noise_key, (UTT, FRAMES, D), jnp.float32)
    amplitude = 0.3 * jnp.power(5.0, position)
    result = noise + amplitude[None, :, None] * direction
    return jnp.clip(result, -8.0, 8.0).astype(jnp.bfloat16)


def spiked(values, own_key, source, target, parts, factor):
    def block_of(dim):
        return (jnp.arange(values.shape[dim]) // (values.shape[dim] // parts)).reshape((-1,) + (1,) * (values.ndim - 1 - dim))

    near = jax.random.permutation(own_key, parts)[block_of(target)]
    other_side = (block_of(target) + parts // 2) % parts
    return jnp.where((block_of(source) == near) | (block_of(source) == other_side), factor * values, values)


def shard_levels(own_key, shape, shards, least, top_value):
    def one(dim, parts):
        steps = jax.random.uniform(jax.random.fold_in(jax.random.fold_in(own_key, 6), dim), (parts,), jnp.float32, least / len(shards), top_value / len(shards))
        return jnp.repeat(jnp.exp(steps), shape[dim] // parts).reshape((-1,) + (1,) * (len(shape) - dim - 1))

    level = one(*shards[0])
    for cut in shards[1:]:
        level = level * one(*cut)
    return level


def scatter_about(own_key, dims, scale, limit, split=(), kind=jnp.bfloat16):
    values = scale * jax.random.normal(own_key, dims, jnp.float32)
    if split:
        values = values * shard_levels(own_key, dims, split, -0.22, 0.18)
    return jnp.clip(values, -limit, limit).astype(kind)


def heavy_noise(own_key, extent, deviation, reach, split, heavy, held_as=jnp.bfloat16):
    drawn = deviation * jax.random.normal(own_key, extent, jnp.float32)
    if split:
        drawn = drawn * shard_levels(own_key, extent, split, -0.22, 0.18)
    return jnp.clip(spiked(drawn, jax.random.fold_in(own_key, 3), *heavy), -reach, reach).astype(held_as)


def setup_inputs(seed: int = 0) -> dict:
    splits = jax.random.split(jax.random.key(seed), 9)
    inputs = draw_inputs(jax.random.fold_in(splits[8], 71), 0)
    ln_gain = jnp.clip(1.0 + 0.15 * jax.random.normal(splits[1], (D,), jnp.float32), 0.25, 1.75)
    w_in = scatter_about(splits[2], (D, 2 * D), D ** -0.5, 0.15625)
    kernel = scatter_about(splits[3], (K, D), K ** -0.5, 1.0, (), jnp.float32)
    bn_gain = jnp.clip(1.0 + 0.15 * jax.random.normal(splits[4], (D,), jnp.float32), 0.25, 1.75)
    bn_bias = jnp.clip(jax.random.uniform(splits[5], (D,), jnp.float32, -0.6, 0.6), -0.6, 0.6)
    w_out = scatter_about(splits[6], (D, D), D ** -0.5, 0.15625)
    cotangent = heavy_noise(splits[7], (UTT, FRAMES, D), 1.0, 24.0, ((1, 128),), (1, 2, 128, 5.5))
    return {"inputs": inputs, "ln_gain": ln_gain, "w_in": w_in, "kernel": kernel, "bn_gain": bn_gain, "bn_bias": bn_bias, "w_out": w_out, "cotangent": cotangent}


EPSILON = 1e-05

def frame_slice(array, utt_index, start, length):
    zero = jnp.zeros((), jnp.int32)
    piece = lax.dynamic_slice(array, (utt_index.astype(jnp.int32), start.astype(jnp.int32), zero), (1, length, array.shape[2]))
    return piece[0]

def layer_norm(x_float):
    ln_mean = lax.optimization_barrier(jnp.mean(x_float, axis=-1, keepdims=True))
    centred = x_float - ln_mean
    ln_rstd = lax.rsqrt(lax.optimization_barrier(jnp.mean(centred * centred, axis=-1, keepdims=True)) + EPSILON)
    return (centred * ln_rstd, ln_rstd)

def reference(inputs, ln_gain, w_in, kernel, bn_gain, bn_bias, w_out, cotangent):
    block_len = math.gcd(FRAMES, 1024)
    per_utt = FRAMES // block_len
    block_ids = jnp.arange(UTT * per_utt, dtype=jnp.int32)
    frame_total = UTT * FRAMES

    def locate(index):
        utt_index = index // per_utt
        start = index % per_utt * block_len
        return (utt_index, start)

    def front(index):
        utt_index, start = locate(index)
        x_float = frame_slice(inputs, utt_index, start, block_len).astype(jnp.float32)
        ln_hat, ln_rstd = layer_norm(x_float)
        normed = (ln_hat * ln_gain).astype(jnp.bfloat16)
        proj = jnp.dot(normed, w_in, preferred_element_type=jnp.float32)
        value_half = proj[:, :D]
        gate_sig = jax.nn.sigmoid(proj[:, D:])
        return (x_float, ln_hat, ln_rstd, value_half, gate_sig)

    def make_gated(index):
        x_float, ln_hat, ln_rstd, value_half, gate_sig = front(index)
        return (value_half * gate_sig).astype(jnp.bfloat16)
    gated = lax.map(make_gated, block_ids).reshape(UTT, FRAMES, D)
    padded = jnp.pad(gated, ((0, 0), (16, 16), (0, 0)))

    def conv_block(index):
        utt_index, start = locate(index)
        window = frame_slice(padded, utt_index, start, block_len + 32).astype(jnp.float32)
        conv_out = jnp.zeros((block_len, D), jnp.float32)
        for tap_index in range(K):
            conv_out = conv_out + kernel[tap_index] * window[tap_index + 1:tap_index + 1 + block_len]
        return (conv_out, window)
    sums = lax.map(lambda index: lax.optimization_barrier(jnp.sum(conv_block(index)[0], axis=0)), block_ids)
    bn_mean = lax.optimization_barrier(jnp.sum(sums, axis=0)) / frame_total

    def spread(index):
        deviate = conv_block(index)[0] - bn_mean
        return lax.optimization_barrier(jnp.sum(deviate * deviate, axis=0))
    bn_var = lax.optimization_barrier(jnp.sum(lax.map(spread, block_ids), axis=0)) / frame_total
    bn_rstd = lax.rsqrt(bn_var + EPSILON)

    def bn_forward(index):
        conv_out, window = conv_block(index)
        normed_bn = (conv_out - bn_mean) * bn_rstd
        bn_out = normed_bn * bn_gain + bn_bias
        return (normed_bn, bn_out, window)

    def tail_step(carry, index):
        weight_acc, bias_acc, gain_acc = carry
        utt_index, start = locate(index)
        normed_bn, bn_out, window = bn_forward(index)
        act_sig = jax.nn.sigmoid(bn_out)
        act = (bn_out * act_sig).astype(jnp.bfloat16)
        x_float = frame_slice(inputs, utt_index, start, block_len).astype(jnp.float32)
        branch = lax.dot_general(act, w_out, (((1,), (1,)), ((), ())), preferred_element_type=jnp.float32)
        out_block = (x_float + branch).astype(jnp.bfloat16)
        cot_rows = frame_slice(cotangent, utt_index, start, block_len)
        d_act = jnp.dot(cot_rows, w_out, preferred_element_type=jnp.float32)
        weight_acc = weight_acc + lax.dot_general(cot_rows, act, (((0,), (0,)), ((), ())), preferred_element_type=jnp.float32)
        d_bn = d_act * (act_sig + bn_out * act_sig * (1.0 - act_sig))
        bias_acc = bias_acc + lax.optimization_barrier(jnp.sum(d_bn, axis=0))
        gain_acc = gain_acc + lax.optimization_barrier(jnp.sum(d_bn * normed_bn, axis=0))
        return ((weight_acc, bias_acc, gain_acc), (out_block, d_bn))
    start_carry = (jnp.zeros((D, D), jnp.float32), jnp.zeros((D,), jnp.float32), jnp.zeros((D,), jnp.float32))
    (d_w_out, d_bn_bias, d_bn_gain), (out_blocks, d_bn_blocks) = lax.scan(tail_step, start_carry, block_ids)
    outputs = out_blocks.reshape(UTT, FRAMES, D)
    mean_grad = bn_gain * d_bn_bias / frame_total
    mean_cross = bn_gain * d_bn_gain / frame_total

    def make_dconv(pair):
        index, d_bn = pair
        normed_bn, bn_out, window = bn_forward(index)
        return bn_rstd * (d_bn * bn_gain - mean_grad - normed_bn * mean_cross)
    d_conv_blocks = lax.map(make_dconv, (block_ids, d_bn_blocks))
    grad_padded = jnp.pad(d_conv_blocks.reshape(UTT, FRAMES, D), ((0, 0), (16, 16), (0, 0)))

    def back_step(kernel_acc, pair):
        index, d_conv = pair
        utt_index, start = locate(index)
        window = frame_slice(padded, utt_index, start, block_len + 32).astype(jnp.float32)
        kernel_rows = []
        for tap_index in range(K):
            kernel_rows.append(lax.optimization_barrier(jnp.sum(window[tap_index + 1:tap_index + 1 + block_len] * d_conv, axis=0)))
        kernel_acc = kernel_acc + jnp.stack(kernel_rows)
        grad_window = frame_slice(grad_padded, utt_index, start, block_len + 32)
        d_gated = jnp.zeros((block_len, D), jnp.float32)
        for tap_index in range(K):
            d_gated = d_gated + kernel[tap_index] * grad_window[31 - tap_index:31 - tap_index + block_len]
        x_float, ln_hat, ln_rstd, value_half, gate_sig = front(index)
        d_value = d_gated * gate_sig
        d_gate = d_gated * value_half * gate_sig * (1.0 - gate_sig)
        d_proj = jnp.concatenate([d_value, d_gate], axis=-1).astype(jnp.bfloat16)
        d_normed = lax.dot_general(d_proj, w_in, (((1,), (1,)), ((), ())), preferred_element_type=jnp.float32)
        d_hat = d_normed * ln_gain
        d_layer = ln_rstd * (d_hat - lax.optimization_barrier(jnp.mean(d_hat, axis=-1, keepdims=True)) - ln_hat * lax.optimization_barrier(jnp.mean(d_hat * ln_hat, axis=-1, keepdims=True)))
        cot_float = frame_slice(cotangent, utt_index, start, block_len).astype(jnp.float32)
        return (kernel_acc, (cot_float + d_layer).astype(jnp.bfloat16))
    d_kernel, grad_blocks = lax.scan(back_step, jnp.zeros((K, D), jnp.float32), (block_ids, d_conv_blocks))
    d_inputs = grad_blocks.reshape(UTT, FRAMES, D)
    return (outputs, d_inputs, d_w_out, d_kernel, d_bn_gain, d_bn_bias)
```

```python
import functools
import jax
import jax.numpy as jnp
from jax import lax
from jax.experimental import pallas as pl
from jax.experimental.pallas import tpu as pltpu
from jax.sharding import PartitionSpec as P

D = 1536
K = 32
FRAMES_DEV = 256
UTT = 2
EPSILON = 1e-05
F32 = jnp.float32
BF16 = jnp.bfloat16
STRIDE = {"core": 1, "z": 2, "y": 8, "x": 32}
SIZE = {"core": 2, "z": 4, "y": 4, "x": 4}
ORDERS = (("x", "y", "z"), ("y", "z", "x"), ("z", "x", "y"))
HALF = D // 2


def coord(me, axis):
    return lax.rem(me // STRIDE[axis], SIZE[axis])


def peers(me, axis):
    q = coord(me, axis)
    found = []
    for delta in range(1, SIZE[axis]):
        other = lax.rem(q + delta, SIZE[axis])
        found.append((other, me + (other - q) * STRIDE[axis]))
    return found


class Net:
    def __init__(self, me, send_sem, recv_sem):
        self.me, self.send_sem, self.recv_sem, self.used = me, send_sem, recv_sem, 0
        self.started = []

    def send(self, src, dst, device):
        slot = self.used
        self.used += 1
        copy = pltpu.make_async_remote_copy(
            src_ref=src,
            dst_ref=dst,
            send_sem=self.send_sem.at[slot],
            recv_sem=self.recv_sem.at[slot],
            device_id=(device,),
            device_id_type=pl.DeviceIdType.MESH,
        )
        copy.start()
        self.started.append(copy)
        return copy

    def drain(self):
        for copy in self.started:
            copy.wait_send()


def greet(me, axes, extra=()):
    barrier = pltpu.get_barrier_semaphore()
    count = 0
    for axis in axes:
        for _, device in peers(me, axis):
            pl.semaphore_signal(
                barrier, inc=1, device_id=(device,), device_id_type=pl.DeviceIdType.MESH
            )
            count += 1
    for device in extra:
        pl.semaphore_signal(
            barrier, inc=1, device_id=(device,), device_id_type=pl.DeviceIdType.MESH
        )
        count += 1
    pl.semaphore_wait(barrier, count)


AXES = ("core", "z", "y", "x")


def merge_stats(parts, rows):
    mean = functools.reduce(jnp.add, [p[0:1] for p in parts]) * (1.0 / len(parts))
    spread = functools.reduce(jnp.add, [p[1:2] for p in parts])
    for p in parts:
        gap = p[0:1] - mean
        spread = spread + rows * gap * gap
    return jnp.concatenate([mean, spread], axis=0)


def reduce_kernel(merge, x_ref, o_ref, cur, got, send_sem, recv_sem):
    me = lax.axis_index("seq")
    greet(me, AXES)
    net = Net(me, send_sem, recv_sem)
    value = x_ref[...]
    rows = UTT * FRAMES_DEV
    slot = 0
    for level, axis in enumerate(AXES):
        cur[level] = value
        copies = []
        for _, device in peers(me, axis):
            copies.append((net.send(cur.at[level], got.at[slot], device), slot))
            slot += 1
        parts = [value]
        for copy, index in copies:
            copy.wait_recv()
            parts.append(got[index])
        if merge:
            value = merge_stats(parts, float(rows))
        else:
            value = functools.reduce(jnp.add, parts)
        rows *= SIZE[axis]
    o_ref[...] = value
    net.drain()


def reduce_small(x, merge, collective_id):
    return pl.pallas_call(
        functools.partial(reduce_kernel, merge),
        out_shape=jax.ShapeDtypeStruct((2, D), F32),
        in_specs=[pl.BlockSpec(memory_space=pltpu.VMEM)],
        out_specs=pl.BlockSpec(memory_space=pltpu.VMEM),
        scratch_shapes=[
            pltpu.VMEM((4, 2, D), F32),
            pltpu.VMEM((10, 2, D), F32),
            pltpu.SemaphoreType.DMA((10,)),
            pltpu.SemaphoreType.DMA((10,)),
        ],
        compiler_params=pltpu.CompilerParams(collective_id=collective_id, has_side_effects=True),
    )(x)


class DKernel:
    def __init__(self, net, src, core_buf, got_core, got_x, cz, got_z, cy, got_y, full, other):
        self.net = net
        self.src, self.core_buf, self.got_core = src, core_buf, got_core
        self.got_x, self.cz, self.got_z = got_x, cz, got_z
        self.cy, self.got_y, self.full, self.other = cy, got_y, full, other

    def start(self):
        me = self.net.me
        core = coord(me, "core")
        self.c0 = [self.net.send(self.src.at[1 - core], self.got_core, me + 1 - 2 * core)]

    def to_x(self):
        me = self.net.me
        core = coord(me, "core")
        x = coord(me, "x")
        self.c0[0].wait_recv()
        self.core_buf[...] = self.src[core] + self.got_core[...]
        self.cx_c = [
            self.net.send(self.core_buf.at[other], self.got_x.at[i], device)
            for i, (other, device) in enumerate(peers(me, "x"))
        ]

    def to_z(self):
        me = self.net.me
        total = self.core_buf[coord(me, "x")]
        for i, copy in enumerate(self.cx_c):
            copy.wait_recv()
            total = total + self.got_x[i]
        self.cz[...] = total
        self.cz_c = [
            self.net.send(self.cz, self.got_z.at[i], device)
            for i, (_, device) in enumerate(peers(me, "z"))
        ]

    def to_y(self):
        me = self.net.me
        total = self.cz[...]
        for i, copy in enumerate(self.cz_c):
            copy.wait_recv()
            total = total + self.got_z[i]
        self.cy[...] = total
        self.cy_c = [
            self.net.send(self.cy, self.got_y.at[i], device)
            for i, (_, device) in enumerate(peers(me, "y"))
        ]

    def gather_x(self):
        me = self.net.me
        total = self.cy[...]
        for i, copy in enumerate(self.cy_c):
            copy.wait_recv()
            total = total + self.got_y[i]
        x = coord(me, "x")
        self.full[x] = total
        self.gx_c = [
            self.net.send(self.full.at[x], self.full.at[x], device)
            for _, device in peers(me, "x")
        ]

    def gather_core(self):
        me = self.net.me
        core = coord(me, "core")
        for copy in self.gx_c:
            copy.wait_recv()
        self.gc_c = self.net.send(self.full, self.other, me + 1 - 2 * core)

    def finish(self, out):
        core = coord(self.net.me, "core")
        self.gc_c.wait_recv()
        for i in range(4):
            mine = self.full[i]
            theirs = self.other[i]
            out[pl.ds(8 * i, 8), 0:HALF] = jnp.where(core == 0, mine, theirs)
            out[pl.ds(8 * i, 8), HALF:D] = jnp.where(core == 0, theirs, mine)


DK_SCRATCH = [
    pltpu.VMEM((4, 8, HALF), F32),
    pltpu.VMEM((4, 8, HALF), F32),
    pltpu.VMEM((3, 8, HALF), F32),
    pltpu.VMEM((8, HALF), F32),
    pltpu.VMEM((3, 8, HALF), F32),
    pltpu.VMEM((8, HALF), F32),
    pltpu.VMEM((3, 8, HALF), F32),
    pltpu.VMEM((4, 8, HALF), F32),
    pltpu.VMEM((4, 8, HALF), F32),
]


def pick(ref, dims, axis, index):
    where = dims.index(axis)
    if where == 0:
        return ref.at[index]
    if where == 1:
        return ref.at[:, index]
    return ref.at[:, :, index]


class Scatter:
    def __init__(self, net, src, got_core, s1, got1, s2, got2, s3, got3, tail, got_tail):
        self.net, self.src, self.got_core = net, src, got_core
        self.s = [s1, s2, s3]
        self.got = [got1, got2, got3]
        self.tail, self.got_tail = tail, got_tail

    def start(self, part):
        me = self.net.me
        core = coord(me, "core")
        return self.net.send(self.src.at[1 - core, part], self.got_core.at[part], me + 1 - 2 * core)

    def dims(self, part, level):
        gone = ORDERS[part][:level]
        return [a for a in ("x", "y", "z") if a not in gone]

    def add_core(self, part, copy):
        core = coord(self.net.me, "core")
        copy.wait_recv()

        def body(i, carry):
            x, y = i // 4, lax.rem(i, 4)
            mine = self.src[core, part, x, y].astype(F32)
            theirs = self.got_core[part, x, y].astype(F32)
            self.s[0][part, x, y] = (mine + theirs).astype(BF16)
            return carry

        lax.fori_loop(0, 16, body, 0)

    def send_level(self, part, level):
        me = self.net.me
        axis = ORDERS[part][level]
        dims = self.dims(part, level)
        return [
            self.net.send(
                pick(self.s[level].at[part], dims, axis, other),
                self.got[level].at[part, i],
                device,
            )
            for i, (other, device) in enumerate(peers(me, axis))
        ]

    def add_level(self, part, level, copies):
        me = self.net.me
        axis = ORDERS[part][level]
        dims = self.dims(part, level)
        own = pick(self.s[level].at[part], dims, axis, coord(me, axis))
        for copy in copies:
            copy.wait_recv()
        got = self.got[level].at[part]
        if level == 2:
            total = own[...].astype(F32)
            for i in range(3):
                total = total + got[i].astype(F32)
            return total
        for a in range(4):
            total = own[a].astype(F32)
            for i in range(3):
                total = total + got[i, a].astype(F32)
            self.s[level + 1][part, a] = total.astype(BF16)

    def exchange(self, totals):
        core = coord(self.net.me, "core")
        self.mine = []
        for part in range(3):
            for half in range(2):
                low = totals[part][half * 24 : half * 24 + 12]
                high = totals[part][half * 24 + 12 : half * 24 + 24]
                self.mine.append(jnp.where(core == 0, low, high))
                self.tail[part * 2 + half] = jnp.where(core == 0, high, low)
        self.copy = self.net.send(self.tail, self.got_tail, self.net.me + 1 - 2 * core)

    def finish(self, out):
        core = coord(self.net.me, "core")
        self.copy.wait_recv()
        for piece in range(6):
            mine = self.mine[piece]
            theirs = self.got_tail[piece]
            out[:, piece * 128 : piece * 128 + 128] = jnp.where(core == 0, mine, theirs)
            out[:, HALF + piece * 128 : HALF + piece * 128 + 128] = jnp.where(core == 0, theirs, mine)


RS_SCRATCH = [
    pltpu.VMEM((3, 4, 4, 4, 48, 128), BF16),
    pltpu.VMEM((3, 4, 4, 4, 48, 128), BF16),
    pltpu.VMEM((3, 3, 4, 4, 48, 128), BF16),
    pltpu.VMEM((3, 4, 4, 48, 128), BF16),
    pltpu.VMEM((3, 3, 4, 48, 128), BF16),
    pltpu.VMEM((3, 4, 48, 128), BF16),
    pltpu.VMEM((3, 3, 48, 128), BF16),
    pltpu.VMEM((6, 12, 128), F32),
    pltpu.VMEM((6, 12, 128), F32),
]


def scatter_kernel(p_ref, dk_ref, dw_ref, dk_out, *scratch):
    send_sem, recv_sem = scratch[-2:]
    me = lax.axis_index("seq")
    greet(me, AXES)
    net = Net(me, send_sem, recv_sem)
    rs = Scatter(net, p_ref, *scratch[: len(RS_SCRATCH)])
    dk = DKernel(net, dk_ref, *scratch[len(RS_SCRATCH) : -2])
    dk.start()
    firsts = [rs.start(part) for part in range(3)]
    dk.to_x()
    levels = []
    for part in range(3):
        rs.add_core(part, firsts[part])
        levels.append(rs.send_level(part, 0))
    dk.to_z()
    for level in range(2):
        nexts = []
        for part in range(3):
            rs.add_level(part, level, levels[part])
            nexts.append(rs.send_level(part, level + 1))
        levels = nexts
        if level == 0:
            dk.to_y()
        else:
            dk.gather_x()
    totals = [rs.add_level(part, 2, levels[part]) for part in range(3)]
    rs.exchange(totals)
    dk.gather_core()
    rs.finish(dw_ref)
    dk.finish(dk_out)
    net.drain()


def scatter_all(partial, dk):
    return pl.pallas_call(
        scatter_kernel,
        out_shape=(jax.ShapeDtypeStruct((D // 128, D), F32), jax.ShapeDtypeStruct((K, D), F32)),
        in_specs=[pl.BlockSpec(memory_space=pltpu.VMEM)] * 2,
        out_specs=[pl.BlockSpec(memory_space=pltpu.VMEM)] * 2,
        scratch_shapes=RS_SCRATCH
        + DK_SCRATCH
        + [
            pltpu.SemaphoreType.DMA((48,)),
            pltpu.SemaphoreType.DMA((48,)),
        ],
        compiler_params=pltpu.CompilerParams(
            collective_id=2, has_side_effects=True, vmem_limit_bytes=60 * 1024 * 1024
        ),
    )(partial, dk)


def with_halo(block, sides, width):
    for axis, dim in sides:
        count = lax.axis_size(axis)
        forward = [(i, i + 1) for i in range(count - 1)]
        backward = [(target, source) for source, target in forward]
        low = lax.ppermute(
            lax.slice_in_dim(block, block.shape[dim] - width, None, axis=dim), axis, forward
        )
        high = lax.ppermute(lax.slice_in_dim(block, 0, width, axis=dim), axis, backward)
        block = jnp.concatenate([low, block, high], axis=dim)
    return block


def on_device(inputs, ln_gain, w_in, kernel, bn_gain, bn_bias, w_out, cotangent):
    devices_seq = lax.axis_size("seq")
    frame_total = UTT * FRAMES_DEV * devices_seq
    rows_here = UTT * FRAMES_DEV
    x_float = inputs.astype(jnp.float32)
    ln_mean = jnp.mean(x_float, axis=-1, keepdims=True)
    centred = x_float - ln_mean
    ln_rstd = lax.rsqrt(jnp.mean(centred * centred, axis=-1, keepdims=True) + EPSILON)
    ln_hat = centred * ln_rstd
    normed = (ln_hat * ln_gain).astype(jnp.bfloat16).reshape(rows_here, D)
    proj = jnp.dot(normed, w_in, preferred_element_type=jnp.float32)
    value_half = proj[:, :D]
    gate_sig = jax.nn.sigmoid(proj[:, D:])
    gated = (value_half * gate_sig).astype(jnp.bfloat16).reshape(UTT, FRAMES_DEV, D)
    padded = with_halo(gated, (("seq", 1),), 16)
    conv_out = jnp.zeros((UTT, FRAMES_DEV, D), jnp.float32)
    for tap_index in range(K):
        conv_out = conv_out + kernel[tap_index] * padded[
            :, tap_index + 1 : tap_index + 1 + FRAMES_DEV
        ].astype(jnp.float32)
    here_mean = jnp.mean(conv_out, axis=(0, 1))
    here_gap = conv_out - here_mean
    here_spread = jnp.sum(here_gap * here_gap, axis=(0, 1))
    stats = reduce_small(jnp.stack([here_mean, here_spread]), True, 0)
    bn_mean = stats[0]
    deviate = conv_out - bn_mean
    bn_var = stats[1] / frame_total
    bn_rstd = lax.rsqrt(bn_var + EPSILON)
    normed_bn = deviate * bn_rstd
    bn_out = normed_bn * bn_gain + bn_bias
    act_sig = jax.nn.sigmoid(bn_out)
    act = (bn_out * act_sig).astype(jnp.bfloat16).reshape(rows_here, D)
    branch = lax.dot_general(
        act, w_out, (((1,), (1,)), ((), ())), preferred_element_type=jnp.float32
    )
    outputs = (
        (x_float.reshape(rows_here, D) + branch).astype(jnp.bfloat16).reshape(UTT, FRAMES_DEV, D)
    )
    cot_rows = cotangent.reshape(rows_here, D)
    partial = lax.dot_general(
        cot_rows, act, (((0,), (0,)), ((), ())), preferred_element_type=jnp.float32
    ).astype(jnp.bfloat16)
    partial = partial.reshape(64, 24, 2, 3, 2, 128).transpose(2, 3, 0, 4, 1, 5)
    partial = partial.reshape(2, 3, 4, 4, 4, 48, 128)
    d_act = jnp.dot(cot_rows, w_out, preferred_element_type=jnp.float32)
    d_bn = d_act.reshape(UTT, FRAMES_DEV, D) * (act_sig + bn_out * act_sig * (1.0 - act_sig))
    scaled_grad = d_bn * bn_gain
    local_bias = jnp.sum(d_bn, axis=(0, 1))
    local_gain = jnp.sum(d_bn * normed_bn, axis=(0, 1))
    sums = reduce_small(jnp.stack([local_bias, local_gain]), False, 1)
    d_bn_bias, d_bn_gain = sums[0], sums[1]
    mean_grad = bn_gain * d_bn_bias / frame_total
    mean_cross = bn_gain * d_bn_gain / frame_total
    d_conv = bn_rstd * (scaled_grad - mean_grad - normed_bn * mean_cross)
    kernel_rows = []
    for tap_index in range(K):
        window = padded[:, tap_index + 1 : tap_index + 1 + FRAMES_DEV].astype(jnp.float32)
        kernel_rows.append(jnp.sum(window * d_conv, axis=(0, 1)))
    d_kernel = jnp.stack(kernel_rows)
    d_kernel = d_kernel.reshape(4, 8, 2, HALF).transpose(2, 0, 1, 3)
    grad_padded = with_halo(d_conv.astype(jnp.bfloat16), (("seq", 1),), 16).astype(d_conv.dtype)
    d_gated = jnp.zeros((UTT, FRAMES_DEV, D), jnp.float32)
    for tap_index in range(K):
        d_gated = (
            d_gated
            + kernel[tap_index] * grad_padded[:, 31 - tap_index : 31 - tap_index + FRAMES_DEV]
        )
    d_gated = d_gated.reshape(rows_here, D)
    d_value = d_gated * gate_sig
    d_gate = d_gated * value_half * gate_sig * (1.0 - gate_sig)
    d_proj = jnp.concatenate([d_value, d_gate], axis=-1).astype(jnp.bfloat16)
    d_normed = lax.dot_general(
        d_proj, w_in, (((1,), (1,)), ((), ())), preferred_element_type=jnp.float32
    )
    d_hat = d_normed.reshape(UTT, FRAMES_DEV, D) * ln_gain
    d_layer = ln_rstd * (
        d_hat
        - jnp.mean(d_hat, axis=-1, keepdims=True)
        - ln_hat * jnp.mean(d_hat * ln_hat, axis=-1, keepdims=True)
    )
    d_inputs = (cotangent.astype(jnp.float32) + d_layer).astype(jnp.bfloat16)
    d_w_out, d_kernel = scatter_all(partial, d_kernel)
    return (outputs, d_inputs, d_w_out, d_kernel, d_bn_gain, d_bn_bias)


def solution(mesh):
    return jax.shard_map(
        on_device,
        mesh=mesh,
        in_specs=(P(None, "seq", None), P(), P(), P(), P(), P(), P(), P(None, "seq", None)),
        out_specs=(P(None, "seq", None), P(None, "seq", None), P("seq", None), P(), P(), P()),
        check_vma=False,
    )
```

```python
import functools
import jax
import jax.numpy as jnp
from jax import lax
from jax.experimental import pallas as pl
from jax.experimental.pallas import tpu as pltpu
from jax.sharding import PartitionSpec as P

D = 1536
K = 32
FRAMES_DEV = 256
UTT = 2
EPSILON = 1e-05
F32 = jnp.float32
BF16 = jnp.bfloat16
STRIDE = {"core": 1, "z": 2, "y": 8, "x": 32}
SIZE = {"core": 2, "z": 4, "y": 4, "x": 4}
ORDERS = (("x", "y", "z"), ("y", "z", "x"), ("z", "x", "y"))
HALF = D // 2


def coord(me, axis):
    return lax.rem(me // STRIDE[axis], SIZE[axis])


def peers(me, axis):
    q = coord(me, axis)
    found = []
    for delta in range(1, SIZE[axis]):
        other = lax.rem(q + delta, SIZE[axis])
        found.append((other, me + (other - q) * STRIDE[axis]))
    return found


class Net:
    def __init__(self, me, send_sem, recv_sem):
        self.me, self.send_sem, self.recv_sem, self.used = me, send_sem, recv_sem, 0
        self.started = []

    def send(self, src, dst, device):
        slot = self.used
        self.used += 1
        copy = pltpu.make_async_remote_copy(
            src_ref=src,
            dst_ref=dst,
            send_sem=self.send_sem.at[slot],
            recv_sem=self.recv_sem.at[slot],
            device_id=(device,),
            device_id_type=pl.DeviceIdType.MESH,
        )
        copy.start()
        self.started.append(copy)
        return copy

    def drain(self):
        for copy in self.started:
            copy.wait_send()


def greet(me, axes, extra=()):
    barrier = pltpu.get_barrier_semaphore()
    count = 0
    for axis in axes:
        for _, device in peers(me, axis):
            pl.semaphore_signal(
                barrier, inc=1, device_id=(device,), device_id_type=pl.DeviceIdType.MESH
            )
            count += 1
    for device in extra:
        pl.semaphore_signal(
            barrier, inc=1, device_id=(device,), device_id_type=pl.DeviceIdType.MESH
        )
        count += 1
    pl.semaphore_wait(barrier, count)


AXES = ("core", "z", "y", "x")


def merge_stats(parts, rows):
    mean = functools.reduce(jnp.add, [p[0:1] for p in parts]) * (1.0 / len(parts))
    spread = functools.reduce(jnp.add, [p[1:2] for p in parts])
    for p in parts:
        gap = p[0:1] - mean
        spread = spread + rows * gap * gap
    return jnp.concatenate([mean, spread], axis=0)


class DKernel:
    def __init__(self, net, src, core_buf, got_core, got_x, cz, got_z, cy, got_y, full, other):
        self.net = net
        self.src, self.core_buf, self.got_core = src, core_buf, got_core
        self.got_x, self.cz, self.got_z = got_x, cz, got_z
        self.cy, self.got_y, self.full, self.other = cy, got_y, full, other

    def start(self):
        me = self.net.me
        core = coord(me, "core")
        self.c0 = [self.net.send(self.src.at[1 - core], self.got_core, me + 1 - 2 * core)]

    def to_x(self):
        me = self.net.me
        core = coord(me, "core")
        x = coord(me, "x")
        self.c0[0].wait_recv()
        self.core_buf[...] = self.src[core] + self.got_core[...]
        self.cx_c = [
            self.net.send(self.core_buf.at[other], self.got_x.at[i], device)
            for i, (other, device) in enumerate(peers(me, "x"))
        ]

    def to_z(self):
        me = self.net.me
        total = self.core_buf[coord(me, "x")]
        for i, copy in enumerate(self.cx_c):
            copy.wait_recv()
            total = total + self.got_x[i]
        self.cz[...] = total
        self.cz_c = [
            self.net.send(self.cz, self.got_z.at[i], device)
            for i, (_, device) in enumerate(peers(me, "z"))
        ]

    def to_y(self):
        me = self.net.me
        total = self.cz[...]
        for i, copy in enumerate(self.cz_c):
            copy.wait_recv()
            total = total + self.got_z[i]
        self.cy[...] = total
        self.cy_c = [
            self.net.send(self.cy, self.got_y.at[i], device)
            for i, (_, device) in enumerate(peers(me, "y"))
        ]

    def gather_x(self):
        me = self.net.me
        total = self.cy[...]
        for i, copy in enumerate(self.cy_c):
            copy.wait_recv()
            total = total + self.got_y[i]
        x = coord(me, "x")
        self.full[x] = total
        self.gx_c = [
            self.net.send(self.full.at[x], self.full.at[x], device)
            for _, device in peers(me, "x")
        ]

    def gather_core(self):
        me = self.net.me
        core = coord(me, "core")
        for copy in self.gx_c:
            copy.wait_recv()
        self.gc_c = self.net.send(self.full, self.other, me + 1 - 2 * core)

    def finish(self, out):
        core = coord(self.net.me, "core")
        self.gc_c.wait_recv()
        for i in range(4):
            mine = self.full[i]
            theirs = self.other[i]
            out[pl.ds(8 * i, 8), 0:HALF] = jnp.where(core == 0, mine, theirs)
            out[pl.ds(8 * i, 8), HALF:D] = jnp.where(core == 0, theirs, mine)


DK_SCRATCH = [
    pltpu.VMEM((4, 8, HALF), F32),
    pltpu.VMEM((4, 8, HALF), F32),
    pltpu.VMEM((3, 8, HALF), F32),
    pltpu.VMEM((8, HALF), F32),
    pltpu.VMEM((3, 8, HALF), F32),
    pltpu.VMEM((8, HALF), F32),
    pltpu.VMEM((3, 8, HALF), F32),
    pltpu.VMEM((4, 8, HALF), F32),
    pltpu.VMEM((4, 8, HALF), F32),
]


def pick(ref, dims, axis, index):
    where = dims.index(axis)
    if where == 0:
        return ref.at[index]
    if where == 1:
        return ref.at[:, index]
    return ref.at[:, :, index]


class Scatter:
    def __init__(self, net, src, got_core, s1, got1, s2, got2, s3, got3, tail, got_tail):
        self.net, self.src, self.got_core = net, src, got_core
        self.s = [s1, s2, s3]
        self.got = [got1, got2, got3]
        self.tail, self.got_tail = tail, got_tail

    def start(self, part):
        me = self.net.me
        core = coord(me, "core")
        return self.net.send(self.src.at[1 - core, part], self.got_core.at[part], me + 1 - 2 * core)

    def dims(self, part, level):
        gone = ORDERS[part][:level]
        return [a for a in ("x", "y", "z") if a not in gone]

    def add_core(self, part, copy):
        core = coord(self.net.me, "core")
        copy.wait_recv()

        def body(i, carry):
            x, y = i // 4, lax.rem(i, 4)
            mine = self.src[core, part, x, y].astype(F32)
            theirs = self.got_core[part, x, y].astype(F32)
            self.s[0][part, x, y] = (mine + theirs).astype(BF16)
            return carry

        lax.fori_loop(0, 16, body, 0)

    def send_level(self, part, level):
        me = self.net.me
        axis = ORDERS[part][level]
        dims = self.dims(part, level)
        return [
            self.net.send(
                pick(self.s[level].at[part], dims, axis, other),
                self.got[level].at[part, i],
                device,
            )
            for i, (other, device) in enumerate(peers(me, axis))
        ]

    def add_level(self, part, level, copies):
        me = self.net.me
        axis = ORDERS[part][level]
        dims = self.dims(part, level)
        own = pick(self.s[level].at[part], dims, axis, coord(me, axis))
        for copy in copies:
            copy.wait_recv()
        got = self.got[level].at[part]
        if level == 2:
            total = own[...].astype(F32)
            for i in range(3):
                total = total + got[i].astype(F32)
            return total
        for a in range(4):
            total = own[a].astype(F32)
            for i in range(3):
                total = total + got[i, a].astype(F32)
            self.s[level + 1][part, a] = total.astype(BF16)

    def exchange(self, totals):
        core = coord(self.net.me, "core")
        self.mine = []
        for part in range(3):
            for half in range(2):
                low = totals[part][half * 24 : half * 24 + 12]
                high = totals[part][half * 24 + 12 : half * 24 + 24]
                self.mine.append(jnp.where(core == 0, low, high))
                self.tail[part * 2 + half] = jnp.where(core == 0, high, low)
        self.copy = self.net.send(self.tail, self.got_tail, self.net.me + 1 - 2 * core)

    def finish(self, out):
        core = coord(self.net.me, "core")
        self.copy.wait_recv()
        for piece in range(6):
            mine = self.mine[piece]
            theirs = self.got_tail[piece]
            out[:, piece * 128 : piece * 128 + 128] = jnp.where(core == 0, mine, theirs)
            out[:, HALF + piece * 128 : HALF + piece * 128 + 128] = jnp.where(core == 0, theirs, mine)


RS_SCRATCH = [
    pltpu.VMEM((3, 4, 4, 4, 48, 128), BF16),
    pltpu.VMEM((3, 4, 4, 4, 48, 128), BF16),
    pltpu.VMEM((3, 3, 4, 4, 48, 128), BF16),
    pltpu.VMEM((3, 4, 4, 48, 128), BF16),
    pltpu.VMEM((3, 3, 4, 48, 128), BF16),
    pltpu.VMEM((3, 4, 48, 128), BF16),
    pltpu.VMEM((3, 3, 48, 128), BF16),
    pltpu.VMEM((6, 12, 128), F32),
    pltpu.VMEM((6, 12, 128), F32),
]


class Reduce:
    def __init__(self, net, merge, cur, got):
        self.net, self.merge, self.cur, self.got = net, merge, cur, got
        self.rows, self.level, self.slot = float(UTT * FRAMES_DEV), 0, 0

    def start(self, value):
        self.value = value
        self.cur[self.level] = value
        self.copies = []
        for _, device in peers(self.net.me, AXES[self.level]):
            self.copies.append(
                (self.net.send(self.cur.at[self.level], self.got.at[self.slot], device), self.slot)
            )
            self.slot += 1

    def take(self):
        parts = [self.value]
        for copy, index in self.copies:
            copy.wait_recv()
            parts.append(self.got[index])
        if self.merge:
            value = merge_stats(parts, self.rows)
        else:
            value = functools.reduce(jnp.add, parts)
        self.rows *= SIZE[AXES[self.level]]
        self.level += 1
        return value

    def step(self):
        self.start(self.take())


ROWS = UTT * FRAMES_DEV
CHUNK = 256
CHUNKS = D // CHUNK
HALO = 16
OWN = HALO * 8


def dot(a, b):
    return jnp.dot(a, b, preferred_element_type=F32)


def dot_t(a, b):
    return lax.dot_general(a, b, (((1,), (1,)), ((), ())), preferred_element_type=F32)


def span(index, size):
    return pl.ds(pl.multiple_of(index * size, size), size)


def frame_of(row):
    return (row & 7) * 32 + (row >> 3)


def fold(x):
    return jnp.sum(x.reshape(x.shape[0] // 8, 8, x.shape[1]), axis=0)


class Halo:
    def __init__(self, me, devices, out, got, send_sem, recv_sem):
        self.out, self.got, self.send_sem, self.recv_sem = out, got, send_sem, recv_sem
        self.right = lax.rem(me + 1, devices)
        self.left = lax.rem(me + devices - 1, devices)

    def copies(self, c):
        return [
            pltpu.make_async_remote_copy(
                src_ref=self.out.at[c, way],
                dst_ref=self.got.at[c, way],
                send_sem=self.send_sem.at[c, way],
                recv_sem=self.recv_sem.at[c, way],
                device_id=(device,),
                device_id_type=pl.DeviceIdType.MESH,
            )
            for way, device in enumerate((self.right, self.left))
        ]

    def push(self, c, select, blocks):
        for u in range(UTT):
            edge = dot(select[...], blocks[u]).astype(BF16)
            self.out[c, 0, u] = edge[0:HALO]
            self.out[c, 1, u] = edge[HALO : 2 * HALO]
        for copy in self.copies(c):
            copy.start()

    def wait(self, c):
        for copy in self.copies(c):
            copy.wait_recv()

    def drain(self):
        for c in range(CHUNKS):
            for copy in self.copies(c):
                copy.wait_send()


def extend(ext, u, cols, low, high, row_id):
    for j in range(HALO):
        below = pltpu.roll(ext[u, OWN + (16 + j) * 8 : OWN + (17 + j) * 8, cols], 1, 0)
        ext[u, j * 8 : j * 8 + 8, cols] = jnp.where(row_id == 0, low[j : j + 1], below)
        above = pltpu.roll(ext[u, OWN + j * 8 : OWN + j * 8 + 8, cols], 7, 0)
        ext[u, (48 + j) * 8 : (49 + j) * 8, cols] = jnp.where(row_id == 7, high[j : j + 1], above)


def convolve(ext, u, cols, taps, forward):
    for base in range(0, 32, 8):
        acc = [None] * 8
        reach = range(base + 1, base + 40) if forward else range(base, base + 39)
        for e in reach:
            x = ext[u, e * 8 : e * 8 + 8, cols]
            for o in range(8):
                k = e - (base + o) - 1 if forward else base + o + 31 - e
                if 0 <= k < K:
                    term = taps[k] * x
                    acc[o] = term if acc[o] is None else acc[o] + term
        yield base, acc


def whole_kernel(n_dev, x_hbm, lng_ref, win_hbm, ker_ref, bng_ref, bnb_ref, wout_hbm, cot_hbm,
                 out_hbm, din_hbm, dw_ref, dk_ref, dbn_ref, *scratch):
    s = dict(zip([name for name, _ in SCRATCH], scratch))
    me = lax.axis_index("seq")
    local = s["local_sem"]
    loads = [
        pltpu.make_async_copy(x_hbm, s["x_raw"], local.at[0]),
        pltpu.make_async_copy(win_hbm, s["w_in"], local.at[1]),
        pltpu.make_async_copy(cot_hbm, s["cot_raw"], local.at[2]),
        pltpu.make_async_copy(wout_hbm, s["w_out"], local.at[3]),
    ]
    for load in loads:
        load.start()
    net = Net(me, s["send_sem"], s["recv_sem"])
    halo1 = Halo(me, n_dev, s["h_out1"], s["h_got1"], s["h_send1"], s["h_recv1"])
    halo2 = Halo(me, n_dev, s["h_out2"], s["h_got2"], s["h_send2"], s["h_recv2"])

    perm, perm_t, eye, select = s["perm"], s["perm_t"], s["eye"], s["select"]
    r0 = lax.broadcasted_iota(jnp.int32, (256, 256), 0)
    r1 = lax.broadcasted_iota(jnp.int32, (256, 256), 1)
    perm[...] = jnp.where(frame_of(r0) == r1, 1.0, 0.0).astype(BF16)
    perm_t[...] = jnp.where(frame_of(r1) == r0, 1.0, 0.0).astype(BF16)
    eye[...] = jnp.where(r0 == r1, 1.0, 0.0).astype(BF16)
    q0 = lax.broadcasted_iota(jnp.int32, (32, 256), 0)
    q1 = lax.broadcasted_iota(jnp.int32, (32, 256), 1)
    edge_frame = jnp.where(q0 < HALO, FRAMES_DEV - HALO + q0, q0 - HALO)
    select[...] = jnp.where(frame_of(q1) == edge_frame, 1.0, 0.0).astype(BF16)
    row_id = lax.broadcasted_iota(jnp.int32, (8, 128), 0)

    x_p, normed, mu_ref, rstd_ref = s["x_p"], s["bf"], s["mu"], s["rstd"]
    loads[0].wait()

    def norm_tile(i, carry):
        u, part = i // 4, lax.rem(i, 4)
        rows = span(i, 64)
        x = dot(perm[span(part, 64), :], s["x_raw"][u])
        x_p[rows, :] = x.astype(BF16)
        mean = jnp.mean(x, axis=-1, keepdims=True)
        gap = x - mean
        rstd = lax.rsqrt(jnp.mean(gap * gap, axis=-1, keepdims=True) + EPSILON)
        mu_ref[rows, :] = mean
        rstd_ref[rows, :] = rstd
        normed[rows, :] = (gap * rstd * lng_ref[...]).astype(BF16)
        return carry

    lax.fori_loop(0, 8, norm_tile, 0)
    greet(me, AXES, (halo1.left, halo1.right))
    loads[1].wait()
    w_in, val, gs, ext_g, ext_d = s["w_in"], s["val"], s["gs"], s["ext_g"], s["ext_d"]

    def project(c, carry):
        cols = span(c, CHUNK)
        val[:, cols] = dot(normed[...], w_in[:, cols])
        gate_cols = pl.ds(pl.multiple_of(D + c * CHUNK, CHUNK), CHUNK)
        gs[:, cols] = dot(normed[...], w_in[:, gate_cols])
        blocks = []
        for u in range(UTT):
            rows = pl.ds(u * 256, 256)
            sig = jax.nn.sigmoid(gs[rows, cols])
            gs[rows, cols] = sig
            gated = (val[rows, cols] * sig).astype(BF16)
            ext_g[u, OWN : OWN + 256, cols] = gated.astype(F32)
            blocks.append(gated)
        halo1.push(c, select, blocks)
        return carry

    lax.fori_loop(0, CHUNKS, project, 0)

    def halo_rows(halo, c, u, lane):
        low = halo.got[c, 0, u, :, lane : lane + 128].astype(F32)
        high = halo.got[c, 1, u, :, lane : lane + 128].astype(F32)
        return jnp.where(me == 0, 0.0, low), jnp.where(me == n_dev - 1, 0.0, high)

    conv, stat = s["conv"], s["stat"]

    def taps_of(cols):
        return [jnp.broadcast_to(ker_ref[k : k + 1, cols], (8, 128)) for k in range(K)]

    def conv_chunk(c, carry):
        halo1.wait(c)
        for half in range(2):
            cols = pl.ds(pl.multiple_of(c * CHUNK + half * 128, 128), 128)
            taps = taps_of(cols)
            total = jnp.zeros((8, 128), F32)
            for u in range(UTT):
                low, high = halo_rows(halo1, c, u, half * 128)
                extend(ext_g, u, cols, low, high, row_id)
                for base, acc in convolve(ext_g, u, cols, taps, True):
                    for o in range(8):
                        conv[pl.ds(u * 256 + (base + o) * 8, 8), cols] = acc[o]
                        total = total + acc[o]
            mean = jnp.sum(total, axis=0, keepdims=True) * (1.0 / ROWS)
            gap = conv[:, cols] - mean
            stat[0:1, cols] = mean
            stat[1:2, cols] = jnp.sum(fold(gap * gap), axis=0, keepdims=True)
        return carry

    lax.fori_loop(0, CHUNKS, conv_chunk, 0)

    ar1 = Reduce(net, True, s["cur1"], s["ar1"])
    ar1.start(stat[...])
    loads[2].wait()
    cot_p, cot_t, w_out = s["cot_p"], s["cot_t"], s["w_out"]

    def turn(c, carry):
        cols = span(c, CHUNK)
        for u in range(UTT):
            cot_p[u * 256 : u * 256 + 256, cols] = dot(perm[...], s["cot_raw"][u, :, cols]).astype(BF16)
        cot_t[cols, :] = dot_t(eye[...], cot_p[:, cols]).astype(BF16)
        return carry

    lax.fori_loop(0, CHUNKS, turn, 0)
    ar1.step()
    loads[3].wait()

    def act_grad(c, carry):
        cols = span(c, CHUNK)
        res = dot(cot_p[...], w_out[:, cols])
        for u in range(UTT):
            ext_d[u, OWN : OWN + 256, cols] = res[u * 256 : u * 256 + 256]
        return carry

    lax.fori_loop(0, CHUNKS // 2, act_grad, 0)
    ar1.step()
    lax.fori_loop(CHUNKS // 2, CHUNKS, act_grad, 0)
    ar1.step()
    stats = ar1.take()
    total_rows = float(ROWS * n_dev)
    coef = s["coef"]
    coef[0:1, :] = stats[0:1]
    coef[1:2, :] = lax.rsqrt(stats[1:2] * (1.0 / total_rows) + EPSILON)
    act = s["bf"]

    def bn_block(cb, carry):
        cols = span(cb, 128)
        mean, rstd = coef[0:1, cols], coef[1:2, cols]
        gain, bias = bng_ref[:, cols], bnb_ref[:, cols]
        sum_bias = jnp.zeros((8, 128), F32)
        sum_gain = jnp.zeros((8, 128), F32)
        for u in range(UTT):
            rows = pl.ds(u * 256, 256)
            xhat = (conv[rows, cols] - mean) * rstd
            bn = xhat * gain + bias
            sig = jax.nn.sigmoid(bn)
            conv[rows, cols] = xhat
            act[rows, cols] = (bn * sig).astype(BF16)
            d_bn = ext_d[u, OWN : OWN + 256, cols] * (sig + bn * sig * (1.0 - sig))
            ext_d[u, OWN : OWN + 256, cols] = d_bn
            sum_bias = sum_bias + fold(d_bn)
            sum_gain = sum_gain + fold(d_bn * xhat)
        stat[0:1, cols] = jnp.sum(sum_gain, axis=0, keepdims=True)
        stat[1:2, cols] = jnp.sum(sum_bias, axis=0, keepdims=True)
        return carry

    lax.fori_loop(0, D // 128, bn_block, 0)
    ar2 = Reduce(net, False, s["cur2"], s["ar2"])
    ar2.start(stat[...])

    core = coord(me, "core")
    part_ref = s["part"]
    rs = Scatter(net, part_ref, *[s[name] for name in RS_NAMES])

    def weight_part(h, p):
        cols = pl.ds(pl.multiple_of(h * HALF + p * CHUNK, CHUNK), CHUNK)

        def tile(m, carry):
            res = dot(cot_t[span(m, 192), :], act[:, cols])
            for j in range(8):
                piece = res[j * 24 : j * 24 + 24]
                piece = jnp.concatenate([piece[:, 0:128], piece[:, 128:256]], axis=0).astype(BF16)
                part_ref[h, p, m // 2, lax.rem(m, 2) * 2 + j // 4, j % 4] = piece
            return carry

        lax.fori_loop(0, 8, tile, 0)

    firsts = []
    for p in range(3):
        weight_part(1 - core, p)
        firsts.append(rs.start(p))
    ar2.step()
    saves = []

    def branch(u):
        rows = pl.ds(u * 256, 256)

        def tile(n, carry):
            cols = span(n, CHUNK)
            res = dot_t(act[rows, :], w_out[cols, :])
            res = (x_p[rows, cols].astype(F32) + res).astype(BF16)
            s["x_raw"][u, :, cols] = dot(perm_t[...], res).astype(BF16)
            return carry

        lax.fori_loop(0, CHUNKS, tile, 0)
        copy = pltpu.make_async_copy(s["x_raw"].at[u], out_hbm.at[u], local.at[4 + u])
        copy.start()
        saves.append(copy)

    branch(0)
    ar2.step()
    branch(1)
    ar2.step()
    for p in range(3):
        weight_part(core, p)
    sums = ar2.take()
    dbn_ref[...] = sums
    gain_row = bng_ref[...]
    rstd_row = coef[1:2, :]
    coef[2:3, :] = rstd_row * gain_row
    coef[3:4, :] = rstd_row * (gain_row * sums[1:2] * (1.0 / total_rows))
    coef[4:5, :] = rstd_row * (gain_row * sums[0:1] * (1.0 / total_rows))

    def conv_grad(c, carry):
        cols = span(c, CHUNK)
        blocks = []
        for u in range(UTT):
            d_bn = ext_d[u, OWN : OWN + 256, cols]
            xhat = conv[u * 256 : u * 256 + 256, cols]
            d_conv = d_bn * coef[2:3, cols] - coef[3:4, cols] - xhat * coef[4:5, cols]
            ext_d[u, OWN : OWN + 256, cols] = d_conv
            blocks.append(d_conv.astype(BF16))
        halo2.push(c, select, blocks)
        return carry

    lax.fori_loop(0, CHUNKS, conv_grad, 0)

    levels = []
    for p in range(3):
        rs.add_core(p, firsts[p])
        levels.append(rs.send_level(p, 0))

    dk_src = s["dk_src"]

    def kernel_grad(h):
        def body(n, carry):
            cols = pl.ds(pl.multiple_of(h * HALF + n * 128, 128), 128)
            acc = [jnp.zeros((8, 128), F32)] * K
            for u in range(UTT):
                for base in range(0, 32, 8):
                    grads = [
                        ext_d[u, OWN + (base + o) * 8 : OWN + (base + o) * 8 + 8, cols] for o in range(8)
                    ]
                    for e in range(base + 1, base + 40):
                        x = ext_g[u, e * 8 : e * 8 + 8, cols]
                        for o in range(8):
                            k = e - (base + o) - 1
                            if 0 <= k < K:
                                acc[k] = acc[k] + x * grads[o]
            for k in range(K):
                dk_src[h, k // 8, k % 8 : k % 8 + 1, span(n, 128)] = jnp.sum(acc[k], axis=0, keepdims=True)
            return carry

        lax.fori_loop(0, HALF // 128, body, 0)

    dk = DKernel(net, dk_src, *[s[name] for name in DK_NAMES])
    kernel_grad(1 - core)
    dk.start()
    nexts = []
    for p in range(3):
        rs.add_level(p, 0, levels[p])
        nexts.append(rs.send_level(p, 1))
    kernel_grad(core)
    dk.to_x()
    d_proj = s["d_proj"]

    def input_grad(c, carry):
        halo2.wait(c)
        for half in range(2):
            start = pl.multiple_of(c * CHUNK + half * 128, 128)
            cols = pl.ds(start, 128)
            gate_cols = pl.ds(pl.multiple_of(D + start, 128), 128)
            taps = taps_of(cols)
            for u in range(UTT):
                low, high = halo_rows(halo2, c, u, half * 128)
                extend(ext_d, u, cols, low, high, row_id)
                for base, acc in convolve(ext_d, u, cols, taps, False):
                    rows = pl.ds(u * 256 + base * 8, 64)
                    grad = jnp.concatenate(acc, axis=0)
                    sig = gs[rows, cols]
                    by_sig = grad * sig
                    d_proj[rows, cols] = by_sig.astype(BF16)
                    d_proj[rows, gate_cols] = (by_sig * val[rows, cols] * (1.0 - sig)).astype(BF16)
        return carry

    lax.fori_loop(0, CHUNKS // 2, input_grad, 0)
    levels = nexts
    nexts = []
    for p in range(3):
        rs.add_level(p, 1, levels[p])
        nexts.append(rs.send_level(p, 2))
    dk.to_z()
    lax.fori_loop(CHUNKS // 2, CHUNKS, input_grad, 0)
    rs.exchange([rs.add_level(p, 2, nexts[p]) for p in range(3)])
    dk.to_y()

    def frame_grad(u):
        rows_u = pl.ds(u * 256, 256)

        def tile(n, carry):
            cols = span(n, CHUNK)
            conv[rows_u, cols] = dot_t(d_proj[rows_u, :], w_in[cols, :])
            return carry

        lax.fori_loop(0, CHUNKS, tile, 0)

    def norm_grad(u):
        def tile(i, carry):
            rows = pl.ds(pl.multiple_of(u * 256 + i * 32, 32), 32)
            d_hat = conv[rows, :] * lng_ref[...]
            rstd = rstd_ref[rows, :]
            hat = (x_p[rows, :].astype(F32) - mu_ref[rows, :]) * rstd
            m1 = jnp.mean(d_hat, axis=-1, keepdims=True)
            m2 = jnp.mean(d_hat * hat, axis=-1, keepdims=True)
            grad = rstd * (d_hat - m1 - hat * m2)
            act[rows, :] = (cot_p[rows, :].astype(F32) + grad).astype(BF16)
            return carry

        lax.fori_loop(0, 8, tile, 0)

        def back(n, carry):
            cols = span(n, CHUNK)
            s["cot_raw"][u, :, cols] = dot(perm_t[...], act[u * 256 : u * 256 + 256, cols]).astype(BF16)
            return carry

        lax.fori_loop(0, CHUNKS, back, 0)
        copy = pltpu.make_async_copy(s["cot_raw"].at[u], din_hbm.at[u], local.at[6 + u])
        copy.start()
        saves.append(copy)

    frame_grad(0)
    dk.gather_x()
    norm_grad(0)
    dk.gather_core()
    frame_grad(1)
    rs.finish(dw_ref)
    dk.finish(dk_ref)
    norm_grad(1)
    for copy in saves:
        copy.wait()
    net.drain()
    halo1.drain()
    halo2.drain()


RS_NAMES = ["got_core", "s1", "got1", "s2", "got2", "s3", "got3", "tail", "got_tail"]
DK_NAMES = ["dk%d" % i for i in range(len(DK_SCRATCH))]
VM = pltpu.VMEM
SCRATCH = [
    ("x_raw", VM((UTT, 256, D), BF16)),
    ("w_in", VM((D, 2 * D), BF16)),
    ("cot_raw", VM((UTT, 256, D), BF16)),
    ("w_out", VM((D, D), BF16)),
    ("perm", VM((256, 256), BF16)),
    ("perm_t", VM((256, 256), BF16)),
    ("eye", VM((256, 256), BF16)),
    ("select", VM((32, 256), BF16)),
    ("x_p", VM((ROWS, D), BF16)),
    ("bf", VM((ROWS, D), BF16)),
    ("mu", VM((ROWS, 1), F32)),
    ("rstd", VM((ROWS, 1), F32)),
    ("val", VM((ROWS, D), F32)),
    ("gs", VM((ROWS, D), F32)),
    ("ext_g", VM((UTT, 512, D), F32)),
    ("ext_d", VM((UTT, 512, D), F32)),
    ("conv", VM((ROWS, D), F32)),
    ("stat", VM((2, D), F32)),
    ("coef", VM((8, D), F32)),
    ("cot_p", VM((ROWS, D), BF16)),
    ("cot_t", VM((D, ROWS), BF16)),
    ("d_proj", VM((ROWS, 2 * D), BF16)),
    ("part", VM((2, 3, 4, 4, 4, 48, 128), BF16)),
    ("h_out1", VM((CHUNKS, 2, UTT, HALO, CHUNK), BF16)),
    ("h_got1", VM((CHUNKS, 2, UTT, HALO, CHUNK), BF16)),
    ("h_out2", VM((CHUNKS, 2, UTT, HALO, CHUNK), BF16)),
    ("h_got2", VM((CHUNKS, 2, UTT, HALO, CHUNK), BF16)),
    ("cur1", VM((4, 2, D), F32)),
    ("ar1", VM((10, 2, D), F32)),
    ("cur2", VM((4, 2, D), F32)),
    ("ar2", VM((10, 2, D), F32)),
    ("dk_src", VM((2, 4, 8, HALF), F32)),
]
SCRATCH += list(zip(RS_NAMES, RS_SCRATCH)) + list(zip(DK_NAMES, DK_SCRATCH))
SCRATCH += [
    ("local_sem", pltpu.SemaphoreType.DMA((8,))),
    ("send_sem", pltpu.SemaphoreType.DMA((72,))),
    ("recv_sem", pltpu.SemaphoreType.DMA((72,))),
    ("h_send1", pltpu.SemaphoreType.DMA((CHUNKS, 2))),
    ("h_recv1", pltpu.SemaphoreType.DMA((CHUNKS, 2))),
    ("h_send2", pltpu.SemaphoreType.DMA((CHUNKS, 2))),
    ("h_recv2", pltpu.SemaphoreType.DMA((CHUNKS, 2))),
]


def on_device(inputs, ln_gain, w_in, kernel, bn_gain, bn_bias, w_out, cotangent):
    any_spec = pl.BlockSpec(memory_space=pl.ANY)
    vmem_spec = pl.BlockSpec(memory_space=pltpu.VMEM)
    outputs, d_inputs, d_w_out, d_kernel, d_bn = pl.pallas_call(
        functools.partial(whole_kernel, lax.axis_size("seq")),
        out_shape=(
            jax.ShapeDtypeStruct((UTT, FRAMES_DEV, D), BF16),
            jax.ShapeDtypeStruct((UTT, FRAMES_DEV, D), BF16),
            jax.ShapeDtypeStruct((D // 128, D), F32),
            jax.ShapeDtypeStruct((K, D), F32),
            jax.ShapeDtypeStruct((2, D), F32),
        ),
        in_specs=[any_spec, vmem_spec, any_spec, vmem_spec, vmem_spec, vmem_spec, any_spec, any_spec],
        out_specs=[any_spec, any_spec, vmem_spec, vmem_spec, vmem_spec],
        scratch_shapes=[spec for _, spec in SCRATCH],
        compiler_params=pltpu.CompilerParams(
            collective_id=0, has_side_effects=True, vmem_limit_bytes=67043328
        ),
    )(
        inputs,
        ln_gain.reshape(1, D),
        w_in,
        kernel,
        bn_gain.reshape(1, D),
        bn_bias.reshape(1, D),
        w_out,
        cotangent,
    )
    return (outputs, d_inputs, d_w_out, d_kernel, d_bn[0], d_bn[1])


def solution(mesh):
    return jax.shard_map(
        on_device,
        mesh=mesh,
        in_specs=(P(None, "seq", None), P(), P(), P(), P(), P(), P(), P(None, "seq", None)),
        out_specs=(P(None, "seq", None), P(None, "seq", None), P("seq", None), P(), P(), P()),
        check_vma=False,
    )
```

```python
import functools
import jax
import jax.numpy as jnp
from jax import lax
from jax.experimental import pallas as pl
from jax.experimental.pallas import tpu as pltpu
from jax.sharding import PartitionSpec as P

D = 1536
K = 32
FRAMES_DEV = 256
UTT = 2
EPSILON = 1e-05
F32 = jnp.float32
BF16 = jnp.bfloat16
STRIDE = {"core": 1, "z": 2, "y": 8, "x": 32}
SIZE = {"core": 2, "z": 4, "y": 4, "x": 4}
ORDERS = (("x", "y", "z"), ("y", "z", "x"), ("z", "x", "y"))
HALF = D // 2


def coord(me, axis):
    return lax.rem(me // STRIDE[axis], SIZE[axis])


def peers(me, axis):
    q = coord(me, axis)
    found = []
    for delta in range(1, SIZE[axis]):
        other = lax.rem(q + delta, SIZE[axis])
        found.append((other, me + (other - q) * STRIDE[axis]))
    return found


class Net:
    def __init__(self, me, send_sem, recv_sem):
        self.me, self.send_sem, self.recv_sem, self.used = me, send_sem, recv_sem, 0
        self.started = []

    def send(self, src, dst, device):
        slot = self.used
        self.used += 1
        copy = pltpu.make_async_remote_copy(
            src_ref=src,
            dst_ref=dst,
            send_sem=self.send_sem.at[slot],
            recv_sem=self.recv_sem.at[slot],
            device_id=(device,),
            device_id_type=pl.DeviceIdType.MESH,
        )
        copy.start()
        self.started.append(copy)
        return copy

    def drain(self):
        for copy in self.started:
            copy.wait_send()


def greet(me, axes, extra=()):
    barrier = pltpu.get_barrier_semaphore()
    count = 0
    for axis in axes:
        for _, device in peers(me, axis):
            pl.semaphore_signal(
                barrier, inc=1, device_id=(device,), device_id_type=pl.DeviceIdType.MESH
            )
            count += 1
    for device in extra:
        pl.semaphore_signal(
            barrier, inc=1, device_id=(device,), device_id_type=pl.DeviceIdType.MESH
        )
        count += 1
    pl.semaphore_wait(barrier, count)


AXES = ("core", "z", "y", "x")


def merge_stats(parts, rows):
    mean = functools.reduce(jnp.add, [p[0:1] for p in parts]) * (1.0 / len(parts))
    spread = functools.reduce(jnp.add, [p[1:2] for p in parts])
    for p in parts:
        gap = p[0:1] - mean
        spread = spread + rows * gap * gap
    return jnp.concatenate([mean, spread], axis=0)


class DKernel:
    def __init__(self, net, src, core_buf, got_core, got_x, cz, got_z, cy, got_y, full, other):
        self.net = net
        self.src, self.core_buf, self.got_core = src, core_buf, got_core
        self.got_x, self.cz, self.got_z = got_x, cz, got_z
        self.cy, self.got_y, self.full, self.other = cy, got_y, full, other

    def start(self):
        me = self.net.me
        core = coord(me, "core")
        self.c0 = [self.net.send(self.src.at[1 - core], self.got_core, me + 1 - 2 * core)]

    def to_x(self):
        me = self.net.me
        core = coord(me, "core")
        x = coord(me, "x")
        self.c0[0].wait_recv()
        self.core_buf[...] = self.src[core] + self.got_core[...]
        self.cx_c = [
            self.net.send(self.core_buf.at[other], self.got_x.at[i], device)
            for i, (other, device) in enumerate(peers(me, "x"))
        ]

    def to_z(self):
        me = self.net.me
        total = self.core_buf[coord(me, "x")]
        for i, copy in enumerate(self.cx_c):
            copy.wait_recv()
            total = total + self.got_x[i]
        self.cz[...] = total
        self.cz_c = [
            self.net.send(self.cz, self.got_z.at[i], device)
            for i, (_, device) in enumerate(peers(me, "z"))
        ]

    def to_y(self):
        me = self.net.me
        total = self.cz[...]
        for i, copy in enumerate(self.cz_c):
            copy.wait_recv()
            total = total + self.got_z[i]
        self.cy[...] = total
        self.cy_c = [
            self.net.send(self.cy, self.got_y.at[i], device)
            for i, (_, device) in enumerate(peers(me, "y"))
        ]

    def gather_x(self):
        me = self.net.me
        total = self.cy[...]
        for i, copy in enumerate(self.cy_c):
            copy.wait_recv()
            total = total + self.got_y[i]
        x = coord(me, "x")
        self.full[x] = total
        self.gx_c = [
            self.net.send(self.full.at[x], self.full.at[x], device)
            for _, device in peers(me, "x")
        ]

    def gather_core(self):
        me = self.net.me
        core = coord(me, "core")
        for copy in self.gx_c:
            copy.wait_recv()
        self.gc_c = self.net.send(self.full, self.other, me + 1 - 2 * core)

    def finish(self, out):
        core = coord(self.net.me, "core")
        self.gc_c.wait_recv()
        for i in range(4):
            mine = self.full[i]
            theirs = self.other[i]
            out[pl.ds(8 * i, 8), 0:HALF] = jnp.where(core == 0, mine, theirs)
            out[pl.ds(8 * i, 8), HALF:D] = jnp.where(core == 0, theirs, mine)


DK_SCRATCH = [
    pltpu.VMEM((4, 8, HALF), F32),
    pltpu.VMEM((4, 8, HALF), F32),
    pltpu.VMEM((3, 8, HALF), F32),
    pltpu.VMEM((8, HALF), F32),
    pltpu.VMEM((3, 8, HALF), F32),
    pltpu.VMEM((8, HALF), F32),
    pltpu.VMEM((3, 8, HALF), F32),
    pltpu.VMEM((4, 8, HALF), F32),
    pltpu.VMEM((4, 8, HALF), F32),
]


def pick(ref, dims, axis, index):
    where = dims.index(axis)
    if where == 0:
        return ref.at[index]
    if where == 1:
        return ref.at[:, index]
    return ref.at[:, :, index]


class Scatter:
    def __init__(self, net, src, got_core, s1, got1, s2, got2, s3, got3, tail, got_tail):
        self.net, self.src, self.got_core = net, src, got_core
        self.s = [s1, s2, s3]
        self.got = [got1, got2, got3]
        self.tail, self.got_tail = tail, got_tail

    def start(self, part):
        me = self.net.me
        core = coord(me, "core")
        return self.net.send(self.src.at[1 - core, part], self.got_core.at[part], me + 1 - 2 * core)

    def dims(self, part, level):
        gone = ORDERS[part][:level]
        return [a for a in ("x", "y", "z") if a not in gone]

    def add_core(self, part, copy):
        core = coord(self.net.me, "core")
        copy.wait_recv()

        def body(i, carry):
            x, y = i // 4, lax.rem(i, 4)
            mine = self.src[core, part, x, y].astype(F32)
            theirs = self.got_core[part, x, y].astype(F32)
            self.s[0][part, x, y] = (mine + theirs).astype(BF16)
            return carry

        lax.fori_loop(0, 16, body, 0)

    def send_level(self, part, level):
        me = self.net.me
        axis = ORDERS[part][level]
        dims = self.dims(part, level)
        return [
            self.net.send(
                pick(self.s[level].at[part], dims, axis, other),
                self.got[level].at[part, i],
                device,
            )
            for i, (other, device) in enumerate(peers(me, axis))
        ]

    def add_level(self, part, level, copies):
        me = self.net.me
        axis = ORDERS[part][level]
        dims = self.dims(part, level)
        own = pick(self.s[level].at[part], dims, axis, coord(me, axis))
        for copy in copies:
            copy.wait_recv()
        got = self.got[level].at[part]
        if level == 2:
            total = own[...].astype(F32)
            for i in range(3):
                total = total + got[i].astype(F32)
            return total
        for a in range(4):
            total = own[a].astype(F32)
            for i in range(3):
                total = total + got[i, a].astype(F32)
            self.s[level + 1][part, a] = total.astype(BF16)

    def exchange(self, totals):
        core = coord(self.net.me, "core")
        self.mine = []
        for part in range(3):
            for half in range(2):
                low = totals[part][half * 24 : half * 24 + 12]
                high = totals[part][half * 24 + 12 : half * 24 + 24]
                self.mine.append(jnp.where(core == 0, low, high))
                self.tail[part * 2 + half] = jnp.where(core == 0, high, low)
        self.copy = self.net.send(self.tail, self.got_tail, self.net.me + 1 - 2 * core)

    def finish(self, out):
        core = coord(self.net.me, "core")
        self.copy.wait_recv()
        for piece in range(6):
            mine = self.mine[piece]
            theirs = self.got_tail[piece]
            out[:, piece * 128 : piece * 128 + 128] = jnp.where(core == 0, mine, theirs)
            out[:, HALF + piece * 128 : HALF + piece * 128 + 128] = jnp.where(core == 0, theirs, mine)


RS_SCRATCH = [
    pltpu.VMEM((3, 4, 4, 4, 48, 128), BF16),
    pltpu.VMEM((3, 4, 4, 4, 48, 128), BF16),
    pltpu.VMEM((3, 3, 4, 4, 48, 128), BF16),
    pltpu.VMEM((3, 4, 4, 48, 128), BF16),
    pltpu.VMEM((3, 3, 4, 48, 128), BF16),
    pltpu.VMEM((3, 4, 48, 128), BF16),
    pltpu.VMEM((3, 3, 48, 128), BF16),
    pltpu.VMEM((6, 12, 128), F32),
    pltpu.VMEM((6, 12, 128), F32),
]


class Reduce:
    def __init__(self, net, merge, cur, got):
        self.net, self.merge, self.cur, self.got = net, merge, cur, got
        self.rows, self.level, self.slot = float(UTT * FRAMES_DEV), 0, 0

    def start(self, value):
        self.value = value
        self.cur[self.level] = value
        self.copies = []
        for _, device in peers(self.net.me, AXES[self.level]):
            self.copies.append(
                (self.net.send(self.cur.at[self.level], self.got.at[self.slot], device), self.slot)
            )
            self.slot += 1

    def take(self):
        parts = [self.value]
        for copy, index in self.copies:
            copy.wait_recv()
            parts.append(self.got[index])
        if self.merge:
            value = merge_stats(parts, self.rows)
        else:
            value = functools.reduce(jnp.add, parts)
        self.rows *= SIZE[AXES[self.level]]
        self.level += 1
        return value

    def step(self):
        self.start(self.take())


ROWS = UTT * FRAMES_DEV
CHUNK = 256
CHUNKS = D // CHUNK
HALO = 16
OWN = HALO * 8


def dot(a, b):
    return jnp.dot(a, b, preferred_element_type=F32)


def dot_t(a, b):
    return lax.dot_general(a, b, (((1,), (1,)), ((), ())), preferred_element_type=F32)


def span(index, size):
    return pl.ds(pl.multiple_of(index * size, size), size)


def frame_of(row):
    return (row & 7) * 32 + (row >> 3)


def fold(x):
    return jnp.sum(x.reshape(x.shape[0] // 8, 8, x.shape[1]), axis=0)


class Halo:
    def __init__(self, me, devices, out, got, send_sem, recv_sem):
        self.out, self.got, self.send_sem, self.recv_sem = out, got, send_sem, recv_sem
        self.right = lax.rem(me + 1, devices)
        self.left = lax.rem(me + devices - 1, devices)

    def copies(self, c):
        return [
            pltpu.make_async_remote_copy(
                src_ref=self.out.at[c, way],
                dst_ref=self.got.at[c, way],
                send_sem=self.send_sem.at[c, way],
                recv_sem=self.recv_sem.at[c, way],
                device_id=(device,),
                device_id_type=pl.DeviceIdType.MESH,
            )
            for way, device in enumerate((self.right, self.left))
        ]

    def push(self, c, select, blocks):
        for u in range(UTT):
            edge = dot(select[...], blocks[u]).astype(BF16)
            self.out[c, 0, u] = edge[0:HALO]
            self.out[c, 1, u] = edge[HALO : 2 * HALO]
        for copy in self.copies(c):
            copy.start()

    def wait(self, c):
        for copy in self.copies(c):
            copy.wait_recv()

    def drain(self):
        for c in range(CHUNKS):
            for copy in self.copies(c):
                copy.wait_send()


def extend(ext, u, cols, low, high, row_id):
    for j in range(HALO):
        below = pltpu.roll(ext[u, OWN + (16 + j) * 8 : OWN + (17 + j) * 8, cols], 1, 0)
        ext[u, j * 8 : j * 8 + 8, cols] = jnp.where(row_id == 0, low[j : j + 1], below)
        above = pltpu.roll(ext[u, OWN + j * 8 : OWN + j * 8 + 8, cols], 7, 0)
        ext[u, (48 + j) * 8 : (49 + j) * 8, cols] = jnp.where(row_id == 7, high[j : j + 1], above)


def convolve(ext, u, cols, taps, forward):
    for base in range(0, 32, 8):
        acc = [None] * 8
        reach = range(base + 1, base + 40) if forward else range(base, base + 39)
        for e in reach:
            x = ext[u, e * 8 : e * 8 + 8, cols]
            for o in range(8):
                k = e - (base + o) - 1 if forward else base + o + 31 - e
                if 0 <= k < K:
                    term = taps[k] * x
                    acc[o] = term if acc[o] is None else acc[o] + term
        yield base, acc


def whole_kernel(n_dev, x_hbm, lng_ref, win_hbm, ker_ref, bng_ref, bnb_ref, wout_hbm, cot_hbm,
                 out_hbm, din_hbm, dw_ref, dk_ref, dbn_ref, *scratch):
    s = dict(zip([name for name, _ in SCRATCH], scratch))
    me = lax.axis_index("seq")
    local = s["local_sem"]
    load_x = [pltpu.make_async_copy(x_hbm.at[u], s["x_raw"].at[u], local.at[u]) for u in range(UTT)]
    load_cot = pltpu.make_async_copy(cot_hbm, s["cot_raw"], local.at[2])
    load_out = pltpu.make_async_copy(wout_hbm, s["w_out"], local.at[3])

    def load_in(c):
        found = []
        for side in range(2):
            cols = pl.ds(pl.multiple_of(side * D + c * CHUNK, CHUNK), CHUNK)
            found.append(
                pltpu.make_async_copy(win_hbm.at[:, cols], s["w_in"].at[:, cols], s["win_sem"].at[c, side])
            )
        return found

    for copy in load_x + load_in(0):
        copy.start()
    vec = s["vec"]
    for row, ref in enumerate((lng_ref, bng_ref, bnb_ref)):
        vec[row : row + 1, :] = ref[...].reshape(1, D)
    net = Net(me, s["send_sem"], s["recv_sem"])
    halo1 = Halo(me, n_dev, s["h_out1"], s["h_got1"], s["h_send1"], s["h_recv1"])
    halo2 = Halo(me, n_dev, s["h_out2"], s["h_got2"], s["h_send2"], s["h_recv2"])

    perm, eye, select = s["perm"], s["eye"], s["select"]
    r0 = lax.broadcasted_iota(jnp.int32, (256, 256), 0)
    r1 = lax.broadcasted_iota(jnp.int32, (256, 256), 1)
    perm[...] = jnp.where(frame_of(r0) == r1, 1.0, 0.0).astype(BF16)
    eye[...] = jnp.where(r0 == r1, 1.0, 0.0).astype(BF16)
    q0 = lax.broadcasted_iota(jnp.int32, (32, 256), 0)
    q1 = lax.broadcasted_iota(jnp.int32, (32, 256), 1)
    edge_frame = jnp.where(q0 < HALO, FRAMES_DEV - HALO + q0, q0 - HALO)
    select[...] = jnp.where(frame_of(q1) == edge_frame, 1.0, 0.0).astype(BF16)
    row_id = lax.broadcasted_iota(jnp.int32, (8, 128), 0)

    x_p, normed, mu_ref, rstd_ref = s["x_p"], s["bf"], s["mu"], s["rstd"]
    for copy in load_x:
        copy.wait()
    for c in range(1, CHUNKS):
        for copy in load_in(c):
            copy.start()

    def norm_tile(i, carry):
        u, part = i // 4, lax.rem(i, 4)
        rows = span(i, 64)
        x = dot(perm[span(part, 64), :], s["x_raw"][u])
        x_p[rows, :] = x.astype(BF16)
        mean = jnp.mean(x, axis=-1, keepdims=True)
        gap = x - mean
        rstd = lax.rsqrt(jnp.mean(gap * gap, axis=-1, keepdims=True) + EPSILON)
        mu_ref[rows, :] = mean
        rstd_ref[rows, :] = rstd
        normed[rows, :] = (gap * rstd * vec[0:1, :]).astype(BF16)
        return carry

    lax.fori_loop(0, 8, norm_tile, 0)
    greet(me, AXES, (halo1.left, halo1.right))
    w_in, val, gs, ext_g, ext_d = s["w_in"], s["val"], s["gs"], s["ext_g"], s["ext_d"]

    def project(c, carry):
        cols = span(c, CHUNK)
        for copy in load_in(c):
            copy.wait()
        val[:, cols] = dot(normed[...], w_in[:, cols])
        gate_cols = pl.ds(pl.multiple_of(D + c * CHUNK, CHUNK), CHUNK)
        gs[:, cols] = dot(normed[...], w_in[:, gate_cols])
        blocks = []
        for u in range(UTT):
            rows = pl.ds(u * 256, 256)
            sig = jax.nn.sigmoid(gs[rows, cols])
            gs[rows, cols] = sig
            gated = (val[rows, cols] * sig).astype(BF16)
            ext_g[u, OWN : OWN + 256, cols] = gated.astype(F32)
            blocks.append(gated)
        halo1.push(c, select, blocks)
        return carry

    lax.fori_loop(0, CHUNKS, project, 0)
    load_cot.start()
    load_out.start()

    def halo_rows(halo, c, u, lane):
        low = halo.got[c, 0, u, :, lane : lane + 128].astype(F32)
        high = halo.got[c, 1, u, :, lane : lane + 128].astype(F32)
        return jnp.where(me == 0, 0.0, low), jnp.where(me == n_dev - 1, 0.0, high)

    conv, stat = s["conv"], s["stat"]

    def taps_of(cols):
        return [jnp.broadcast_to(ker_ref[k : k + 1, cols], (8, 128)) for k in range(K)]

    def conv_chunk(c, carry):
        halo1.wait(c)
        for half in range(2):
            cols = pl.ds(pl.multiple_of(c * CHUNK + half * 128, 128), 128)
            taps = taps_of(cols)
            total = jnp.zeros((8, 128), F32)
            for u in range(UTT):
                low, high = halo_rows(halo1, c, u, half * 128)
                extend(ext_g, u, cols, low, high, row_id)
                for base, acc in convolve(ext_g, u, cols, taps, True):
                    for o in range(8):
                        conv[pl.ds(u * 256 + (base + o) * 8, 8), cols] = acc[o]
                        total = total + acc[o]
            mean = jnp.sum(total, axis=0, keepdims=True) * (1.0 / ROWS)
            gap = conv[:, cols] - mean
            stat[0:1, cols] = mean
            stat[1:2, cols] = jnp.sum(fold(gap * gap), axis=0, keepdims=True)
        return carry

    lax.fori_loop(0, CHUNKS, conv_chunk, 0)

    ar1 = Reduce(net, True, s["cur1"], s["ar1"])
    ar1.start(stat[...])
    load_cot.wait()
    cot_p, cot_t, w_out = s["cot_p"], s["cot_t"], s["w_out"]

    def turn(c, carry):
        cols = span(c, CHUNK)
        for u in range(UTT):
            cot_p[u * 256 : u * 256 + 256, cols] = dot(perm[...], s["cot_raw"][u, :, cols]).astype(BF16)
        cot_t[cols, :] = dot_t(eye[...], cot_p[:, cols]).astype(BF16)
        return carry

    lax.fori_loop(0, CHUNKS, turn, 0)
    ar1.step()
    load_out.wait()

    def act_grad(c, carry):
        cols = span(c, CHUNK)
        res = dot(cot_p[...], w_out[:, cols])
        for u in range(UTT):
            ext_d[u, OWN : OWN + 256, cols] = res[u * 256 : u * 256 + 256]
        return carry

    lax.fori_loop(0, CHUNKS // 2, act_grad, 0)
    ar1.step()
    lax.fori_loop(CHUNKS // 2, CHUNKS, act_grad, 0)
    ar1.step()
    stats = ar1.take()
    total_rows = float(ROWS * n_dev)
    coef = s["coef"]
    coef[0:1, :] = stats[0:1]
    coef[1:2, :] = lax.rsqrt(stats[1:2] * (1.0 / total_rows) + EPSILON)
    act = s["bf"]

    def bn_block(cb, carry):
        cols = span(cb, 128)
        mean, rstd = coef[0:1, cols], coef[1:2, cols]
        gain, bias = vec[1:2, cols], vec[2:3, cols]
        sum_bias = jnp.zeros((8, 128), F32)
        sum_gain = jnp.zeros((8, 128), F32)
        for u in range(UTT):
            rows = pl.ds(u * 256, 256)
            xhat = (conv[rows, cols] - mean) * rstd
            bn = xhat * gain + bias
            sig = jax.nn.sigmoid(bn)
            conv[rows, cols] = xhat
            act[rows, cols] = (bn * sig).astype(BF16)
            d_bn = ext_d[u, OWN : OWN + 256, cols] * (sig + bn * sig * (1.0 - sig))
            ext_d[u, OWN : OWN + 256, cols] = d_bn
            sum_bias = sum_bias + fold(d_bn)
            sum_gain = sum_gain + fold(d_bn * xhat)
        stat[0:1, cols] = jnp.sum(sum_gain, axis=0, keepdims=True)
        stat[1:2, cols] = jnp.sum(sum_bias, axis=0, keepdims=True)
        return carry

    lax.fori_loop(0, D // 128, bn_block, 0)
    ar2 = Reduce(net, False, s["cur2"], s["ar2"])
    ar2.start(stat[...])

    core = coord(me, "core")
    part_ref = s["part"]
    rs = Scatter(net, part_ref, *[s[name] for name in RS_NAMES])

    def weight_part(h, p):
        cols = pl.ds(pl.multiple_of(h * HALF + p * CHUNK, CHUNK), CHUNK)

        def weight_tile(m, carry):
            res = dot(cot_t[span(m, 384), :], act[:, cols])
            for j in range(16):
                piece = res[j * 24 : j * 24 + 24]
                piece = jnp.concatenate([piece[:, 0:128], piece[:, 128:256]], axis=0).astype(BF16)
                part_ref[h, p, m, j // 4, j % 4] = piece
            return carry

        lax.fori_loop(0, 4, weight_tile, 0)

    firsts = []
    for p in range(3):
        weight_part(1 - core, p)
        firsts.append(rs.start(p))
    ar2.step()
    saves = []

    def branch(n, carry):
        cols = span(n, CHUNK)
        res = dot_t(act[...], w_out[cols, :])
        s["out_p"][:, cols] = (x_p[:, cols].astype(F32) + res).astype(BF16)
        return carry

    lax.fori_loop(0, CHUNKS // 2, branch, 0)
    ar2.step()
    lax.fori_loop(CHUNKS // 2, CHUNKS, branch, 0)
    copy = pltpu.make_async_copy(s["out_p"], out_hbm, local.at[4])
    copy.start()
    saves.append(copy)
    ar2.step()
    for p in range(3):
        weight_part(core, p)
    sums = ar2.take()
    dbn_ref[...] = sums
    gain_row = vec[1:2, :]
    rstd_row = coef[1:2, :]
    coef[2:3, :] = rstd_row * gain_row
    coef[3:4, :] = rstd_row * (gain_row * sums[1:2] * (1.0 / total_rows))
    coef[4:5, :] = rstd_row * (gain_row * sums[0:1] * (1.0 / total_rows))

    def conv_grad(c, carry):
        cols = span(c, CHUNK)
        blocks = []
        for u in range(UTT):
            d_bn = ext_d[u, OWN : OWN + 256, cols]
            xhat = conv[u * 256 : u * 256 + 256, cols]
            d_conv = d_bn * coef[2:3, cols] - coef[3:4, cols] - xhat * coef[4:5, cols]
            ext_d[u, OWN : OWN + 256, cols] = d_conv
            blocks.append(d_conv.astype(BF16))
        halo2.push(c, select, blocks)
        return carry

    lax.fori_loop(0, CHUNKS, conv_grad, 0)

    levels = []
    for p in range(3):
        rs.add_core(p, firsts[p])
        levels.append(rs.send_level(p, 0))

    dk_src = s["dk_src"]

    def kernel_grad(h):
        def body(n, carry):
            cols = pl.ds(pl.multiple_of(h * HALF + n * 128, 128), 128)
            for first in range(0, K, 16):
                acc = [jnp.zeros((8, 128), F32)] * 16
                for u in range(UTT):
                    for base in range(0, 32, 8):
                        grads = [
                            ext_d[u, OWN + (base + o) * 8 : OWN + (base + o) * 8 + 8, cols]
                            for o in range(8)
                        ]
                        for e in range(base + first + 1, base + first + 24):
                            x = ext_g[u, e * 8 : e * 8 + 8, cols]
                            for o in range(8):
                                k = e - (base + o) - 1 - first
                                if 0 <= k < 16:
                                    acc[k] = acc[k] + x * grads[o]
                for a in range(16):
                    k = first + a
                    dk_src[h, k // 8, k % 8 : k % 8 + 1, span(n, 128)] = jnp.sum(
                        acc[a], axis=0, keepdims=True
                    )
            return carry

        lax.fori_loop(0, HALF // 128, body, 0)

    dk = DKernel(net, dk_src, *[s[name] for name in DK_NAMES])
    kernel_grad(1 - core)
    dk.start()
    nexts = []
    for p in range(3):
        rs.add_level(p, 0, levels[p])
        nexts.append(rs.send_level(p, 1))
    kernel_grad(core)
    dk.to_x()
    d_proj = s["d_proj"]

    def input_grad(c, carry):
        halo2.wait(c)
        for half in range(2):
            start = pl.multiple_of(c * CHUNK + half * 128, 128)
            cols = pl.ds(start, 128)
            gate_cols = pl.ds(pl.multiple_of(D + start, 128), 128)
            taps = taps_of(cols)
            for u in range(UTT):
                low, high = halo_rows(halo2, c, u, half * 128)
                extend(ext_d, u, cols, low, high, row_id)
                for base, acc in convolve(ext_d, u, cols, taps, False):
                    rows = pl.ds(u * 256 + base * 8, 64)
                    grad = jnp.concatenate(acc, axis=0)
                    sig = gs[rows, cols]
                    by_sig = grad * sig
                    d_proj[rows, cols] = by_sig.astype(BF16)
                    d_proj[rows, gate_cols] = (by_sig * val[rows, cols] * (1.0 - sig)).astype(BF16)
        return carry

    lax.fori_loop(0, CHUNKS // 2, input_grad, 0)
    levels = nexts
    nexts = []
    for p in range(3):
        rs.add_level(p, 1, levels[p])
        nexts.append(rs.send_level(p, 2))
    dk.to_z()
    lax.fori_loop(CHUNKS // 2, CHUNKS, input_grad, 0)
    rs.exchange([rs.add_level(p, 2, nexts[p]) for p in range(3)])
    dk.to_y()

    def frame_grad(u):
        rows_u = pl.ds(u * 256, 256)

        def tile(n, carry):
            cols = span(n, CHUNK)
            conv[rows_u, cols] = dot_t(d_proj[rows_u, :], w_in[cols, :])
            return carry

        lax.fori_loop(0, CHUNKS, tile, 0)

    def norm_grad(u):
        def tile(i, carry):
            rows = pl.ds(pl.multiple_of(u * 256 + i * 32, 32), 32)
            d_hat = conv[rows, :] * vec[0:1, :]
            rstd = rstd_ref[rows, :]
            hat = (x_p[rows, :].astype(F32) - mu_ref[rows, :]) * rstd
            m1 = jnp.mean(d_hat, axis=-1, keepdims=True)
            m2 = jnp.mean(d_hat * hat, axis=-1, keepdims=True)
            grad = rstd * (d_hat - m1 - hat * m2)
            act[rows, :] = (cot_p[rows, :].astype(F32) + grad).astype(BF16)
            return carry

        lax.fori_loop(0, 8, tile, 0)

        rows_u = pl.ds(u * 256, 256)
        copy = pltpu.make_async_copy(act.at[rows_u], din_hbm.at[rows_u], local.at[6 + u])
        copy.start()
        saves.append(copy)

    frame_grad(0)
    dk.gather_x()
    norm_grad(0)
    dk.gather_core()
    frame_grad(1)
    rs.finish(dw_ref)
    dk.finish(dk_ref)
    norm_grad(1)
    for copy in saves:
        copy.wait()
    net.drain()
    halo1.drain()
    halo2.drain()


RS_NAMES = ["got_core", "s1", "got1", "s2", "got2", "s3", "got3", "tail", "got_tail"]
DK_NAMES = ["dk%d" % i for i in range(len(DK_SCRATCH))]
VM = pltpu.VMEM
SCRATCH = [
    ("x_raw", VM((UTT, 256, D), BF16)),
    ("w_in", VM((D, 2 * D), BF16)),
    ("cot_raw", VM((UTT, 256, D), BF16)),
    ("w_out", VM((D, D), BF16)),
    ("perm", VM((256, 256), BF16)),
    ("win_sem", pltpu.SemaphoreType.DMA((CHUNKS, 2))),
    ("vec", VM((3, D), F32)),
    ("out_p", VM((ROWS, D), BF16)),
    ("eye", VM((256, 256), BF16)),
    ("select", VM((32, 256), BF16)),
    ("x_p", VM((ROWS, D), BF16)),
    ("bf", VM((ROWS, D), BF16)),
    ("mu", VM((ROWS, 1), F32)),
    ("rstd", VM((ROWS, 1), F32)),
    ("val", VM((ROWS, D), F32)),
    ("gs", VM((ROWS, D), F32)),
    ("ext_g", VM((UTT, 512, D), F32)),
    ("ext_d", VM((UTT, 512, D), F32)),
    ("conv", VM((ROWS, D), F32)),
    ("stat", VM((2, D), F32)),
    ("coef", VM((8, D), F32)),
    ("cot_p", VM((ROWS, D), BF16)),
    ("cot_t", VM((D, ROWS), BF16)),
    ("d_proj", VM((ROWS, 2 * D), BF16)),
    ("part", VM((2, 3, 4, 4, 4, 48, 128), BF16)),
    ("h_out1", VM((CHUNKS, 2, UTT, HALO, CHUNK), BF16)),
    ("h_got1", VM((CHUNKS, 2, UTT, HALO, CHUNK), BF16)),
    ("h_out2", VM((CHUNKS, 2, UTT, HALO, CHUNK), BF16)),
    ("h_got2", VM((CHUNKS, 2, UTT, HALO, CHUNK), BF16)),
    ("cur1", VM((4, 2, D), F32)),
    ("ar1", VM((10, 2, D), F32)),
    ("cur2", VM((4, 2, D), F32)),
    ("ar2", VM((10, 2, D), F32)),
    ("dk_src", VM((2, 4, 8, HALF), F32)),
]
SCRATCH += list(zip(RS_NAMES, RS_SCRATCH)) + list(zip(DK_NAMES, DK_SCRATCH))
SCRATCH += [
    ("local_sem", pltpu.SemaphoreType.DMA((8,))),
    ("send_sem", pltpu.SemaphoreType.DMA((72,))),
    ("recv_sem", pltpu.SemaphoreType.DMA((72,))),
    ("h_send1", pltpu.SemaphoreType.DMA((CHUNKS, 2))),
    ("h_recv1", pltpu.SemaphoreType.DMA((CHUNKS, 2))),
    ("h_send2", pltpu.SemaphoreType.DMA((CHUNKS, 2))),
    ("h_recv2", pltpu.SemaphoreType.DMA((CHUNKS, 2))),
]


def finish_kernel(out_p, din_p, dw, dk, dbn, out_ref, din_ref, dw_out, dk_out, gain_out, bias_out, perm_t):
    @pl.when((pl.program_id(0) == 0) & (pl.program_id(1) == 0))
    def _():
        r0 = lax.broadcasted_iota(jnp.int32, (256, 256), 0)
        r1 = lax.broadcasted_iota(jnp.int32, (256, 256), 1)
        perm_t[...] = jnp.where(frame_of(r1) == r0, 1.0, 0.0).astype(BF16)
        dw_out[...] = dw[...]
        dk_out[...] = dk[...]
        gain_out[...] = dbn[0:1, :].reshape(D)
        bias_out[...] = dbn[1:2, :].reshape(D)

    out_ref[0] = dot(perm_t[...], out_p[...]).astype(BF16)
    din_ref[0] = dot(perm_t[...], din_p[...]).astype(BF16)


def on_device(inputs, ln_gain, w_in, kernel, bn_gain, bn_bias, w_out, cotangent):
    any_spec = pl.BlockSpec(memory_space=pl.ANY)
    vmem_spec = pl.BlockSpec(memory_space=pltpu.VMEM)
    flat = jax.ShapeDtypeStruct((ROWS, D), BF16)
    out_p, din_p, dw, dk, dbn = pl.pallas_call(
        functools.partial(whole_kernel, lax.axis_size("seq")),
        out_shape=(
            flat,
            flat,
            jax.ShapeDtypeStruct((D // 128, D), F32),
            jax.ShapeDtypeStruct((K, D), F32),
            jax.ShapeDtypeStruct((2, D), F32),
        ),
        in_specs=[any_spec, vmem_spec, any_spec, vmem_spec, vmem_spec, vmem_spec, any_spec, any_spec],
        out_specs=[any_spec, any_spec, vmem_spec, vmem_spec, vmem_spec],
        scratch_shapes=[spec for _, spec in SCRATCH],
        compiler_params=pltpu.CompilerParams(
            collective_id=0, has_side_effects=True, vmem_limit_bytes=67043328
        ),
    )(inputs, ln_gain, w_in, kernel, bn_gain, bn_bias, w_out, cotangent)

    def whole(shape):
        return pl.BlockSpec(shape, lambda u, c: (0,) * len(shape))

    wide = D // 2
    rows_spec = pl.BlockSpec((256, wide), lambda u, c: (u, c))
    block_spec = pl.BlockSpec((1, 256, wide), lambda u, c: (u, 0, c))
    full = jax.ShapeDtypeStruct((UTT, FRAMES_DEV, D), BF16)
    return pl.pallas_call(
        finish_kernel,
        grid=(UTT, 2),
        out_shape=(
            full,
            full,
            jax.ShapeDtypeStruct((D // 128, D), F32),
            jax.ShapeDtypeStruct((K, D), F32),
            jax.ShapeDtypeStruct((D,), F32),
            jax.ShapeDtypeStruct((D,), F32),
        ),
        in_specs=[rows_spec, rows_spec, whole((D // 128, D)), whole((K, D)), whole((2, D))],
        out_specs=[block_spec, block_spec, whole((D // 128, D)), whole((K, D)), whole((D,)), whole((D,))],
        scratch_shapes=[pltpu.VMEM((256, 256), BF16)],
    )(out_p, din_p, dw, dk, dbn)


def solution(mesh):
    return jax.shard_map(
        on_device,
        mesh=mesh,
        in_specs=(P(None, "seq", None), P(), P(), P(), P(), P(), P(), P(None, "seq", None)),
        out_specs=(P(None, "seq", None), P(None, "seq", None), P("seq", None), P(), P(), P()),
        check_vma=False,
    )
```

```python
import functools
import jax
import jax.numpy as jnp
from jax import lax
from jax.experimental import pallas as pl
from jax.experimental.pallas import tpu as pltpu
from jax.sharding import PartitionSpec as P

D = 1536
K = 32
FRAMES_DEV = 256
UTT = 2
EPSILON = 1e-05
F32 = jnp.float32
BF16 = jnp.bfloat16
STRIDE = {"core": 1, "z": 2, "y": 8, "x": 32}
SIZE = {"core": 2, "z": 4, "y": 4, "x": 4}
ORDERS = (("x", "y", "z"), ("y", "z", "x"), ("z", "x", "y"))
HALF = D // 2


def coord(me, axis):
    return lax.rem(me // STRIDE[axis], SIZE[axis])


def peers(me, axis):
    q = coord(me, axis)
    found = []
    for delta in range(1, SIZE[axis]):
        other = lax.rem(q + delta, SIZE[axis])
        found.append((other, me + (other - q) * STRIDE[axis]))
    return found


class Net:
    def __init__(self, me, send_sem, recv_sem):
        self.me, self.send_sem, self.recv_sem, self.used = me, send_sem, recv_sem, 0
        self.started = []

    def send(self, src, dst, device):
        slot = self.used
        self.used += 1
        copy = pltpu.make_async_remote_copy(
            src_ref=src,
            dst_ref=dst,
            send_sem=self.send_sem.at[slot],
            recv_sem=self.recv_sem.at[slot],
            device_id=(device,),
            device_id_type=pl.DeviceIdType.MESH,
        )
        copy.start()
        self.started.append(copy)
        return copy

    def drain(self):
        for copy in self.started:
            copy.wait_send()


def greet(me, axes, extra=()):
    barrier = pltpu.get_barrier_semaphore()
    count = 0
    for axis in axes:
        for _, device in peers(me, axis):
            pl.semaphore_signal(
                barrier, inc=1, device_id=(device,), device_id_type=pl.DeviceIdType.MESH
            )
            count += 1
    for device in extra:
        pl.semaphore_signal(
            barrier, inc=1, device_id=(device,), device_id_type=pl.DeviceIdType.MESH
        )
        count += 1
    return lambda: pl.semaphore_wait(barrier, count)


AXES = ("core", "z", "y", "x")


def merge_stats(parts, rows):
    mean = functools.reduce(jnp.add, [p[0:1] for p in parts]) * (1.0 / len(parts))
    spread = functools.reduce(jnp.add, [p[1:2] for p in parts])
    for p in parts:
        gap = p[0:1] - mean
        spread = spread + rows * gap * gap
    return jnp.concatenate([mean, spread], axis=0)


class DKernel:
    def __init__(self, net, src, core_buf, got_core, got_x, cz, got_z, cy, got_y, full, other):
        self.net = net
        self.src, self.core_buf, self.got_core = src, core_buf, got_core
        self.got_x, self.cz, self.got_z = got_x, cz, got_z
        self.cy, self.got_y, self.full, self.other = cy, got_y, full, other

    def start(self):
        me = self.net.me
        core = coord(me, "core")
        self.c0 = [self.net.send(self.src.at[1 - core], self.got_core, me + 1 - 2 * core)]

    def to_x(self):
        me = self.net.me
        core = coord(me, "core")
        x = coord(me, "x")
        self.c0[0].wait_recv()
        self.core_buf[...] = self.src[core] + self.got_core[...]
        self.cx_c = [
            self.net.send(self.core_buf.at[other], self.got_x.at[i], device)
            for i, (other, device) in enumerate(peers(me, "x"))
        ]

    def to_z(self):
        me = self.net.me
        total = self.core_buf[coord(me, "x")]
        for i, copy in enumerate(self.cx_c):
            copy.wait_recv()
            total = total + self.got_x[i]
        self.cz[...] = total
        self.cz_c = [
            self.net.send(self.cz, self.got_z.at[i], device)
            for i, (_, device) in enumerate(peers(me, "z"))
        ]

    def to_y(self):
        me = self.net.me
        total = self.cz[...]
        for i, copy in enumerate(self.cz_c):
            copy.wait_recv()
            total = total + self.got_z[i]
        self.cy[...] = total
        self.cy_c = [
            self.net.send(self.cy, self.got_y.at[i], device)
            for i, (_, device) in enumerate(peers(me, "y"))
        ]

    def gather_x(self):
        me = self.net.me
        total = self.cy[...]
        for i, copy in enumerate(self.cy_c):
            copy.wait_recv()
            total = total + self.got_y[i]
        x = coord(me, "x")
        self.full[x] = total
        self.gx_c = [
            self.net.send(self.full.at[x], self.full.at[x], device)
            for _, device in peers(me, "x")
        ]

    def gather_core(self):
        me = self.net.me
        core = coord(me, "core")
        for copy in self.gx_c:
            copy.wait_recv()
        self.gc_c = self.net.send(self.full, self.other, me + 1 - 2 * core)

    def finish(self, out):
        core = coord(self.net.me, "core")
        self.gc_c.wait_recv()
        for i in range(4):
            mine = self.full[i]
            theirs = self.other[i]
            out[pl.ds(8 * i, 8), 0:HALF] = jnp.where(core == 0, mine, theirs)
            out[pl.ds(8 * i, 8), HALF:D] = jnp.where(core == 0, theirs, mine)


DK_SCRATCH = [
    pltpu.VMEM((4, 8, HALF), F32),
    pltpu.VMEM((4, 8, HALF), F32),
    pltpu.VMEM((3, 8, HALF), F32),
    pltpu.VMEM((8, HALF), F32),
    pltpu.VMEM((3, 8, HALF), F32),
    pltpu.VMEM((8, HALF), F32),
    pltpu.VMEM((3, 8, HALF), F32),
    pltpu.VMEM((4, 8, HALF), F32),
    pltpu.VMEM((4, 8, HALF), F32),
]


def pick(ref, dims, axis, index):
    where = dims.index(axis)
    if where == 0:
        return ref.at[index]
    if where == 1:
        return ref.at[:, index]
    return ref.at[:, :, index]


class Scatter:
    def __init__(self, net, src, got_core, s1, got1, s2, got2, s3, got3, tail, got_tail):
        self.net, self.src, self.got_core = net, src, got_core
        self.s = [s1, s2, s3]
        self.got = [got1, got2, got3]
        self.tail, self.got_tail = tail, got_tail

    def start(self, part):
        me = self.net.me
        core = coord(me, "core")
        return self.net.send(self.src.at[1 - core, part], self.got_core.at[part], me + 1 - 2 * core)

    def dims(self, part, level):
        gone = ORDERS[part][:level]
        return [a for a in ("x", "y", "z") if a not in gone]

    def add_core(self, part, copy):
        core = coord(self.net.me, "core")
        copy.wait_recv()

        def body(i, carry):
            x, y = i // 4, lax.rem(i, 4)
            mine = self.src[core, part, x, y].astype(F32)
            theirs = self.got_core[part, x, y].astype(F32)
            self.s[0][part, x, y] = (mine + theirs).astype(BF16)
            return carry

        lax.fori_loop(0, 16, body, 0, unroll=2)

    def send_level(self, part, level):
        me = self.net.me
        axis = ORDERS[part][level]
        dims = self.dims(part, level)
        return [
            self.net.send(
                pick(self.s[level].at[part], dims, axis, other),
                self.got[level].at[part, i],
                device,
            )
            for i, (other, device) in enumerate(peers(me, axis))
        ]

    def add_level(self, part, level, copies):
        me = self.net.me
        axis = ORDERS[part][level]
        dims = self.dims(part, level)
        own = pick(self.s[level].at[part], dims, axis, coord(me, axis))
        for copy in copies:
            copy.wait_recv()
        got = self.got[level].at[part]
        if level == 2:
            total = own[...].astype(F32)
            for i in range(3):
                total = total + got[i].astype(F32)
            return total
        for a in range(4):
            total = own[a].astype(F32)
            for i in range(3):
                total = total + got[i, a].astype(F32)
            self.s[level + 1][part, a] = total.astype(BF16)

    def exchange(self, totals):
        core = coord(self.net.me, "core")
        self.mine = []
        for part in range(3):
            for half in range(2):
                low = totals[part][half * 24 : half * 24 + 12]
                high = totals[part][half * 24 + 12 : half * 24 + 24]
                self.mine.append(jnp.where(core == 0, low, high))
                self.tail[part * 2 + half] = jnp.where(core == 0, high, low)
        self.copy = self.net.send(self.tail, self.got_tail, self.net.me + 1 - 2 * core)

    def finish(self, out):
        core = coord(self.net.me, "core")
        self.copy.wait_recv()
        for piece in range(6):
            mine = self.mine[piece]
            theirs = self.got_tail[piece]
            out[:, piece * 128 : piece * 128 + 128] = jnp.where(core == 0, mine, theirs)
            out[:, HALF + piece * 128 : HALF + piece * 128 + 128] = jnp.where(core == 0, theirs, mine)


RS_SCRATCH = [
    pltpu.VMEM((3, 4, 4, 4, 48, 128), BF16),
    pltpu.VMEM((3, 4, 4, 4, 48, 128), BF16),
    pltpu.VMEM((3, 3, 4, 4, 48, 128), BF16),
    pltpu.VMEM((3, 4, 4, 48, 128), BF16),
    pltpu.VMEM((3, 3, 4, 48, 128), BF16),
    pltpu.VMEM((3, 4, 48, 128), BF16),
    pltpu.VMEM((3, 3, 48, 128), BF16),
    pltpu.VMEM((6, 12, 128), F32),
    pltpu.VMEM((6, 12, 128), F32),
]


class Reduce:
    def __init__(self, net, merge, cur, got):
        self.net, self.merge, self.cur, self.got = net, merge, cur, got
        self.rows, self.level, self.slot = float(UTT * FRAMES_DEV), 0, 0

    def start(self, value):
        self.value = value
        self.cur[self.level] = value
        self.copies = []
        for _, device in peers(self.net.me, AXES[self.level]):
            self.copies.append(
                (self.net.send(self.cur.at[self.level], self.got.at[self.slot], device), self.slot)
            )
            self.slot += 1

    def take(self):
        parts = [self.value]
        for copy, index in self.copies:
            copy.wait_recv()
            parts.append(self.got[index])
        if self.merge:
            value = merge_stats(parts, self.rows)
        else:
            value = functools.reduce(jnp.add, parts)
        self.rows *= SIZE[AXES[self.level]]
        self.level += 1
        return value

    def step(self):
        self.start(self.take())


ROWS = UTT * FRAMES_DEV
CHUNK = 256
CHUNKS = D // CHUNK
HALO = 16
OWN = HALO * 8


def dot(a, b):
    return jnp.dot(a, b, preferred_element_type=F32)


def dot_t(a, b):
    return lax.dot_general(a, b, (((1,), (1,)), ((), ())), preferred_element_type=F32)


def span(index, size):
    return pl.ds(pl.multiple_of(index * size, size), size)


def frame_of(row):
    return (row & 7) * 32 + (row >> 3)


def fold(x):
    return jnp.sum(x.reshape(x.shape[0] // 8, 8, x.shape[1]), axis=0)


class Halo:
    def __init__(self, me, devices, out, got, send_sem, recv_sem):
        self.out, self.got, self.send_sem, self.recv_sem = out, got, send_sem, recv_sem
        self.right = lax.rem(me + 1, devices)
        self.left = lax.rem(me + devices - 1, devices)

    def copies(self, c):
        return [
            pltpu.make_async_remote_copy(
                src_ref=self.out.at[c, way],
                dst_ref=self.got.at[c, way],
                send_sem=self.send_sem.at[c, way],
                recv_sem=self.recv_sem.at[c, way],
                device_id=(device,),
                device_id_type=pl.DeviceIdType.MESH,
            )
            for way, device in enumerate((self.right, self.left))
        ]

    def push(self, c, select, blocks):
        for u in range(UTT):
            edge = dot(select[...], blocks[u]).astype(BF16)
            self.out[c, 0, u] = edge[0:HALO]
            self.out[c, 1, u] = edge[HALO : 2 * HALO]
        for copy in self.copies(c):
            copy.start()

    def wait(self, c):
        for copy in self.copies(c):
            copy.wait_recv()

    def drain(self):
        for c in range(CHUNKS):
            for copy in self.copies(c):
                copy.wait_send()


def extend(ext, u, cols, low, high, row_id):
    for j in range(HALO):
        below = pltpu.roll(ext[u, OWN + (16 + j) * 8 : OWN + (17 + j) * 8, cols], 1, 0)
        ext[u, j * 8 : j * 8 + 8, cols] = jnp.where(row_id == 0, low[j : j + 1], below)
        above = pltpu.roll(ext[u, OWN + j * 8 : OWN + j * 8 + 8, cols], 7, 0)
        ext[u, (48 + j) * 8 : (49 + j) * 8, cols] = jnp.where(row_id == 7, high[j : j + 1], above)


def convolve(ext, u, cols, taps, offset):
    low, high = taps[0::2], taps[1::2]
    both = [a + b for a, b in zip(low, high)]

    def x(n):
        return ext[u, (n + offset) * 8 : (n + offset) * 8 + 8, cols]

    def product(weights, source, start, first):
        acc = list(start)
        for n in range(first, first + 23):
            value = source(n)
            for p in range(8):
                m = n - first - p
                if 0 <= m < 16:
                    term = weights[m] * value
                    acc[p] = term if acc[p] is None else acc[p] + term
        return acc

    for first in (0, 8):
        shared = product(both, lambda n: x(2 * n + 1), [None] * 8, first)
        even = product(low, lambda n: x(2 * n) - x(2 * n + 1), shared, first)
        odd = product(high, lambda n: x(2 * n + 2) - x(2 * n + 1), shared, first)
        yield 2 * first, [v for pair in zip(even, odd) for v in pair]


def whole_kernel(n_dev, x_hbm, lng_ref, win_hbm, ker_ref, bng_ref, bnb_ref, wout_hbm, cot_hbm,
                 out_hbm, din_hbm, dw_ref, dk_ref, dbn_ref, *scratch):
    s = dict(zip([name for name, _ in SCRATCH], scratch))
    me = lax.axis_index("seq")
    local = s["local_sem"]
    load_x = [pltpu.make_async_copy(x_hbm.at[u], s["x_raw"].at[u], local.at[u]) for u in range(UTT)]
    load_cot = pltpu.make_async_copy(cot_hbm, s["cot_raw"], local.at[2])
    load_out = pltpu.make_async_copy(wout_hbm, s["w_out"], local.at[3])

    def load_in(c):
        found = []
        for side in range(2):
            cols = pl.ds(pl.multiple_of(side * D + c * CHUNK, CHUNK), CHUNK)
            found.append(
                pltpu.make_async_copy(win_hbm.at[:, cols], s["w_in"].at[:, cols], s["win_sem"].at[c, side])
            )
        return found

    for copy in load_x + load_in(0):
        copy.start()
    vec = s["vec"]
    for row, ref in enumerate((lng_ref, bng_ref, bnb_ref)):
        vec[row : row + 1, :] = ref[...].reshape(1, D)
    net = Net(me, s["send_sem"], s["recv_sem"])
    halo1 = Halo(me, n_dev, s["h_out1"], s["h_got1"], s["h_send1"], s["h_recv1"])
    halo2 = Halo(me, n_dev, s["h_out2"], s["h_got2"], s["h_send2"], s["h_recv2"])

    entered = greet(me, AXES, (halo1.left, halo1.right))
    perm, eye, select = s["perm"], s["eye"], s["select"]
    r0 = lax.broadcasted_iota(jnp.int32, (256, 256), 0)
    r1 = lax.broadcasted_iota(jnp.int32, (256, 256), 1)
    perm[...] = jnp.where(frame_of(r0) == r1, 1.0, 0.0).astype(BF16)
    eye[...] = jnp.where(r0 == r1, 1.0, 0.0).astype(BF16)
    q0 = lax.broadcasted_iota(jnp.int32, (32, 256), 0)
    q1 = lax.broadcasted_iota(jnp.int32, (32, 256), 1)
    edge_frame = jnp.where(q0 < HALO, FRAMES_DEV - HALO + q0, q0 - HALO)
    select[...] = jnp.where(frame_of(q1) == edge_frame, 1.0, 0.0).astype(BF16)
    row_id = lax.broadcasted_iota(jnp.int32, (8, 128), 0)

    x_p, normed, mu_ref, rstd_ref = s["x_p"], s["bf"], s["mu"], s["rstd"]
    for copy in load_x:
        copy.wait()
    for c in range(1, CHUNKS):
        for copy in load_in(c):
            copy.start()

    def permute(c, carry):
        cols = span(c, CHUNK)
        for u in range(UTT):
            x_p[u * 256 : u * 256 + 256, cols] = dot(perm[...], s["x_raw"][u, :, cols]).astype(BF16)
        return carry

    lax.fori_loop(0, CHUNKS, permute, 0)

    def norm_tile(i, carry):
        rows = span(i, 16)
        x = x_p[rows, :].astype(F32)
        mean = jnp.mean(x, axis=-1, keepdims=True)
        gap = x - mean
        rstd = lax.rsqrt(jnp.mean(gap * gap, axis=-1, keepdims=True) + EPSILON)
        mu_ref[rows, :] = mean
        rstd_ref[rows, :] = rstd
        normed[rows, :] = (gap * rstd * vec[0:1, :]).astype(BF16)
        return carry

    lax.fori_loop(0, ROWS // 16, norm_tile, 0, unroll=4)
    entered()
    w_in, val, gs, ext_g, ext_d = s["w_in"], s["val"], s["gs"], s["ext_g"], s["ext_d"]

    def project(c, carry):
        for copy in load_in(c):
            copy.wait()
        project_chunk(c)
        return carry

    def project_chunk(c):
        cols = span(c, CHUNK)
        val[:, cols] = dot(normed[...], w_in[:, cols])
        gate_cols = pl.ds(pl.multiple_of(D + c * CHUNK, CHUNK), CHUNK)
        gs[:, cols] = dot(normed[...], w_in[:, gate_cols])
        blocks = []
        for u in range(UTT):
            rows = pl.ds(u * 256, 256)
            sig = jax.nn.sigmoid(gs[rows, cols])
            gs[rows, cols] = sig
            gated = (val[rows, cols] * sig).astype(BF16)
            ext_g[u, OWN : OWN + 256, cols] = gated.astype(F32)
            blocks.append(gated)
        halo1.push(c, select, blocks)

    lax.fori_loop(0, CHUNKS, project, 0)
    load_cot.start()
    load_out.start()

    def halo_rows(halo, c, u, lane):
        low = halo.got[c, 0, u, :, lane : lane + 128].astype(F32)
        high = halo.got[c, 1, u, :, lane : lane + 128].astype(F32)
        return jnp.where(me == 0, 0.0, low), jnp.where(me == n_dev - 1, 0.0, high)

    conv, stat = s["conv"], s["stat"]

    def taps_of(cols):
        return [jnp.broadcast_to(ker_ref[k : k + 1, cols], (8, 128)) for k in range(K)]

    def conv_only(c, carry):
        halo1.wait(c)
        conv_chunk(c)
        return carry

    def conv_chunk(c):
        for half in range(2):
            cols = pl.ds(pl.multiple_of(c * CHUNK + half * 128, 128), 128)
            taps = taps_of(cols)
            total = jnp.zeros((8, 128), F32)
            for u in range(UTT):
                low, high = halo_rows(halo1, c, u, half * 128)
                extend(ext_g, u, cols, low, high, row_id)
                for base, acc in convolve(ext_g, u, cols, taps, 1):
                    for o in range(16):
                        conv[pl.ds(u * 256 + (base + o) * 8, 8), cols] = acc[o]
                        total = total + acc[o]
            mean = jnp.sum(total, axis=0, keepdims=True) * (1.0 / ROWS)
            gap = conv[:, cols] - mean
            stat[0:1, cols] = mean
            stat[1:2, cols] = jnp.sum(fold(gap * gap), axis=0, keepdims=True)

    wide = (slice(0, HALF), slice(HALF, D))
    ar1 = [Reduce(net, True, s["cur"].at[h], s["got"].at[h]) for h in range(2)]
    ar2 = [Reduce(net, False, s["cur"].at[2 + h], s["got"].at[2 + h]) for h in range(2)]
    lax.fori_loop(0, 3, conv_only, 0)
    ar1[0].start(stat[:, wide[0]])
    lax.fori_loop(3, 4, conv_only, 0)
    ar1[0].step()
    lax.fori_loop(4, CHUNKS, conv_only, 0)
    ar1[0].step()
    ar1[1].start(stat[:, wide[1]])
    load_cot.wait()
    cot_p, cot_t, w_out = s["cot_p"], s["cot_t"], s["w_out"]

    def turn(c, carry):
        cols = span(c, CHUNK)
        for u in range(UTT):
            cot_p[u * 256 : u * 256 + 256, cols] = dot(perm[...], s["cot_raw"][u, :, cols]).astype(BF16)
        cot_t[cols, :] = dot_t(eye[...], cot_p[:, cols]).astype(BF16)
        return carry

    lax.fori_loop(0, CHUNKS, turn, 0, unroll=2)
    ar1[1].step()
    ar1[0].step()
    load_out.wait()

    def act_grad(c, carry):
        cols = span(c, CHUNK)
        res = dot(cot_p[...], w_out[:, cols])
        for u in range(UTT):
            ext_d[u, OWN : OWN + 256, cols] = res[u * 256 : u * 256 + 256]
        return carry

    total_rows = float(ROWS * n_dev)
    coef = s["coef"]

    def use_stats(h):
        stats = ar1[h].take()
        coef[0:1, wide[h]] = stats[0:1]
        coef[1:2, wide[h]] = lax.rsqrt(stats[1:2] * (1.0 / total_rows) + EPSILON)

    lax.fori_loop(0, CHUNKS // 2, act_grad, 0)
    ar1[1].step()
    lax.fori_loop(CHUNKS // 2, CHUNKS, act_grad, 0)
    use_stats(0)
    act = s["bf"]

    def bn_block(cb, carry):
        cols = span(cb, 128)
        mean, rstd = coef[0:1, cols], coef[1:2, cols]
        gain, bias = vec[1:2, cols], vec[2:3, cols]
        sum_bias = jnp.zeros((8, 128), F32)
        sum_gain = jnp.zeros((8, 128), F32)
        for u in range(UTT):
            rows = pl.ds(u * 256, 256)
            xhat = (conv[rows, cols] - mean) * rstd
            bn = xhat * gain + bias
            sig = jax.nn.sigmoid(bn)
            conv[rows, cols] = xhat
            act[rows, cols] = (bn * sig).astype(BF16)
            d_bn = ext_d[u, OWN : OWN + 256, cols] * (sig + bn * sig * (1.0 - sig))
            ext_d[u, OWN : OWN + 256, cols] = d_bn
            sum_bias = sum_bias + fold(d_bn)
            sum_gain = sum_gain + fold(d_bn * xhat)
        stat[0:1, cols] = jnp.sum(sum_gain, axis=0, keepdims=True)
        stat[1:2, cols] = jnp.sum(sum_bias, axis=0, keepdims=True)
        return carry

    core = coord(me, "core")
    part_ref = s["part"]
    rs = Scatter(net, part_ref, *[s[name] for name in RS_NAMES])

    def weight_part(h, p):
        cols = pl.ds(pl.multiple_of(h * HALF + p * CHUNK, CHUNK), CHUNK)

        def weight_tile(m, carry):
            res = dot(cot_t[span(m, 384), :], act[:, cols])
            for j in range(16):
                piece = res[j * 24 : j * 24 + 24]
                piece = jnp.concatenate([piece[:, 0:128], piece[:, 128:256]], axis=0).astype(BF16)
                part_ref[h, p, m, j // 4, j % 4] = piece
            return carry

        lax.fori_loop(0, 4, weight_tile, 0, unroll=2)

    saves = []

    def branch(n, carry):
        cols = span(n, CHUNK)
        res = dot_t(act[...], w_out[cols, :])
        s["out_p"][:, cols] = (x_p[:, cols].astype(F32) + res).astype(BF16)
        return carry

    def use_sums(h):
        sums = ar2[h].take()
        dbn_ref[:, wide[h]] = sums
        gain_row = vec[1:2, wide[h]]
        rstd_row = coef[1:2, wide[h]]
        coef[2:3, wide[h]] = rstd_row * gain_row
        coef[3:4, wide[h]] = rstd_row * (gain_row * sums[1:2] * (1.0 / total_rows))
        coef[4:5, wide[h]] = rstd_row * (gain_row * sums[0:1] * (1.0 / total_rows))

    lax.fori_loop(0, 6, bn_block, 0)
    ar1[1].step()
    ar2[0].start(stat[:, wide[0]])
    weight_part(0, 0)
    weight_part(0, 1)
    ar2[0].step()
    weight_part(0, 2)
    use_stats(1)
    lax.fori_loop(6, 12, bn_block, 0)
    ar2[0].step()
    ar2[1].start(stat[:, wide[1]])
    weight_part(1, 0)
    weight_part(1, 1)
    ar2[1].step()
    weight_part(1, 2)
    lax.fori_loop(0, CHUNKS // 2, branch, 0)
    ar2[0].step()
    ar2[1].step()
    firsts = [rs.start(p) for p in range(3)]
    lax.fori_loop(CHUNKS // 2, CHUNKS, branch, 0)
    copy = pltpu.make_async_copy(s["out_p"], out_hbm, local.at[4])
    copy.start()
    saves.append(copy)
    use_sums(0)

    def conv_grad(c, carry):
        cols = span(c, CHUNK)
        blocks = []
        for u in range(UTT):
            d_bn = ext_d[u, OWN : OWN + 256, cols]
            xhat = conv[u * 256 : u * 256 + 256, cols]
            d_conv = d_bn * coef[2:3, cols] - coef[3:4, cols] - xhat * coef[4:5, cols]
            ext_d[u, OWN : OWN + 256, cols] = d_conv
            conv[u * 256 : u * 256 + 256, cols] = jnp.zeros((256, CHUNK), F32)
            blocks.append(d_conv.astype(BF16))
        halo2.push(c, select, blocks)
        return carry

    dk_src = s["dk_src"]

    def kernel_grad(h):
        def tap_sums(n, carry):
            cols = pl.ds(pl.multiple_of(h * HALF + n * 128, 128), 128)
            for u in range(UTT):
                grads = [ext_d[u, OWN + i * 8 : OWN + i * 8 + 8, cols] for i in range(32)]
                for base, acc in convolve(ext_g, u, cols, grads, 1):
                    for part in range(2):
                        row = base // 8 + part
                        folded = jnp.concatenate(
                            [jnp.sum(a, axis=0, keepdims=True) for a in acc[part * 8 : part * 8 + 8]],
                            axis=0,
                        )
                        if u == 0:
                            dk_src[h, row, :, span(n, 128)] = folded
                        else:
                            dk_src[h, row, :, span(n, 128)] += folded
            return carry

        lax.fori_loop(0, HALF // 128, tap_sums, 0)

    lax.fori_loop(0, 3, conv_grad, 0)
    ar2[1].step()
    kernel_grad(0)
    use_sums(1)
    lax.fori_loop(3, CHUNKS, conv_grad, 0)

    levels = []
    for p in range(3):
        rs.add_core(p, firsts[p])
        levels.append(rs.send_level(p, 0))

    dk = DKernel(net, dk_src, *[s[name] for name in DK_NAMES])
    kernel_grad(1)
    dk.start()
    grads = (s["d_proj0"], s["d_proj1"])

    def input_grad(c, d_proj):
        halo2.wait(c)
        for half in range(2):
            start = pl.multiple_of(c * CHUNK + half * 128, 128)
            cols = pl.ds(start, 128)
            taps = taps_of(cols)[::-1]
            lane = half * 128
            for u in range(UTT):
                low, high = halo_rows(halo2, c, u, lane)
                extend(ext_d, u, cols, low, high, row_id)
                for base, acc in convolve(ext_d, u, cols, taps, 0):
                    rows = pl.ds(u * 256 + base * 8, 128)
                    grad = jnp.concatenate(acc, axis=0)
                    sig = gs[rows, cols]
                    by_sig = grad * sig
                    d_proj[rows, lane : lane + 128] = by_sig.astype(BF16)
                    d_proj[rows, CHUNK + lane : CHUNK + lane + 128] = (
                        by_sig * val[rows, cols] * (1.0 - sig)
                    ).astype(BF16)

    def frame_grad(c, d_proj):
        cols = span(c, CHUNK)
        gate_cols = pl.ds(pl.multiple_of(D + c * CHUNK, CHUNK), CHUNK)
        for n in range(CHUNKS):
            rows = slice(n * CHUNK, n * CHUNK + CHUNK)
            weights = jnp.concatenate([w_in[rows, cols], w_in[rows, gate_cols]], axis=1)
            conv[:, rows] += dot_t(d_proj[...], weights)

    def both(j, carry):
        for odd in range(2):
            c = 2 * j + odd
            input_grad(c + 1, grads[1 - odd])
            frame_grad(c, grads[odd])
        return carry

    input_grad(0, grads[0])
    lax.fori_loop(0, 1, both, 0)
    dk.to_x()
    nexts = []
    for p in range(3):
        rs.add_level(p, 0, levels[p])
        nexts.append(rs.send_level(p, 1))
    lax.fori_loop(1, 2, both, 0)
    dk.to_z()
    levels = nexts
    nexts = []
    for p in range(3):
        rs.add_level(p, 1, levels[p])
        nexts.append(rs.send_level(p, 2))
    input_grad(5, grads[1])
    dk.to_y()
    frame_grad(4, grads[0])
    halo1.drain()
    halo2.drain()
    rs.exchange([rs.add_level(p, 2, nexts[p]) for p in range(3)])
    dk.gather_x()
    frame_grad(5, grads[1])
    dk.gather_core()

    def norm_grad(u):
        def tile(i, carry):
            rows = pl.ds(pl.multiple_of(u * 128 + i * 16, 16), 16)
            d_hat = conv[rows, :] * vec[0:1, :]
            rstd = rstd_ref[rows, :]
            hat = (x_p[rows, :].astype(F32) - mu_ref[rows, :]) * rstd
            m1 = jnp.mean(d_hat, axis=-1, keepdims=True)
            m2 = jnp.mean(d_hat * hat, axis=-1, keepdims=True)
            grad = rstd * (d_hat - m1 - hat * m2)
            act[rows, :] = (cot_p[rows, :].astype(F32) + grad).astype(BF16)
            return carry

        lax.fori_loop(0, 8, tile, 0, unroll=4)
        rows_u = pl.ds(u * 128, 128)
        copy = pltpu.make_async_copy(act.at[rows_u], din_hbm.at[rows_u], local.at[6 + u])
        copy.start()
        saves.append(copy)

    norm_grad(0)
    norm_grad(1)
    norm_grad(2)
    rs.finish(dw_ref)
    norm_grad(3)
    dk.finish(dk_ref)
    net.drain()
    for copy in saves:
        copy.wait()


RS_NAMES = ["got_core", "s1", "got1", "s2", "got2", "s3", "got3", "tail", "got_tail"]
DK_NAMES = ["dk%d" % i for i in range(len(DK_SCRATCH))]
VM = pltpu.VMEM
SCRATCH = [
    ("x_raw", VM((UTT, 256, D), BF16)),
    ("w_in", VM((D, 2 * D), BF16)),
    ("cot_raw", VM((UTT, 256, D), BF16)),
    ("w_out", VM((D, D), BF16)),
    ("perm", VM((256, 256), BF16)),
    ("win_sem", pltpu.SemaphoreType.DMA((CHUNKS, 2))),
    ("vec", VM((3, D), F32)),
    ("out_p", VM((ROWS, D), BF16)),
    ("eye", VM((256, 256), BF16)),
    ("select", VM((32, 256), BF16)),
    ("x_p", VM((ROWS, D), BF16)),
    ("bf", VM((ROWS, D), BF16)),
    ("mu", VM((ROWS, 1), F32)),
    ("rstd", VM((ROWS, 1), F32)),
    ("val", VM((ROWS, D), F32)),
    ("gs", VM((ROWS, D), F32)),
    ("ext_g", VM((UTT, 512, D), F32)),
    ("ext_d", VM((UTT, 512, D), F32)),
    ("conv", VM((ROWS, D), F32)),
    ("stat", VM((2, D), F32)),
    ("coef", VM((8, D), F32)),
    ("cot_p", VM((ROWS, D), BF16)),
    ("cot_t", VM((D, ROWS), BF16)),
    ("d_proj0", VM((ROWS, 2 * CHUNK), BF16)),
    ("d_proj1", VM((ROWS, 2 * CHUNK), BF16)),
    ("part", VM((2, 3, 4, 4, 4, 48, 128), BF16)),
    ("h_out1", VM((CHUNKS, 2, UTT, HALO, CHUNK), BF16)),
    ("h_got1", VM((CHUNKS, 2, UTT, HALO, CHUNK), BF16)),
    ("h_out2", VM((CHUNKS, 2, UTT, HALO, CHUNK), BF16)),
    ("h_got2", VM((CHUNKS, 2, UTT, HALO, CHUNK), BF16)),
    ("cur", VM((4, 4, 2, HALF), F32)),
    ("got", VM((4, 10, 2, HALF), F32)),
    ("dk_src", VM((2, 4, 8, HALF), F32)),
]
SCRATCH += list(zip(RS_NAMES, RS_SCRATCH)) + list(zip(DK_NAMES, DK_SCRATCH))
SCRATCH += [
    ("local_sem", pltpu.SemaphoreType.DMA((12,))),
    ("send_sem", pltpu.SemaphoreType.DMA((88,))),
    ("recv_sem", pltpu.SemaphoreType.DMA((88,))),
    ("h_send1", pltpu.SemaphoreType.DMA((CHUNKS, 2))),
    ("h_recv1", pltpu.SemaphoreType.DMA((CHUNKS, 2))),
    ("h_send2", pltpu.SemaphoreType.DMA((CHUNKS, 2))),
    ("h_recv2", pltpu.SemaphoreType.DMA((CHUNKS, 2))),
]


def finish_kernel(out_p, din_p, dw, dk, dbn, out_ref, din_ref, dw_out, dk_out, gain_out, bias_out, perm_t):
    @pl.when((pl.program_id(0) == 0) & (pl.program_id(1) == 0))
    def _():
        r0 = lax.broadcasted_iota(jnp.int32, (256, 256), 0)
        r1 = lax.broadcasted_iota(jnp.int32, (256, 256), 1)
        perm_t[...] = jnp.where(frame_of(r1) == r0, 1.0, 0.0).astype(BF16)
        dw_out[...] = dw[...]
        dk_out[...] = dk[...]
        gain_out[...] = dbn[0:1, :].reshape(D)
        bias_out[...] = dbn[1:2, :].reshape(D)

    out_ref[0] = dot(perm_t[...], out_p[...]).astype(BF16)
    din_ref[0] = dot(perm_t[...], din_p[...]).astype(BF16)


def on_device(inputs, ln_gain, w_in, kernel, bn_gain, bn_bias, w_out, cotangent):
    any_spec = pl.BlockSpec(memory_space=pl.ANY)
    vmem_spec = pl.BlockSpec(memory_space=pltpu.VMEM)
    flat = jax.ShapeDtypeStruct((ROWS, D), BF16)
    out_p, din_p, dw, dk, dbn = pl.pallas_call(
        functools.partial(whole_kernel, lax.axis_size("seq")),
        out_shape=(
            flat,
            flat,
            jax.ShapeDtypeStruct((D // 128, D), F32),
            jax.ShapeDtypeStruct((K, D), F32),
            jax.ShapeDtypeStruct((2, D), F32),
        ),
        in_specs=[any_spec, vmem_spec, any_spec, vmem_spec, vmem_spec, vmem_spec, any_spec, any_spec],
        out_specs=[any_spec, any_spec, vmem_spec, vmem_spec, vmem_spec],
        scratch_shapes=[spec for _, spec in SCRATCH],
        compiler_params=pltpu.CompilerParams(
            collective_id=0, has_side_effects=True, vmem_limit_bytes=67043328
        ),
    )(inputs, ln_gain, w_in, kernel, bn_gain, bn_bias, w_out, cotangent)

    def whole(shape):
        return pl.BlockSpec(shape, lambda u, c: (0,) * len(shape))

    wide = D // 2
    rows_spec = pl.BlockSpec((256, wide), lambda u, c: (u, c))
    block_spec = pl.BlockSpec((1, 256, wide), lambda u, c: (u, 0, c))
    full = jax.ShapeDtypeStruct((UTT, FRAMES_DEV, D), BF16)
    return pl.pallas_call(
        finish_kernel,
        grid=(UTT, 2),
        out_shape=(
            full,
            full,
            jax.ShapeDtypeStruct((D // 128, D), F32),
            jax.ShapeDtypeStruct((K, D), F32),
            jax.ShapeDtypeStruct((D,), F32),
            jax.ShapeDtypeStruct((D,), F32),
        ),
        in_specs=[rows_spec, rows_spec, whole((D // 128, D)), whole((K, D)), whole((2, D))],
        out_specs=[block_spec, block_spec, whole((D // 128, D)), whole((K, D)), whole((D,)), whole((D,))],
        scratch_shapes=[pltpu.VMEM((256, 256), BF16)],
    )(out_p, din_p, dw, dk, dbn)


def solution(mesh):
    return jax.shard_map(
        on_device,
        mesh=mesh,
        in_specs=(P(None, "seq", None), P(), P(), P(), P(), P(), P(), P(None, "seq", None)),
        out_specs=(P(None, "seq", None), P(None, "seq", None), P("seq", None), P(), P(), P()),
        check_vma=False,
    )
```

```python
import functools
import jax
import jax.numpy as jnp
from jax import lax
from jax.experimental import pallas as pl
from jax.experimental.pallas import tpu as pltpu
from jax.sharding import PartitionSpec as P

D = 1536
K = 32
FRAMES_DEV = 256
UTT = 2
EPSILON = 1e-05
F32 = jnp.float32
BF16 = jnp.bfloat16
STRIDE = {"core": 1, "z": 2, "y": 8, "x": 32}
SIZE = {"core": 2, "z": 4, "y": 4, "x": 4}
ORDERS = (("x", "y", "z"), ("y", "z", "x"), ("z", "x", "y"))
HALF = D // 2


def coord(me, axis):
    return lax.rem(me // STRIDE[axis], SIZE[axis])


def peers(me, axis):
    q = coord(me, axis)
    found = []
    for delta in range(1, SIZE[axis]):
        other = lax.rem(q + delta, SIZE[axis])
        found.append((other, me + (other - q) * STRIDE[axis]))
    return found


class Net:
    def __init__(self, me, send_sem, recv_sem):
        self.me, self.send_sem, self.recv_sem, self.used = me, send_sem, recv_sem, 0
        self.started = []

    def send(self, src, dst, device):
        slot = self.used
        self.used += 1
        copy = pltpu.make_async_remote_copy(
            src_ref=src,
            dst_ref=dst,
            send_sem=self.send_sem.at[slot],
            recv_sem=self.recv_sem.at[slot],
            device_id=(device,),
            device_id_type=pl.DeviceIdType.MESH,
        )
        copy.start()
        self.started.append(copy)
        return copy

    def drain(self):
        for copy in self.started:
            copy.wait_send()


def greet(me, axes, extra=()):
    barrier = pltpu.get_barrier_semaphore()
    count = 0
    for axis in axes:
        for _, device in peers(me, axis):
            pl.semaphore_signal(
                barrier, inc=1, device_id=(device,), device_id_type=pl.DeviceIdType.MESH
            )
            count += 1
    for device in extra:
        pl.semaphore_signal(
            barrier, inc=1, device_id=(device,), device_id_type=pl.DeviceIdType.MESH
        )
        count += 1
    return lambda: pl.semaphore_wait(barrier, count)


AXES = ("core", "z", "y", "x")


def merge_stats(parts, rows):
    mean = functools.reduce(jnp.add, [p[0:1] for p in parts]) * (1.0 / len(parts))
    spread = functools.reduce(jnp.add, [p[1:2] for p in parts])
    for p in parts:
        gap = p[0:1] - mean
        spread = spread + rows * gap * gap
    return jnp.concatenate([mean, spread], axis=0)


class DKernel:
    def __init__(self, net, src, core_buf, got_core, got_x, cz, got_z, cy, got_y, full, other):
        self.net = net
        self.src, self.core_buf, self.got_core = src, core_buf, got_core
        self.got_x, self.cz, self.got_z = got_x, cz, got_z
        self.cy, self.got_y, self.full, self.other = cy, got_y, full, other

    def start(self):
        me = self.net.me
        core = coord(me, "core")
        self.c0 = [self.net.send(self.src.at[1 - core], self.got_core, me + 1 - 2 * core)]

    def to_x(self):
        me = self.net.me
        core = coord(me, "core")
        x = coord(me, "x")
        self.c0[0].wait_recv()
        self.core_buf[...] = self.src[core] + self.got_core[...]
        self.cx_c = [
            self.net.send(self.core_buf.at[other], self.got_x.at[i], device)
            for i, (other, device) in enumerate(peers(me, "x"))
        ]

    def to_z(self):
        me = self.net.me
        total = self.core_buf[coord(me, "x")]
        for i, copy in enumerate(self.cx_c):
            copy.wait_recv()
            total = total + self.got_x[i]
        self.cz[...] = total
        self.cz_c = [
            self.net.send(self.cz, self.got_z.at[i], device)
            for i, (_, device) in enumerate(peers(me, "z"))
        ]

    def to_y(self):
        me = self.net.me
        total = self.cz[...]
        for i, copy in enumerate(self.cz_c):
            copy.wait_recv()
            total = total + self.got_z[i]
        self.cy[...] = total
        self.cy_c = [
            self.net.send(self.cy, self.got_y.at[i], device)
            for i, (_, device) in enumerate(peers(me, "y"))
        ]

    def gather_x(self):
        me = self.net.me
        total = self.cy[...]
        for i, copy in enumerate(self.cy_c):
            copy.wait_recv()
            total = total + self.got_y[i]
        x = coord(me, "x")
        self.full[x] = total
        self.gx_c = [
            self.net.send(self.full.at[x], self.full.at[x], device)
            for _, device in peers(me, "x")
        ]

    def gather_core(self):
        me = self.net.me
        core = coord(me, "core")
        for copy in self.gx_c:
            copy.wait_recv()
        self.gc_c = self.net.send(self.full, self.other, me + 1 - 2 * core)

    def finish(self, out):
        core = coord(self.net.me, "core")
        self.gc_c.wait_recv()
        for i in range(4):
            mine = self.full[i]
            theirs = self.other[i]
            out[pl.ds(8 * i, 8), 0:HALF] = jnp.where(core == 0, mine, theirs)
            out[pl.ds(8 * i, 8), HALF:D] = jnp.where(core == 0, theirs, mine)


DK_SCRATCH = [
    pltpu.VMEM((4, 8, HALF), F32),
    pltpu.VMEM((4, 8, HALF), F32),
    pltpu.VMEM((3, 8, HALF), F32),
    pltpu.VMEM((8, HALF), F32),
    pltpu.VMEM((3, 8, HALF), F32),
    pltpu.VMEM((8, HALF), F32),
    pltpu.VMEM((3, 8, HALF), F32),
    pltpu.VMEM((4, 8, HALF), F32),
    pltpu.VMEM((4, 8, HALF), F32),
]


def pick(ref, dims, axis, index):
    where = dims.index(axis)
    if where == 0:
        return ref.at[index]
    if where == 1:
        return ref.at[:, index]
    return ref.at[:, :, index]


class Scatter:
    def __init__(self, net, src, got_core, s1, got1, s2, got2, s3, got3, tail, got_tail):
        self.net, self.src, self.got_core = net, src, got_core
        self.s = [s1, s2, s3]
        self.got = [got1, got2, got3]
        self.tail, self.got_tail = tail, got_tail

    def start(self, part):
        me = self.net.me
        core = coord(me, "core")
        return self.net.send(self.src.at[1 - core, part], self.got_core.at[part], me + 1 - 2 * core)

    def dims(self, part, level):
        gone = ORDERS[part][:level]
        return [a for a in ("x", "y", "z") if a not in gone]

    def add_core(self, part, copy):
        core = coord(self.net.me, "core")
        copy.wait_recv()

        def body(i, carry):
            x, y = i // 4, lax.rem(i, 4)
            mine = self.src[core, part, x, y].astype(F32)
            theirs = self.got_core[part, x, y].astype(F32)
            self.s[0][part, x, y] = (mine + theirs).astype(BF16)
            return carry

        lax.fori_loop(0, 16, body, 0, unroll=2)

    def send_level(self, part, level):
        me = self.net.me
        axis = ORDERS[part][level]
        dims = self.dims(part, level)
        return [
            self.net.send(
                pick(self.s[level].at[part], dims, axis, other),
                self.got[level].at[part, i],
                device,
            )
            for i, (other, device) in enumerate(peers(me, axis))
        ]

    def add_level(self, part, level, copies):
        me = self.net.me
        axis = ORDERS[part][level]
        dims = self.dims(part, level)
        own = pick(self.s[level].at[part], dims, axis, coord(me, axis))
        for copy in copies:
            copy.wait_recv()
        got = self.got[level].at[part]
        if level == 2:
            total = own[...].astype(F32)
            for i in range(3):
                total = total + got[i].astype(F32)
            return total
        for a in range(4):
            total = own[a].astype(F32)
            for i in range(3):
                total = total + got[i, a].astype(F32)
            self.s[level + 1][part, a] = total.astype(BF16)

    def exchange(self, totals):
        core = coord(self.net.me, "core")
        self.mine = []
        for part in range(3):
            for half in range(2):
                low = totals[part][half * 24 : half * 24 + 12]
                high = totals[part][half * 24 + 12 : half * 24 + 24]
                self.mine.append(jnp.where(core == 0, low, high))
                self.tail[part * 2 + half] = jnp.where(core == 0, high, low)
        self.copy = self.net.send(self.tail, self.got_tail, self.net.me + 1 - 2 * core)

    def finish(self, out):
        core = coord(self.net.me, "core")
        self.copy.wait_recv()
        for piece in range(6):
            mine = self.mine[piece]
            theirs = self.got_tail[piece]
            out[:, piece * 128 : piece * 128 + 128] = jnp.where(core == 0, mine, theirs)
            out[:, HALF + piece * 128 : HALF + piece * 128 + 128] = jnp.where(core == 0, theirs, mine)


RS_SCRATCH = [
    pltpu.VMEM((3, 4, 4, 4, 48, 128), BF16),
    pltpu.VMEM((3, 4, 4, 4, 48, 128), BF16),
    pltpu.VMEM((3, 3, 4, 4, 48, 128), BF16),
    pltpu.VMEM((3, 4, 4, 48, 128), BF16),
    pltpu.VMEM((3, 3, 4, 48, 128), BF16),
    pltpu.VMEM((3, 4, 48, 128), BF16),
    pltpu.VMEM((3, 3, 48, 128), BF16),
    pltpu.VMEM((6, 12, 128), F32),
    pltpu.VMEM((6, 12, 128), F32),
]


class Reduce:
    def __init__(self, net, merge, cur, got):
        self.net, self.merge, self.cur, self.got = net, merge, cur, got
        self.rows, self.level, self.slot = float(UTT * FRAMES_DEV), 0, 0

    def start(self, value):
        self.value = value
        self.cur[self.level] = value
        self.copies = []
        for _, device in peers(self.net.me, AXES[self.level]):
            self.copies.append(
                (self.net.send(self.cur.at[self.level], self.got.at[self.slot], device), self.slot)
            )
            self.slot += 1

    def take(self):
        parts = [self.value]
        for copy, index in self.copies:
            copy.wait_recv()
            parts.append(self.got[index])
        if self.merge:
            value = merge_stats(parts, self.rows)
        else:
            value = functools.reduce(jnp.add, parts)
        self.rows *= SIZE[AXES[self.level]]
        self.level += 1
        return value

    def step(self):
        self.start(self.take())


ROWS = UTT * FRAMES_DEV
CHUNK = 256
CHUNKS = D // CHUNK
HALO = 16
OWN = HALO * 8


def dot(a, b):
    return jnp.dot(a, b, preferred_element_type=F32)


def dot_t(a, b):
    return lax.dot_general(a, b, (((1,), (1,)), ((), ())), preferred_element_type=F32)


def span(index, size):
    return pl.ds(pl.multiple_of(index * size, size), size)


def frame_of(row):
    return (row & 7) * 32 + (row >> 3)


def fold(x):
    return jnp.sum(x.reshape(x.shape[0] // 8, 8, x.shape[1]), axis=0)


class Halo:
    def __init__(self, me, devices, out, got, send_sem, recv_sem):
        self.out, self.got, self.send_sem, self.recv_sem = out, got, send_sem, recv_sem
        self.right = lax.rem(me + 1, devices)
        self.left = lax.rem(me + devices - 1, devices)

    def copies(self, c):
        return [
            pltpu.make_async_remote_copy(
                src_ref=self.out.at[c, way],
                dst_ref=self.got.at[c, way],
                send_sem=self.send_sem.at[c, way],
                recv_sem=self.recv_sem.at[c, way],
                device_id=(device,),
                device_id_type=pl.DeviceIdType.MESH,
            )
            for way, device in enumerate((self.right, self.left))
        ]

    def push(self, c, select, blocks):
        for u in range(UTT):
            edge = dot(select[...], blocks[u]).astype(BF16)
            self.out[c, 0, u] = edge[0:HALO]
            self.out[c, 1, u] = edge[HALO : 2 * HALO]
        for copy in self.copies(c):
            copy.start()

    def wait(self, c):
        for copy in self.copies(c):
            copy.wait_recv()

    def drain(self):
        for c in range(CHUNKS):
            for copy in self.copies(c):
                copy.wait_send()


def extend(ext, u, cols, low, high, row_id):
    for j in range(HALO):
        below = pltpu.roll(ext[u, OWN + (16 + j) * 8 : OWN + (17 + j) * 8, cols], 1, 0)
        ext[u, j * 8 : j * 8 + 8, cols] = jnp.where(row_id == 0, low[j : j + 1], below)
        above = pltpu.roll(ext[u, OWN + j * 8 : OWN + j * 8 + 8, cols], 7, 0)
        ext[u, (48 + j) * 8 : (49 + j) * 8, cols] = jnp.where(row_id == 7, high[j : j + 1], above)


def convolve(ext, u, cols, taps, offset):
    low, high = taps[0::2], taps[1::2]
    both = [a + b for a, b in zip(low, high)]

    def x(n):
        return ext[u, (n + offset) * 8 : (n + offset) * 8 + 8, cols]

    def product(weights, source, start, first):
        acc = list(start)
        for n in range(first, first + 23):
            value = source(n)
            for p in range(8):
                m = n - first - p
                if 0 <= m < 16:
                    term = weights[m] * value
                    acc[p] = term if acc[p] is None else acc[p] + term
        return acc

    for first in (0, 8):
        shared = product(both, lambda n: x(2 * n + 1), [None] * 8, first)
        even = product(low, lambda n: x(2 * n) - x(2 * n + 1), shared, first)
        odd = product(high, lambda n: x(2 * n + 2) - x(2 * n + 1), shared, first)
        yield 2 * first, [v for pair in zip(even, odd) for v in pair]


def whole_kernel(n_dev, x_hbm, lng_ref, win_hbm, ker_ref, bng_ref, bnb_ref, wout_hbm, cot_hbm,
                 out_hbm, din_hbm, dw_ref, dk_ref, dbn_ref, *scratch):
    s = dict(zip([name for name, _ in SCRATCH], scratch))
    me = lax.axis_index("seq")
    local = s["local_sem"]
    load_x = [pltpu.make_async_copy(x_hbm.at[u], s["x_raw"].at[u], local.at[u]) for u in range(UTT)]
    load_cot = pltpu.make_async_copy(cot_hbm, s["cot_raw"], local.at[2])
    load_out = pltpu.make_async_copy(wout_hbm, s["w_out"], local.at[3])

    def load_in(c):
        found = []
        for side in range(2):
            cols = pl.ds(pl.multiple_of(side * D + c * CHUNK, CHUNK), CHUNK)
            found.append(
                pltpu.make_async_copy(win_hbm.at[:, cols], s["w_in"].at[:, cols], s["win_sem"].at[c, side])
            )
        return found

    for copy in load_x:
        copy.start()
    vec = s["vec"]
    for row, ref in enumerate((lng_ref, bng_ref, bnb_ref)):
        vec[row : row + 1, :] = ref[...].reshape(1, D)
    net = Net(me, s["send_sem"], s["recv_sem"])
    halo1 = Halo(me, n_dev, s["h_out1"], s["h_got1"], s["h_send1"], s["h_recv1"])
    halo2 = Halo(me, n_dev, s["h_out2"], s["h_got2"], s["h_send2"], s["h_recv2"])

    entered = greet(me, AXES, (halo1.left, halo1.right))
    perm, eye, select = s["perm"], s["eye"], s["select"]
    r0 = lax.broadcasted_iota(jnp.int32, (256, 256), 0)
    r1 = lax.broadcasted_iota(jnp.int32, (256, 256), 1)
    perm[...] = jnp.where(frame_of(r0) == r1, 1.0, 0.0).astype(BF16)
    eye[...] = jnp.where(r0 == r1, 1.0, 0.0).astype(BF16)
    q0 = lax.broadcasted_iota(jnp.int32, (32, 256), 0)
    q1 = lax.broadcasted_iota(jnp.int32, (32, 256), 1)
    edge_frame = jnp.where(q0 < HALO, FRAMES_DEV - HALO + q0, q0 - HALO)
    select[...] = jnp.where(frame_of(q1) == edge_frame, 1.0, 0.0).astype(BF16)
    row_id = lax.broadcasted_iota(jnp.int32, (8, 128), 0)

    x_p, normed, mu_ref, rstd_ref = s["x_p"], s["bf"], s["mu"], s["rstd"]
    for copy in load_x:
        copy.wait()
    for c in range(CHUNKS):
        for copy in load_in(c):
            copy.start()

    def permute(c, carry):
        cols = span(c, CHUNK)
        for u in range(UTT):
            x_p[u * 256 : u * 256 + 256, cols] = dot(perm[...], s["x_raw"][u, :, cols]).astype(BF16)
        return carry

    lax.fori_loop(0, CHUNKS, permute, 0, unroll=2)

    def norm_tile(i, carry):
        rows = span(i, 16)
        x = x_p[rows, :].astype(F32)
        mean = jnp.mean(x, axis=-1, keepdims=True)
        gap = x - mean
        rstd = lax.rsqrt(jnp.mean(gap * gap, axis=-1, keepdims=True) + EPSILON)
        mu_ref[rows, :] = mean
        rstd_ref[rows, :] = rstd
        normed[rows, :] = (gap * rstd * vec[0:1, :]).astype(BF16)
        return carry

    lax.fori_loop(0, ROWS // 16, norm_tile, 0, unroll=4)
    entered()
    w_in, val, gs, ext_g, ext_d = s["w_in"], s["val"], s["gs"], s["ext_g"], s["ext_d"]

    def project(c, carry):
        for copy in load_in(c):
            copy.wait()
        project_chunk(c)
        return carry

    def project_chunk(c):
        cols = span(c, CHUNK)
        val[:, cols] = dot(normed[...], w_in[:, cols])
        gate_cols = pl.ds(pl.multiple_of(D + c * CHUNK, CHUNK), CHUNK)
        gs[:, cols] = dot(normed[...], w_in[:, gate_cols])
        blocks = []
        for u in range(UTT):
            rows = pl.ds(u * 256, 256)
            sig = jax.nn.sigmoid(gs[rows, cols])
            gs[rows, cols] = sig
            gated = (val[rows, cols] * sig).astype(BF16)
            ext_g[u, OWN : OWN + 256, cols] = gated.astype(F32)
            blocks.append(gated)
        halo1.push(c, select, blocks)

    lax.fori_loop(0, CHUNKS, project, 0)
    load_cot.start()
    load_out.start()

    def halo_rows(halo, c, u, lane):
        low = halo.got[c, 0, u, :, lane : lane + 128].astype(F32)
        high = halo.got[c, 1, u, :, lane : lane + 128].astype(F32)
        return jnp.where(me == 0, 0.0, low), jnp.where(me == n_dev - 1, 0.0, high)

    conv, stat = s["conv"], s["stat"]

    def taps_of(cols):
        return [jnp.broadcast_to(ker_ref[k : k + 1, cols], (8, 128)) for k in range(K)]

    def conv_only(c, carry):
        halo1.wait(c)
        conv_chunk(c)
        return carry

    def conv_chunk(c):
        for half in range(2):
            cols = pl.ds(pl.multiple_of(c * CHUNK + half * 128, 128), 128)
            taps = taps_of(cols)
            total = jnp.zeros((8, 128), F32)
            for u in range(UTT):
                low, high = halo_rows(halo1, c, u, half * 128)
                extend(ext_g, u, cols, low, high, row_id)
                for base, acc in convolve(ext_g, u, cols, taps, 1):
                    for o in range(16):
                        conv[pl.ds(u * 256 + (base + o) * 8, 8), cols] = acc[o]
                        total = total + acc[o]
            mean = jnp.sum(total, axis=0, keepdims=True) * (1.0 / ROWS)
            gap = conv[:, cols] - mean
            stat[0:1, cols] = mean
            stat[1:2, cols] = jnp.sum(fold(gap * gap), axis=0, keepdims=True)

    wide = (slice(0, HALF), slice(HALF, D))
    ar1 = [Reduce(net, True, s["cur"].at[h], s["got"].at[h]) for h in range(2)]
    ar2 = [Reduce(net, False, s["cur"].at[2 + h], s["got"].at[2 + h]) for h in range(2)]
    lax.fori_loop(0, 3, conv_only, 0)
    ar1[0].start(stat[:, wide[0]])
    lax.fori_loop(3, 4, conv_only, 0)
    ar1[0].step()
    lax.fori_loop(4, CHUNKS, conv_only, 0)
    ar1[0].step()
    ar1[1].start(stat[:, wide[1]])
    load_cot.wait()
    cot_p, cot_t, w_out = s["cot_p"], s["cot_t"], s["w_out"]

    def turn(c, carry):
        cols = span(c, CHUNK)
        for u in range(UTT):
            cot_p[u * 256 : u * 256 + 256, cols] = dot(perm[...], s["cot_raw"][u, :, cols]).astype(BF16)
        cot_t[cols, :] = dot_t(eye[...], cot_p[:, cols]).astype(BF16)
        return carry

    lax.fori_loop(0, CHUNKS, turn, 0, unroll=2)
    ar1[1].step()
    ar1[0].step()
    load_out.wait()

    def act_grad(c, carry):
        cols = span(c, CHUNK)
        res = dot(cot_p[...], w_out[:, cols])
        for u in range(UTT):
            ext_d[u, OWN : OWN + 256, cols] = res[u * 256 : u * 256 + 256]
        return carry

    total_rows = float(ROWS * n_dev)
    coef = s["coef"]

    def use_stats(h):
        stats = ar1[h].take()
        coef[0:1, wide[h]] = stats[0:1]
        coef[1:2, wide[h]] = lax.rsqrt(stats[1:2] * (1.0 / total_rows) + EPSILON)

    lax.fori_loop(0, CHUNKS // 2, act_grad, 0)
    ar1[1].step()
    lax.fori_loop(CHUNKS // 2, CHUNKS, act_grad, 0)
    use_stats(0)
    act = s["bf"]

    def bn_block(cb, carry):
        cols = span(cb, 128)
        mean, rstd = coef[0:1, cols], coef[1:2, cols]
        gain, bias = vec[1:2, cols], vec[2:3, cols]
        sum_bias = jnp.zeros((8, 128), F32)
        sum_gain = jnp.zeros((8, 128), F32)
        for u in range(UTT):
            rows = pl.ds(u * 256, 256)
            xhat = (conv[rows, cols] - mean) * rstd
            bn = xhat * gain + bias
            sig = jax.nn.sigmoid(bn)
            conv[rows, cols] = xhat
            act[rows, cols] = (bn * sig).astype(BF16)
            d_bn = ext_d[u, OWN : OWN + 256, cols] * (sig + bn * sig * (1.0 - sig))
            ext_d[u, OWN : OWN + 256, cols] = d_bn
            sum_bias = sum_bias + fold(d_bn)
            sum_gain = sum_gain + fold(d_bn * xhat)
        stat[0:1, cols] = jnp.sum(sum_gain, axis=0, keepdims=True)
        stat[1:2, cols] = jnp.sum(sum_bias, axis=0, keepdims=True)
        return carry

    core = coord(me, "core")
    part_ref = s["part"]
    rs = Scatter(net, part_ref, *[s[name] for name in RS_NAMES])

    def weight_part(h, p):
        cols = pl.ds(pl.multiple_of(h * HALF + p * CHUNK, CHUNK), CHUNK)

        def weight_tile(m, carry):
            res = dot(cot_t[span(m, 384), :], act[:, cols])
            for j in range(16):
                piece = res[j * 24 : j * 24 + 24]
                piece = jnp.concatenate([piece[:, 0:128], piece[:, 128:256]], axis=0).astype(BF16)
                part_ref[h, p, m, j // 4, j % 4] = piece
            return carry

        lax.fori_loop(0, 4, weight_tile, 0, unroll=2)

    saves = []

    def branch(n, carry):
        cols = span(n, CHUNK)
        res = dot_t(act[...], w_out[cols, :])
        s["out_p"][:, cols] = (x_p[:, cols].astype(F32) + res).astype(BF16)
        return carry

    def use_sums(h):
        sums = ar2[h].take()
        s["dbn_s"][:, wide[h]] = sums
        gain_row = vec[1:2, wide[h]]
        rstd_row = coef[1:2, wide[h]]
        coef[2:3, wide[h]] = rstd_row * gain_row
        coef[3:4, wide[h]] = rstd_row * (gain_row * sums[1:2] * (1.0 / total_rows))
        coef[4:5, wide[h]] = rstd_row * (gain_row * sums[0:1] * (1.0 / total_rows))

    lax.fori_loop(0, 6, bn_block, 0)
    ar1[1].step()
    ar2[0].start(stat[:, wide[0]])
    weight_part(0, 0)
    weight_part(0, 1)
    ar2[0].step()
    weight_part(0, 2)
    use_stats(1)
    lax.fori_loop(6, 12, bn_block, 0)
    ar2[0].step()
    ar2[1].start(stat[:, wide[1]])
    weight_part(1, 0)
    weight_part(1, 1)
    ar2[1].step()
    weight_part(1, 2)
    firsts = {p: rs.start(p) for p in (2, 1, 0)}
    lax.fori_loop(0, CHUNKS // 2, branch, 0)
    ar2[0].step()
    ar2[1].step()
    lax.fori_loop(CHUNKS // 2, CHUNKS, branch, 0)
    copy = pltpu.make_async_copy(s["out_p"], out_hbm, local.at[4])
    copy.start()
    saves.append(copy)
    use_sums(0)

    def conv_grad(c, carry):
        cols = span(c, CHUNK)
        blocks = []
        for u in range(UTT):
            d_bn = ext_d[u, OWN : OWN + 256, cols]
            xhat = conv[u * 256 : u * 256 + 256, cols]
            d_conv = d_bn * coef[2:3, cols] - coef[3:4, cols] - xhat * coef[4:5, cols]
            ext_d[u, OWN : OWN + 256, cols] = d_conv
            blocks.append(d_conv.astype(BF16))
        halo2.push(c, select, blocks)
        return carry

    dk_src = s["dk_src"]

    def kernel_grad(h):
        def tap_sums(n, carry):
            cols = pl.ds(pl.multiple_of(h * HALF + n * 128, 128), 128)
            for u in range(UTT):
                grads = [ext_d[u, OWN + i * 8 : OWN + i * 8 + 8, cols] for i in range(32)]
                for base, acc in convolve(ext_g, u, cols, grads, 1):
                    for part in range(2):
                        row = base // 8 + part
                        folded = jnp.concatenate(
                            [jnp.sum(a, axis=0, keepdims=True) for a in acc[part * 8 : part * 8 + 8]],
                            axis=0,
                        )
                        if u == 0:
                            dk_src[h, row, :, span(n, 128)] = folded
                        else:
                            dk_src[h, row, :, span(n, 128)] += folded
            return carry

        lax.fori_loop(0, HALF // 128, tap_sums, 0)

    lax.fori_loop(0, 3, conv_grad, 0)
    ar2[1].step()
    levels = {}
    for p in (2, 1, 0):
        rs.add_core(p, firsts[p])
        levels[p] = rs.send_level(p, 0)
    kernel_grad(0)
    use_sums(1)
    lax.fori_loop(3, CHUNKS, conv_grad, 0)

    dk = DKernel(net, dk_src, *[s[name] for name in DK_NAMES])
    kernel_grad(1)
    dk.start()
    grads = (s["d_proj0"], s["d_proj1"])

    def input_grad(c, d_proj):
        halo2.wait(c)
        for half in range(2):
            start = pl.multiple_of(c * CHUNK + half * 128, 128)
            cols = pl.ds(start, 128)
            taps = taps_of(cols)[::-1]
            lane = half * 128
            for u in range(UTT):
                low, high = halo_rows(halo2, c, u, lane)
                extend(ext_d, u, cols, low, high, row_id)
                for base, acc in convolve(ext_d, u, cols, taps, 0):
                    rows = pl.ds(u * 256 + base * 8, 128)
                    grad = jnp.concatenate(acc, axis=0)
                    sig = gs[rows, cols]
                    by_sig = grad * sig
                    d_proj[rows, lane : lane + 128] = by_sig.astype(BF16)
                    d_proj[rows, CHUNK + lane : CHUNK + lane + 128] = (
                        by_sig * val[rows, cols] * (1.0 - sig)
                    ).astype(BF16)

    def frame_grad(c, d_proj):
        cols = span(c, CHUNK)
        gate_cols = pl.ds(pl.multiple_of(D + c * CHUNK, CHUNK), CHUNK)
        for n in range(CHUNKS):
            rows = slice(n * CHUNK, n * CHUNK + CHUNK)
            weights = jnp.concatenate([w_in[rows, cols], w_in[rows, gate_cols]], axis=1)
            if c == 0:
                conv[:, rows] = dot_t(d_proj[...], weights)
            else:
                conv[:, rows] += dot_t(d_proj[...], weights)

    def pair(c):
        input_grad(c + 1, grads[1 - c % 2])
        frame_grad(c, grads[c % 2])

    def next_level(level):
        found = {}
        for p in (2, 1, 0):
            rs.add_level(p, level, levels[p])
            found[p] = rs.send_level(p, level + 1)
        return found

    input_grad(0, grads[0])
    pair(0)
    dk.to_x()
    pair(1)
    dk.to_z()
    levels = next_level(0)
    pair(2)
    dk.to_y()
    pair(3)
    dk.gather_x()
    levels = next_level(1)
    input_grad(5, grads[1])
    halo1.drain()
    halo2.drain()
    dk.gather_core()
    frame_grad(4, grads[0])
    frame_grad(5, grads[1])
    rs.exchange([rs.add_level(p, 2, levels[p]) for p in range(3)])

    def leave(src, dst, sem):
        copy = pltpu.make_async_copy(src, dst, local.at[sem])
        copy.start()
        saves.append(copy)

    leave(s["dbn_s"], dbn_ref, 10)

    def norm_grad(u):
        def tile(i, carry):
            rows = pl.ds(pl.multiple_of(u * 128 + i * 16, 16), 16)
            d_hat = conv[rows, :] * vec[0:1, :]
            rstd = rstd_ref[rows, :]
            hat = (x_p[rows, :].astype(F32) - mu_ref[rows, :]) * rstd
            m1 = jnp.mean(d_hat, axis=-1, keepdims=True)
            m2 = jnp.mean(d_hat * hat, axis=-1, keepdims=True)
            grad = rstd * (d_hat - m1 - hat * m2)
            act[rows, :] = (cot_p[rows, :].astype(F32) + grad).astype(BF16)
            return carry

        lax.fori_loop(0, 8, tile, 0, unroll=4)
        rows_u = pl.ds(u * 128, 128)
        copy = pltpu.make_async_copy(act.at[rows_u], din_hbm.at[rows_u], local.at[6 + u])
        copy.start()
        saves.append(copy)

    norm_grad(0)
    norm_grad(1)
    dk.finish(s["dk_s"])
    leave(s["dk_s"], dk_ref, 11)
    norm_grad(2)
    rs.finish(s["dw_s"])
    leave(s["dw_s"], dw_ref, 5)
    norm_grad(3)
    net.drain()
    for copy in saves:
        copy.wait()


RS_NAMES = ["got_core", "s1", "got1", "s2", "got2", "s3", "got3", "tail", "got_tail"]
DK_NAMES = ["dk%d" % i for i in range(len(DK_SCRATCH))]
VM = pltpu.VMEM
SCRATCH = [
    ("x_raw", VM((UTT, 256, D), BF16)),
    ("w_in", VM((D, 2 * D), BF16)),
    ("cot_raw", VM((UTT, 256, D), BF16)),
    ("w_out", VM((D, D), BF16)),
    ("perm", VM((256, 256), BF16)),
    ("win_sem", pltpu.SemaphoreType.DMA((CHUNKS, 2))),
    ("vec", VM((3, D), F32)),
    ("out_p", VM((ROWS, D), BF16)),
    ("eye", VM((256, 256), BF16)),
    ("select", VM((32, 256), BF16)),
    ("x_p", VM((ROWS, D), BF16)),
    ("bf", VM((ROWS, D), BF16)),
    ("mu", VM((ROWS, 1), F32)),
    ("rstd", VM((ROWS, 1), F32)),
    ("val", VM((ROWS, D), F32)),
    ("gs", VM((ROWS, D), F32)),
    ("ext_g", VM((UTT, 512, D), F32)),
    ("ext_d", VM((UTT, 512, D), F32)),
    ("conv", VM((ROWS, D), F32)),
    ("dbn_s", VM((2, D), F32)),
    ("dk_s", VM((K, D), F32)),
    ("dw_s", VM((D // 128, D), F32)),
    ("stat", VM((2, D), F32)),
    ("coef", VM((8, D), F32)),
    ("cot_p", VM((ROWS, D), BF16)),
    ("cot_t", VM((D, ROWS), BF16)),
    ("d_proj0", VM((ROWS, 2 * CHUNK), BF16)),
    ("d_proj1", VM((ROWS, 2 * CHUNK), BF16)),
    ("part", VM((2, 3, 4, 4, 4, 48, 128), BF16)),
    ("h_out1", VM((CHUNKS, 2, UTT, HALO, CHUNK), BF16)),
    ("h_got1", VM((CHUNKS, 2, UTT, HALO, CHUNK), BF16)),
    ("h_out2", VM((CHUNKS, 2, UTT, HALO, CHUNK), BF16)),
    ("h_got2", VM((CHUNKS, 2, UTT, HALO, CHUNK), BF16)),
    ("cur", VM((4, 4, 2, HALF), F32)),
    ("got", VM((4, 10, 2, HALF), F32)),
    ("dk_src", VM((2, 4, 8, HALF), F32)),
]
SCRATCH += list(zip(RS_NAMES, RS_SCRATCH)) + list(zip(DK_NAMES, DK_SCRATCH))
SCRATCH += [
    ("local_sem", pltpu.SemaphoreType.DMA((12,))),
    ("send_sem", pltpu.SemaphoreType.DMA((88,))),
    ("recv_sem", pltpu.SemaphoreType.DMA((88,))),
    ("h_send1", pltpu.SemaphoreType.DMA((CHUNKS, 2))),
    ("h_recv1", pltpu.SemaphoreType.DMA((CHUNKS, 2))),
    ("h_send2", pltpu.SemaphoreType.DMA((CHUNKS, 2))),
    ("h_recv2", pltpu.SemaphoreType.DMA((CHUNKS, 2))),
]


def finish_kernel(out_p, din_p, dw, dk, dbn, out_ref, din_ref, dw_out, dk_out, gain_out, bias_out, perm_t):
    @pl.when((pl.program_id(0) == 0) & (pl.program_id(1) == 0))
    def _():
        r0 = lax.broadcasted_iota(jnp.int32, (256, 256), 0)
        r1 = lax.broadcasted_iota(jnp.int32, (256, 256), 1)
        perm_t[...] = jnp.where(frame_of(r1) == r0, 1.0, 0.0).astype(BF16)
        dw_out[...] = dw[...]
        dk_out[...] = dk[...]
        gain_out[...] = dbn[0:1, :].reshape(D)
        bias_out[...] = dbn[1:2, :].reshape(D)

    out_ref[0] = dot(perm_t[...], out_p[...]).astype(BF16)
    din_ref[0] = dot(perm_t[...], din_p[...]).astype(BF16)


def on_device(inputs, ln_gain, w_in, kernel, bn_gain, bn_bias, w_out, cotangent):
    any_spec = pl.BlockSpec(memory_space=pl.ANY)
    vmem_spec = pl.BlockSpec(memory_space=pltpu.VMEM)
    flat = jax.ShapeDtypeStruct((ROWS, D), BF16)
    out_p, din_p, dw, dk, dbn = pl.pallas_call(
        functools.partial(whole_kernel, lax.axis_size("seq")),
        out_shape=(
            flat,
            flat,
            jax.ShapeDtypeStruct((D // 128, D), F32),
            jax.ShapeDtypeStruct((K, D), F32),
            jax.ShapeDtypeStruct((2, D), F32),
        ),
        in_specs=[any_spec, vmem_spec, any_spec, vmem_spec, vmem_spec, vmem_spec, any_spec, any_spec],
        out_specs=[any_spec] * 5,
        scratch_shapes=[spec for _, spec in SCRATCH],
        compiler_params=pltpu.CompilerParams(
            collective_id=0, has_side_effects=True, vmem_limit_bytes=67043328
        ),
    )(inputs, ln_gain, w_in, kernel, bn_gain, bn_bias, w_out, cotangent)

    def whole(shape):
        return pl.BlockSpec(shape, lambda u, c: (0,) * len(shape))

    wide = D // 2
    rows_spec = pl.BlockSpec((256, wide), lambda u, c: (u, c))
    block_spec = pl.BlockSpec((1, 256, wide), lambda u, c: (u, 0, c))
    full = jax.ShapeDtypeStruct((UTT, FRAMES_DEV, D), BF16)
    return pl.pallas_call(
        finish_kernel,
        grid=(UTT, 2),
        out_shape=(
            full,
            full,
            jax.ShapeDtypeStruct((D // 128, D), F32),
            jax.ShapeDtypeStruct((K, D), F32),
            jax.ShapeDtypeStruct((D,), F32),
            jax.ShapeDtypeStruct((D,), F32),
        ),
        in_specs=[rows_spec, rows_spec, whole((D // 128, D)), whole((K, D)), whole((2, D))],
        out_specs=[block_spec, block_spec, whole((D // 128, D)), whole((K, D)), whole((D,)), whole((D,))],
        scratch_shapes=[pltpu.VMEM((256, 256), BF16)],
    )(out_p, din_p, dw, dk, dbn)


def solution(mesh):
    return jax.shard_map(
        on_device,
        mesh=mesh,
        in_specs=(P(None, "seq", None), P(), P(), P(), P(), P(), P(), P(None, "seq", None)),
        out_specs=(P(None, "seq", None), P(None, "seq", None), P("seq", None), P(), P(), P()),
        check_vma=False,
    )
```

```python
import functools
import jax
import jax.numpy as jnp
from jax import lax
from jax.experimental import pallas as pl
from jax.experimental.pallas import tpu as pltpu
from jax.sharding import PartitionSpec as P

D = 1536
K = 32
FRAMES_DEV = 256
UTT = 2
EPSILON = 1e-05
F32 = jnp.float32
BF16 = jnp.bfloat16
STRIDE = {"core": 1, "z": 2, "y": 8, "x": 32}
SIZE = {"core": 2, "z": 4, "y": 4, "x": 4}
ORDERS = (("x", "y", "z"), ("y", "z", "x"), ("z", "x", "y"))
HALF = D // 2


def coord(me, axis):
    return lax.rem(me // STRIDE[axis], SIZE[axis])


def peers(me, axis):
    q = coord(me, axis)
    found = []
    for delta in range(1, SIZE[axis]):
        other = lax.rem(q + delta, SIZE[axis])
        found.append((other, me + (other - q) * STRIDE[axis]))
    return found


class Net:
    def __init__(self, me, send_sem, recv_sem):
        self.me, self.send_sem, self.recv_sem, self.used = me, send_sem, recv_sem, 0
        self.started = []

    def send(self, src, dst, device):
        slot = self.used
        self.used += 1
        copy = pltpu.make_async_remote_copy(
            src_ref=src,
            dst_ref=dst,
            send_sem=self.send_sem.at[slot],
            recv_sem=self.recv_sem.at[slot],
            device_id=(device,),
            device_id_type=pl.DeviceIdType.MESH,
        )
        copy.start()
        self.started.append(copy)
        return copy

    def drain(self):
        for copy in self.started:
            copy.wait_send()


def greet(me, axes, extra=()):
    barrier = pltpu.get_barrier_semaphore()
    count = 0
    for axis in axes:
        for _, device in peers(me, axis):
            pl.semaphore_signal(
                barrier, inc=1, device_id=(device,), device_id_type=pl.DeviceIdType.MESH
            )
            count += 1
    for device in extra:
        pl.semaphore_signal(
            barrier, inc=1, device_id=(device,), device_id_type=pl.DeviceIdType.MESH
        )
        count += 1
    return lambda: pl.semaphore_wait(barrier, count)


AXES = ("core", "z", "y", "x")


def merge_stats(parts, rows):
    mean = functools.reduce(jnp.add, [p[0:1] for p in parts]) * (1.0 / len(parts))
    spread = functools.reduce(jnp.add, [p[1:2] for p in parts])
    for p in parts:
        gap = p[0:1] - mean
        spread = spread + rows * gap * gap
    return jnp.concatenate([mean, spread], axis=0)


class DKernel:
    def __init__(self, net, src, sent, core_buf, got_core, got_x, cz, got_z, cy, got_y, full, other):
        self.net = net
        self.src, self.sent, self.core_buf, self.got_core = src, sent, core_buf, got_core
        self.got_x, self.cz, self.got_z = got_x, cz, got_z
        self.cy, self.got_y, self.full, self.other = cy, got_y, full, other

    def start(self):
        me = self.net.me
        core = coord(me, "core")
        self.sent[...] = self.src[1 - core].astype(BF16)
        self.c0 = [self.net.send(self.sent, self.got_core, me + 1 - 2 * core)]

    def to_x(self):
        me = self.net.me
        core = coord(me, "core")
        x = coord(me, "x")
        self.c0[0].wait_recv()
        self.core_buf[...] = (self.src[core] + self.got_core[...].astype(F32)).astype(BF16)
        self.cx_c = [
            self.net.send(self.core_buf.at[other], self.got_x.at[i], device)
            for i, (other, device) in enumerate(peers(me, "x"))
        ]

    def to_z(self):
        me = self.net.me
        total = self.core_buf[coord(me, "x")].astype(F32)
        for i, copy in enumerate(self.cx_c):
            copy.wait_recv()
            total = total + self.got_x[i].astype(F32)
        self.cz[...] = total.astype(BF16)
        self.cz_c = [
            self.net.send(self.cz, self.got_z.at[i], device)
            for i, (_, device) in enumerate(peers(me, "z"))
        ]

    def to_y(self):
        me = self.net.me
        total = self.cz[...].astype(F32)
        for i, copy in enumerate(self.cz_c):
            copy.wait_recv()
            total = total + self.got_z[i].astype(F32)
        self.cy[...] = total.astype(BF16)
        self.cy_c = [
            self.net.send(self.cy, self.got_y.at[i], device)
            for i, (_, device) in enumerate(peers(me, "y"))
        ]

    def gather_x(self):
        me = self.net.me
        total = self.cy[...].astype(F32)
        for i, copy in enumerate(self.cy_c):
            copy.wait_recv()
            total = total + self.got_y[i].astype(F32)
        x = coord(me, "x")
        self.full[x] = total.astype(BF16)
        self.gx_c = [
            self.net.send(self.full.at[x], self.full.at[x], device)
            for _, device in peers(me, "x")
        ]

    def gather_core(self):
        me = self.net.me
        core = coord(me, "core")
        for copy in self.gx_c:
            copy.wait_recv()
        self.gc_c = self.net.send(self.full, self.other, me + 1 - 2 * core)

    def finish(self, out):
        core = coord(self.net.me, "core")
        self.gc_c.wait_recv()
        for i in range(4):
            mine = self.full[i].astype(F32)
            theirs = self.other[i].astype(F32)
            out[pl.ds(8 * i, 8), 0:HALF] = jnp.where(core == 0, mine, theirs)
            out[pl.ds(8 * i, 8), HALF:D] = jnp.where(core == 0, theirs, mine)


DK_SCRATCH = [
    pltpu.VMEM((4, 8, HALF), BF16),
    pltpu.VMEM((4, 8, HALF), BF16),
    pltpu.VMEM((4, 8, HALF), BF16),
    pltpu.VMEM((3, 8, HALF), BF16),
    pltpu.VMEM((8, HALF), BF16),
    pltpu.VMEM((3, 8, HALF), BF16),
    pltpu.VMEM((8, HALF), BF16),
    pltpu.VMEM((3, 8, HALF), BF16),
    pltpu.VMEM((4, 8, HALF), BF16),
    pltpu.VMEM((4, 8, HALF), BF16),
]


def pick(ref, dims, axis, index):
    where = dims.index(axis)
    if where == 0:
        return ref.at[index]
    if where == 1:
        return ref.at[:, index]
    return ref.at[:, :, index]


class Scatter:
    def __init__(self, net, src, got_core, s1, got1, s2, got2, s3, got3, tail, got_tail):
        self.net, self.src, self.got_core = net, src, got_core
        self.s = [s1, s2, s3]
        self.got = [got1, got2, got3]
        self.tail, self.got_tail = tail, got_tail

    def start(self, part):
        me = self.net.me
        core = coord(me, "core")
        return self.net.send(self.src.at[1 - core, part], self.got_core.at[part], me + 1 - 2 * core)

    def dims(self, part, level):
        gone = ORDERS[part][:level]
        return [a for a in ("x", "y", "z") if a not in gone]

    def add_core(self, part, copy):
        core = coord(self.net.me, "core")
        copy.wait_recv()

        def body(i, carry):
            x, y = i // 4, lax.rem(i, 4)
            mine = self.src[core, part, x, y].astype(F32)
            theirs = self.got_core[part, x, y].astype(F32)
            self.s[0][part, x, y] = (mine + theirs).astype(BF16)
            return carry

        lax.fori_loop(0, 16, body, 0, unroll=2)

    def send_level(self, part, level):
        me = self.net.me
        axis = ORDERS[part][level]
        dims = self.dims(part, level)
        return [
            self.net.send(
                pick(self.s[level].at[part], dims, axis, other),
                self.got[level].at[part, i],
                device,
            )
            for i, (other, device) in enumerate(peers(me, axis))
        ]

    def add_level(self, part, level, copies):
        me = self.net.me
        axis = ORDERS[part][level]
        dims = self.dims(part, level)
        own = pick(self.s[level].at[part], dims, axis, coord(me, axis))
        for copy in copies:
            copy.wait_recv()
        got = self.got[level].at[part]
        if level == 2:
            total = own[...].astype(F32)
            for i in range(3):
                total = total + got[i].astype(F32)
            return total
        for a in range(4):
            total = own[a].astype(F32)
            for i in range(3):
                total = total + got[i, a].astype(F32)
            self.s[level + 1][part, a] = total.astype(BF16)

    def exchange(self, totals):
        core = coord(self.net.me, "core")
        self.mine = []
        for part in range(3):
            for half in range(2):
                low = totals[part][half * 24 : half * 24 + 12]
                high = totals[part][half * 24 + 12 : half * 24 + 24]
                self.mine.append(jnp.where(core == 0, low, high))
                self.tail[part * 2 + half] = jnp.where(core == 0, high, low)
        self.copy = self.net.send(self.tail, self.got_tail, self.net.me + 1 - 2 * core)

    def finish(self, out):
        core = coord(self.net.me, "core")
        self.copy.wait_recv()
        for piece in range(6):
            mine = self.mine[piece]
            theirs = self.got_tail[piece]
            out[:, piece * 128 : piece * 128 + 128] = jnp.where(core == 0, mine, theirs)
            out[:, HALF + piece * 128 : HALF + piece * 128 + 128] = jnp.where(core == 0, theirs, mine)


RS_SCRATCH = [
    pltpu.VMEM((3, 4, 4, 4, 48, 128), BF16),
    pltpu.VMEM((3, 4, 4, 4, 48, 128), BF16),
    pltpu.VMEM((3, 3, 4, 4, 48, 128), BF16),
    pltpu.VMEM((3, 4, 4, 48, 128), BF16),
    pltpu.VMEM((3, 3, 4, 48, 128), BF16),
    pltpu.VMEM((3, 4, 48, 128), BF16),
    pltpu.VMEM((3, 3, 48, 128), BF16),
    pltpu.VMEM((6, 12, 128), F32),
    pltpu.VMEM((6, 12, 128), F32),
]


class Reduce:
    def __init__(self, net, merge, cur, got):
        self.net, self.merge, self.cur, self.got = net, merge, cur, got
        self.rows, self.level, self.slot = float(UTT * FRAMES_DEV), 0, 0

    def start(self, value):
        self.value = value
        self.cur[self.level] = value
        self.copies = []
        for _, device in peers(self.net.me, AXES[self.level]):
            self.copies.append(
                (self.net.send(self.cur.at[self.level], self.got.at[self.slot], device), self.slot)
            )
            self.slot += 1

    def take(self):
        parts = [self.value]
        for copy, index in self.copies:
            copy.wait_recv()
            parts.append(self.got[index])
        if self.merge:
            value = merge_stats(parts, self.rows)
        else:
            value = functools.reduce(jnp.add, parts)
        self.rows *= SIZE[AXES[self.level]]
        self.level += 1
        return value

    def step(self):
        self.start(self.take())


ROWS = UTT * FRAMES_DEV
CHUNK = 256
CHUNKS = D // CHUNK
HALO = 16
OWN = HALO * 8


def dot(a, b):
    return jnp.dot(a, b, preferred_element_type=F32)


def dot_t(a, b):
    return lax.dot_general(a, b, (((1,), (1,)), ((), ())), preferred_element_type=F32)


def span(index, size):
    return pl.ds(pl.multiple_of(index * size, size), size)


def frame_of(row):
    return (row & 7) * 32 + (row >> 3)


def fold(x):
    return jnp.sum(x.reshape(x.shape[0] // 8, 8, x.shape[1]), axis=0)


class Halo:
    def __init__(self, me, devices, out, got, send_sem, recv_sem):
        self.out, self.got, self.send_sem, self.recv_sem = out, got, send_sem, recv_sem
        self.right = lax.rem(me + 1, devices)
        self.left = lax.rem(me + devices - 1, devices)

    def copies(self, c):
        return [
            pltpu.make_async_remote_copy(
                src_ref=self.out.at[c, way],
                dst_ref=self.got.at[c, way],
                send_sem=self.send_sem.at[c, way],
                recv_sem=self.recv_sem.at[c, way],
                device_id=(device,),
                device_id_type=pl.DeviceIdType.MESH,
            )
            for way, device in enumerate((self.right, self.left))
        ]

    def push(self, c, select, blocks):
        for u in range(UTT):
            edge = dot(select[...], blocks[u]).astype(BF16)
            self.out[c, 0, u] = edge[0:HALO]
            self.out[c, 1, u] = edge[HALO : 2 * HALO]
        for copy in self.copies(c):
            copy.start()

    def wait(self, c):
        for copy in self.copies(c):
            copy.wait_recv()

    def drain(self):
        for c in range(CHUNKS):
            for copy in self.copies(c):
                copy.wait_send()


def extend(ext, u, cols, low, high, row_id):
    for j in range(HALO):
        below = pltpu.roll(ext[u, OWN + (16 + j) * 8 : OWN + (17 + j) * 8, cols], 1, 0)
        ext[u, j * 8 : j * 8 + 8, cols] = jnp.where(row_id == 0, low[j : j + 1], below)
        above = pltpu.roll(ext[u, OWN + j * 8 : OWN + j * 8 + 8, cols], 7, 0)
        ext[u, (48 + j) * 8 : (49 + j) * 8, cols] = jnp.where(row_id == 7, high[j : j + 1], above)


def convolve(ext, u, cols, taps, offset):
    low, high = taps[0::2], taps[1::2]
    both = [a + b for a, b in zip(low, high)]

    def x(n):
        return ext[u, (n + offset) * 8 : (n + offset) * 8 + 8, cols]

    def product(weights, source, start, first):
        acc = list(start)
        for n in range(first, first + 23):
            value = source(n)
            for p in range(8):
                m = n - first - p
                if 0 <= m < 16:
                    term = weights[m] * value
                    acc[p] = term if acc[p] is None else acc[p] + term
        return acc

    for first in (0, 8):
        shared = product(both, lambda n: x(2 * n + 1), [None] * 8, first)
        even = product(low, lambda n: x(2 * n) - x(2 * n + 1), shared, first)
        odd = product(high, lambda n: x(2 * n + 2) - x(2 * n + 1), shared, first)
        yield 2 * first, [v for pair in zip(even, odd) for v in pair]


def whole_kernel(n_dev, x_hbm, lng_ref, win_hbm, ker_ref, bng_ref, bnb_ref, wout_hbm, cot_hbm,
                 out_hbm, din_hbm, dw_ref, dk_ref, dbn_ref, *scratch):
    s = dict(zip([name for name, _ in SCRATCH], scratch))
    me = lax.axis_index("seq")
    local = s["local_sem"]
    load_x = [pltpu.make_async_copy(x_hbm.at[u], s["x_raw"].at[u], local.at[u]) for u in range(UTT)]
    load_cot = pltpu.make_async_copy(cot_hbm, s["cot_raw"], local.at[2])
    load_out = pltpu.make_async_copy(wout_hbm, s["w_out"], local.at[3])

    def load_in(c):
        found = []
        for side in range(2):
            cols = pl.ds(pl.multiple_of(side * D + c * CHUNK, CHUNK), CHUNK)
            found.append(
                pltpu.make_async_copy(win_hbm.at[:, cols], s["w_in"].at[:, cols], s["win_sem"].at[c, side])
            )
        return found

    for copy in load_x:
        copy.start()
    vec = s["vec"]
    for row, ref in enumerate((lng_ref, bng_ref, bnb_ref)):
        vec[row : row + 1, :] = ref[...].reshape(1, D)
    net = Net(me, s["send_sem"], s["recv_sem"])
    halo1 = Halo(me, n_dev, s["h_out1"], s["h_got1"], s["h_send1"], s["h_recv1"])
    halo2 = Halo(me, n_dev, s["h_out2"], s["h_got2"], s["h_send2"], s["h_recv2"])

    entered = greet(me, AXES, (halo1.left, halo1.right))
    perm, eye, select = s["perm"], s["eye"], s["select"]
    r0 = lax.broadcasted_iota(jnp.int32, (256, 256), 0)
    r1 = lax.broadcasted_iota(jnp.int32, (256, 256), 1)
    perm[...] = jnp.where(frame_of(r0) == r1, 1.0, 0.0).astype(BF16)
    eye[...] = jnp.where(r0 == r1, 1.0, 0.0).astype(BF16)
    q0 = lax.broadcasted_iota(jnp.int32, (32, 256), 0)
    q1 = lax.broadcasted_iota(jnp.int32, (32, 256), 1)
    edge_frame = jnp.where(q0 < HALO, FRAMES_DEV - HALO + q0, q0 - HALO)
    select[...] = jnp.where(frame_of(q1) == edge_frame, 1.0, 0.0).astype(BF16)
    row_id = lax.broadcasted_iota(jnp.int32, (8, 128), 0)

    x_p, normed, mu_ref, rstd_ref = s["x_p"], s["bf"], s["mu"], s["rstd"]
    for copy in load_x:
        copy.wait()
    for c in range(CHUNKS):
        for copy in load_in(c):
            copy.start()

    def permute(c, carry):
        cols = span(c, CHUNK)
        for u in range(UTT):
            x_p[u * 256 : u * 256 + 256, cols] = dot(perm[...], s["x_raw"][u, :, cols]).astype(BF16)
        return carry

    lax.fori_loop(0, CHUNKS, permute, 0, unroll=2)

    def norm_tile(i, carry):
        rows = span(i, 16)
        x = x_p[rows, :].astype(F32)
        mean = jnp.mean(x, axis=-1, keepdims=True)
        gap = x - mean
        rstd = lax.rsqrt(jnp.mean(gap * gap, axis=-1, keepdims=True) + EPSILON)
        mu_ref[rows, :] = mean
        rstd_ref[rows, :] = rstd
        normed[rows, :] = (gap * rstd * vec[0:1, :]).astype(BF16)
        return carry

    lax.fori_loop(0, ROWS // 16, norm_tile, 0, unroll=4)
    entered()
    w_in, val, gs, ext_g, ext_d = s["w_in"], s["val"], s["gs"], s["ext_g"], s["ext_d"]

    def project(c, carry):
        for copy in load_in(c):
            copy.wait()
        project_chunk(c)
        return carry

    def project_chunk(c):
        cols = span(c, CHUNK)
        val[:, cols] = dot(normed[...], w_in[:, cols])
        gate_cols = pl.ds(pl.multiple_of(D + c * CHUNK, CHUNK), CHUNK)
        gs[:, cols] = dot(normed[...], w_in[:, gate_cols])
        blocks = []
        for u in range(UTT):
            rows = pl.ds(u * 256, 256)
            sig = jax.nn.sigmoid(gs[rows, cols])
            gs[rows, cols] = sig
            gated = (val[rows, cols] * sig).astype(BF16)
            ext_g[u, OWN : OWN + 256, cols] = gated.astype(F32)
            blocks.append(gated)
        halo1.push(c, select, blocks)

    lax.fori_loop(0, CHUNKS, project, 0)
    load_cot.start()
    load_out.start()

    def halo_rows(halo, c, u, lane):
        low = halo.got[c, 0, u, :, lane : lane + 128].astype(F32)
        high = halo.got[c, 1, u, :, lane : lane + 128].astype(F32)
        return jnp.where(me == 0, 0.0, low), jnp.where(me == n_dev - 1, 0.0, high)

    conv, stat = s["conv"], s["stat"]

    def taps_of(cols):
        return [jnp.broadcast_to(ker_ref[k : k + 1, cols], (8, 128)) for k in range(K)]

    def conv_only(c, carry):
        halo1.wait(c)
        conv_chunk(c)
        return carry

    def conv_chunk(c):
        for half in range(2):
            cols = pl.ds(pl.multiple_of(c * CHUNK + half * 128, 128), 128)
            taps = taps_of(cols)
            total = jnp.zeros((8, 128), F32)
            for u in range(UTT):
                low, high = halo_rows(halo1, c, u, half * 128)
                extend(ext_g, u, cols, low, high, row_id)
                for base, acc in convolve(ext_g, u, cols, taps, 1):
                    for o in range(16):
                        conv[pl.ds(u * 256 + (base + o) * 8, 8), cols] = acc[o]
                        total = total + acc[o]
            mean = jnp.sum(total, axis=0, keepdims=True) * (1.0 / ROWS)
            gap = conv[:, cols] - mean
            stat[0:1, cols] = mean
            stat[1:2, cols] = jnp.sum(fold(gap * gap), axis=0, keepdims=True)

    wide = (slice(0, HALF), slice(HALF, D))
    ar1 = [Reduce(net, True, s["cur"].at[h], s["got"].at[h]) for h in range(2)]
    ar2 = [Reduce(net, False, s["cur"].at[2 + h], s["got"].at[2 + h]) for h in range(2)]
    lax.fori_loop(0, 3, conv_only, 0)
    ar1[0].start(stat[:, wide[0]])
    lax.fori_loop(3, 4, conv_only, 0)
    ar1[0].step()
    lax.fori_loop(4, CHUNKS, conv_only, 0)
    ar1[0].step()
    ar1[1].start(stat[:, wide[1]])
    load_cot.wait()
    cot_p, cot_t, w_out = s["cot_p"], s["cot_t"], s["w_out"]

    def turn(c, carry):
        cols = span(c, CHUNK)
        for u in range(UTT):
            cot_p[u * 256 : u * 256 + 256, cols] = dot(perm[...], s["cot_raw"][u, :, cols]).astype(BF16)
        cot_t[cols, :] = dot_t(eye[...], cot_p[:, cols]).astype(BF16)
        return carry

    lax.fori_loop(0, CHUNKS, turn, 0, unroll=2)
    ar1[1].step()
    ar1[0].step()
    load_out.wait()

    def act_grad(c, carry):
        cols = span(c, CHUNK)
        res = dot(cot_p[...], w_out[:, cols])
        for u in range(UTT):
            ext_d[u, OWN : OWN + 256, cols] = res[u * 256 : u * 256 + 256]
        return carry

    total_rows = float(ROWS * n_dev)
    coef = s["coef"]

    def use_stats(h):
        stats = ar1[h].take()
        coef[0:1, wide[h]] = stats[0:1]
        coef[1:2, wide[h]] = lax.rsqrt(stats[1:2] * (1.0 / total_rows) + EPSILON)

    lax.fori_loop(0, CHUNKS // 2, act_grad, 0)
    ar1[1].step()
    lax.fori_loop(CHUNKS // 2, CHUNKS, act_grad, 0)
    use_stats(0)
    act = s["bf"]

    def bn_block(cb, carry):
        cols = span(cb, 128)
        mean, rstd = coef[0:1, cols], coef[1:2, cols]
        gain, bias = vec[1:2, cols], vec[2:3, cols]
        sum_bias = jnp.zeros((8, 128), F32)
        sum_gain = jnp.zeros((8, 128), F32)
        for u in range(UTT):
            rows = pl.ds(u * 256, 256)
            xhat = (conv[rows, cols] - mean) * rstd
            bn = xhat * gain + bias
            sig = jax.nn.sigmoid(bn)
            conv[rows, cols] = xhat
            act[rows, cols] = (bn * sig).astype(BF16)
            d_bn = ext_d[u, OWN : OWN + 256, cols] * (sig + bn * sig * (1.0 - sig))
            ext_d[u, OWN : OWN + 256, cols] = d_bn
            sum_bias = sum_bias + fold(d_bn)
            sum_gain = sum_gain + fold(d_bn * xhat)
        stat[0:1, cols] = jnp.sum(sum_gain, axis=0, keepdims=True)
        stat[1:2, cols] = jnp.sum(sum_bias, axis=0, keepdims=True)
        return carry

    core = coord(me, "core")
    part_ref = s["part"]
    rs = Scatter(net, part_ref, *[s[name] for name in RS_NAMES])

    def weight_part(h, p):
        cols = pl.ds(pl.multiple_of(h * HALF + p * CHUNK, CHUNK), CHUNK)

        def weight_tile(m, carry):
            res = dot(cot_t[span(m, 384), :], act[:, cols])
            for j in range(16):
                piece = res[j * 24 : j * 24 + 24]
                piece = jnp.concatenate([piece[:, 0:128], piece[:, 128:256]], axis=0).astype(BF16)
                part_ref[h, p, m, j // 4, j % 4] = piece
            return carry

        lax.fori_loop(0, 4, weight_tile, 0, unroll=2)

    saves = []

    def branch(n, carry):
        cols = span(n, CHUNK)
        res = dot_t(act[...], w_out[cols, :])
        s["out_p"][:, cols] = (x_p[:, cols].astype(F32) + res).astype(BF16)
        return carry

    def use_sums(h):
        sums = ar2[h].take()
        s["dbn_s"][:, wide[h]] = sums
        gain_row = vec[1:2, wide[h]]
        rstd_row = coef[1:2, wide[h]]
        coef[2:3, wide[h]] = rstd_row * gain_row
        coef[3:4, wide[h]] = rstd_row * (gain_row * sums[1:2] * (1.0 / total_rows))
        coef[4:5, wide[h]] = rstd_row * (gain_row * sums[0:1] * (1.0 / total_rows))

    lax.fori_loop(0, 6, bn_block, 0)
    ar1[1].step()
    ar2[0].start(stat[:, wide[0]])
    weight_part(0, 0)
    weight_part(0, 1)
    weight_part(0, 2)
    ar2[0].step()
    use_stats(1)
    lax.fori_loop(6, 12, bn_block, 0)
    ar2[0].step()
    ar2[1].start(stat[:, wide[1]])
    weight_part(1, 0)
    weight_part(1, 1)
    weight_part(1, 2)
    ar2[1].step()
    firsts = {p: rs.start(p) for p in (2, 1, 0)}
    lax.fori_loop(0, CHUNKS // 2, branch, 0)
    ar2[0].step()
    ar2[1].step()
    lax.fori_loop(CHUNKS // 2, CHUNKS, branch, 0)
    copy = pltpu.make_async_copy(s["out_p"], out_hbm, local.at[4])
    copy.start()
    saves.append(copy)
    use_sums(0)

    def conv_grad(c, carry):
        cols = span(c, CHUNK)
        blocks = []
        for u in range(UTT):
            d_bn = ext_d[u, OWN : OWN + 256, cols]
            xhat = conv[u * 256 : u * 256 + 256, cols]
            d_conv = d_bn * coef[2:3, cols] - coef[3:4, cols] - xhat * coef[4:5, cols]
            ext_d[u, OWN : OWN + 256, cols] = d_conv
            blocks.append(d_conv.astype(BF16))
        halo2.push(c, select, blocks)
        return carry

    dk_src = s["dk_src"]

    def kernel_grad(h):
        def tap_sums(n, carry):
            cols = pl.ds(pl.multiple_of(h * HALF + n * 128, 128), 128)
            for u in range(UTT):
                grads = [ext_d[u, OWN + i * 8 : OWN + i * 8 + 8, cols] for i in range(32)]
                for base, acc in convolve(ext_g, u, cols, grads, 1):
                    for part in range(2):
                        row = base // 8 + part
                        folded = jnp.concatenate(
                            [jnp.sum(a, axis=0, keepdims=True) for a in acc[part * 8 : part * 8 + 8]],
                            axis=0,
                        )
                        if u == 0:
                            dk_src[h, row, :, span(n, 128)] = folded
                        else:
                            dk_src[h, row, :, span(n, 128)] += folded
            return carry

        lax.fori_loop(0, HALF // 128, tap_sums, 0)

    lax.fori_loop(0, 3, conv_grad, 0)
    ar2[1].step()
    levels = {}
    for p in (2, 1, 0):
        rs.add_core(p, firsts[p])
        levels[p] = rs.send_level(p, 0)
    kernel_grad(0)
    use_sums(1)
    lax.fori_loop(3, CHUNKS, conv_grad, 0)

    dk = DKernel(net, dk_src, *[s[name] for name in DK_NAMES])
    kernel_grad(1)
    dk.start()
    grads = (s["d_proj0"], s["d_proj1"])

    def input_grad(c, d_proj):
        halo2.wait(c)
        for half in range(2):
            start = pl.multiple_of(c * CHUNK + half * 128, 128)
            cols = pl.ds(start, 128)
            taps = taps_of(cols)[::-1]
            lane = half * 128
            for u in range(UTT):
                low, high = halo_rows(halo2, c, u, lane)
                extend(ext_d, u, cols, low, high, row_id)
                for base, acc in convolve(ext_d, u, cols, taps, 0):
                    rows = pl.ds(u * 256 + base * 8, 128)
                    grad = jnp.concatenate(acc, axis=0)
                    sig = gs[rows, cols]
                    by_sig = grad * sig
                    d_proj[rows, lane : lane + 128] = by_sig.astype(BF16)
                    d_proj[rows, CHUNK + lane : CHUNK + lane + 128] = (
                        by_sig * val[rows, cols] * (1.0 - sig)
                    ).astype(BF16)

    def frame_grad(c, d_proj):
        cols = span(c, CHUNK)
        gate_cols = pl.ds(pl.multiple_of(D + c * CHUNK, CHUNK), CHUNK)
        for n in range(CHUNKS):
            rows = slice(n * CHUNK, n * CHUNK + CHUNK)
            weights = jnp.concatenate([w_in[rows, cols], w_in[rows, gate_cols]], axis=1)
            if c == 0:
                conv[:, rows] = dot_t(d_proj[...], weights)
            else:
                conv[:, rows] += dot_t(d_proj[...], weights)

    def pair(c):
        input_grad(c + 1, grads[1 - c % 2])
        frame_grad(c, grads[c % 2])

    def next_level(level):
        found = {}
        for p in (2, 1, 0):
            rs.add_level(p, level, levels[p])
            found[p] = rs.send_level(p, level + 1)
        return found

    input_grad(0, grads[0])
    dk.to_x()
    pair(0)
    dk.to_z()
    pair(1)
    levels = next_level(0)
    dk.to_y()
    pair(2)
    dk.gather_x()
    pair(3)
    dk.gather_core()
    levels = next_level(1)
    input_grad(5, grads[1])
    halo1.drain()
    halo2.drain()
    frame_grad(4, grads[0])
    frame_grad(5, grads[1])
    rs.exchange([rs.add_level(p, 2, levels[p]) for p in range(3)])

    def leave(src, dst, sem):
        copy = pltpu.make_async_copy(src, dst, local.at[sem])
        copy.start()
        saves.append(copy)

    leave(s["dbn_s"], dbn_ref, 10)

    def norm_grad(u):
        def tile(i, carry):
            rows = pl.ds(pl.multiple_of(u * 128 + i * 16, 16), 16)
            d_hat = conv[rows, :] * vec[0:1, :]
            rstd = rstd_ref[rows, :]
            hat = (x_p[rows, :].astype(F32) - mu_ref[rows, :]) * rstd
            m1 = jnp.mean(d_hat, axis=-1, keepdims=True)
            m2 = jnp.mean(d_hat * hat, axis=-1, keepdims=True)
            grad = rstd * (d_hat - m1 - hat * m2)
            act[rows, :] = (cot_p[rows, :].astype(F32) + grad).astype(BF16)
            return carry

        lax.fori_loop(0, 8, tile, 0, unroll=4)
        rows_u = pl.ds(u * 128, 128)
        copy = pltpu.make_async_copy(act.at[rows_u], din_hbm.at[rows_u], local.at[6 + u])
        copy.start()
        saves.append(copy)

    norm_grad(0)
    norm_grad(1)
    dk.finish(s["dk_s"])
    leave(s["dk_s"], dk_ref, 11)
    norm_grad(2)
    rs.finish(s["dw_s"])
    leave(s["dw_s"], dw_ref, 5)
    norm_grad(3)
    net.drain()
    for copy in saves:
        copy.wait()


RS_NAMES = ["got_core", "s1", "got1", "s2", "got2", "s3", "got3", "tail", "got_tail"]
DK_NAMES = ["dk%d" % i for i in range(len(DK_SCRATCH))]
VM = pltpu.VMEM
SCRATCH = [
    ("x_raw", VM((UTT, 256, D), BF16)),
    ("w_in", VM((D, 2 * D), BF16)),
    ("cot_raw", VM((UTT, 256, D), BF16)),
    ("w_out", VM((D, D), BF16)),
    ("perm", VM((256, 256), BF16)),
    ("win_sem", pltpu.SemaphoreType.DMA((CHUNKS, 2))),
    ("vec", VM((3, D), F32)),
    ("out_p", VM((ROWS, D), BF16)),
    ("eye", VM((256, 256), BF16)),
    ("select", VM((32, 256), BF16)),
    ("x_p", VM((ROWS, D), BF16)),
    ("bf", VM((ROWS, D), BF16)),
    ("mu", VM((ROWS, 1), F32)),
    ("rstd", VM((ROWS, 1), F32)),
    ("val", VM((ROWS, D), F32)),
    ("gs", VM((ROWS, D), F32)),
    ("ext_g", VM((UTT, 512, D), F32)),
    ("ext_d", VM((UTT, 512, D), F32)),
    ("conv", VM((ROWS, D), F32)),
    ("dbn_s", VM((2, D), F32)),
    ("dk_s", VM((K, D), F32)),
    ("dw_s", VM((D // 128, D), F32)),
    ("stat", VM((2, D), F32)),
    ("coef", VM((8, D), F32)),
    ("cot_p", VM((ROWS, D), BF16)),
    ("cot_t", VM((D, ROWS), BF16)),
    ("d_proj0", VM((ROWS, 2 * CHUNK), BF16)),
    ("d_proj1", VM((ROWS, 2 * CHUNK), BF16)),
    ("part", VM((2, 3, 4, 4, 4, 48, 128), BF16)),
    ("h_out1", VM((CHUNKS, 2, UTT, HALO, CHUNK), BF16)),
    ("h_got1", VM((CHUNKS, 2, UTT, HALO, CHUNK), BF16)),
    ("h_out2", VM((CHUNKS, 2, UTT, HALO, CHUNK), BF16)),
    ("h_got2", VM((CHUNKS, 2, UTT, HALO, CHUNK), BF16)),
    ("cur", VM((4, 4, 2, HALF), F32)),
    ("got", VM((4, 10, 2, HALF), F32)),
    ("dk_src", VM((2, 4, 8, HALF), F32)),
]
SCRATCH += list(zip(RS_NAMES, RS_SCRATCH)) + list(zip(DK_NAMES, DK_SCRATCH))
SCRATCH += [
    ("local_sem", pltpu.SemaphoreType.DMA((12,))),
    ("send_sem", pltpu.SemaphoreType.DMA((88,))),
    ("recv_sem", pltpu.SemaphoreType.DMA((88,))),
    ("h_send1", pltpu.SemaphoreType.DMA((CHUNKS, 2))),
    ("h_recv1", pltpu.SemaphoreType.DMA((CHUNKS, 2))),
    ("h_send2", pltpu.SemaphoreType.DMA((CHUNKS, 2))),
    ("h_recv2", pltpu.SemaphoreType.DMA((CHUNKS, 2))),
]


def finish_kernel(out_p, din_p, dw, dk, dbn, out_ref, din_ref, dw_out, dk_out, gain_out, bias_out, perm_t):
    @pl.when((pl.program_id(0) == 0) & (pl.program_id(1) == 0))
    def _():
        r0 = lax.broadcasted_iota(jnp.int32, (256, 256), 0)
        r1 = lax.broadcasted_iota(jnp.int32, (256, 256), 1)
        perm_t[...] = jnp.where(frame_of(r1) == r0, 1.0, 0.0).astype(BF16)
        dw_out[...] = dw[...]
        dk_out[...] = dk[...]
        gain_out[...] = dbn[0:1, :].reshape(D)
        bias_out[...] = dbn[1:2, :].reshape(D)

    out_ref[0] = dot(perm_t[...], out_p[...]).astype(BF16)
    din_ref[0] = dot(perm_t[...], din_p[...]).astype(BF16)


def on_device(inputs, ln_gain, w_in, kernel, bn_gain, bn_bias, w_out, cotangent):
    any_spec = pl.BlockSpec(memory_space=pl.ANY)
    vmem_spec = pl.BlockSpec(memory_space=pltpu.VMEM)
    flat = jax.ShapeDtypeStruct((ROWS, D), BF16)
    out_p, din_p, dw, dk, dbn = pl.pallas_call(
        functools.partial(whole_kernel, lax.axis_size("seq")),
        out_shape=(
            flat,
            flat,
            jax.ShapeDtypeStruct((D // 128, D), F32),
            jax.ShapeDtypeStruct((K, D), F32),
            jax.ShapeDtypeStruct((2, D), F32),
        ),
        in_specs=[any_spec, vmem_spec, any_spec, vmem_spec, vmem_spec, vmem_spec, any_spec, any_spec],
        out_specs=[any_spec] * 5,
        scratch_shapes=[spec for _, spec in SCRATCH],
        compiler_params=pltpu.CompilerParams(
            collective_id=0, has_side_effects=True, vmem_limit_bytes=67043328
        ),
    )(inputs, ln_gain, w_in, kernel, bn_gain, bn_bias, w_out, cotangent)

    def whole(shape):
        return pl.BlockSpec(shape, lambda u, c: (0,) * len(shape))

    wide = D // 2
    rows_spec = pl.BlockSpec((256, wide), lambda u, c: (u, c))
    block_spec = pl.BlockSpec((1, 256, wide), lambda u, c: (u, 0, c))
    full = jax.ShapeDtypeStruct((UTT, FRAMES_DEV, D), BF16)
    return pl.pallas_call(
        finish_kernel,
        grid=(UTT, 2),
        out_shape=(
            full,
            full,
            jax.ShapeDtypeStruct((D // 128, D), F32),
            jax.ShapeDtypeStruct((K, D), F32),
            jax.ShapeDtypeStruct((D,), F32),
            jax.ShapeDtypeStruct((D,), F32),
        ),
        in_specs=[rows_spec, rows_spec, whole((D // 128, D)), whole((K, D)), whole((2, D))],
        out_specs=[block_spec, block_spec, whole((D // 128, D)), whole((K, D)), whole((D,)), whole((D,))],
        scratch_shapes=[pltpu.VMEM((256, 256), BF16)],
    )(out_p, din_p, dw, dk, dbn)


def solution(mesh):
    return jax.shard_map(
        on_device,
        mesh=mesh,
        in_specs=(P(None, "seq", None), P(), P(), P(), P(), P(), P(), P(None, "seq", None)),
        out_specs=(P(None, "seq", None), P(None, "seq", None), P("seq", None), P(), P(), P()),
        check_vma=False,
    )
```

```python
import functools
import jax
import jax.numpy as jnp
from jax import lax
from jax.experimental import pallas as pl
from jax.experimental.pallas import tpu as pltpu
from jax.sharding import PartitionSpec as P

D = 1536
K = 32
FRAMES_DEV = 256
UTT = 2
EPSILON = 1e-05
F32 = jnp.float32
BF16 = jnp.bfloat16
STRIDE = {"core": 1, "z": 2, "y": 8, "x": 32}
SIZE = {"core": 2, "z": 4, "y": 4, "x": 4}
ORDERS = (("x", "y", "z"), ("y", "z", "x"), ("z", "x", "y"))
HALF = D // 2


def coord(me, axis):
    return lax.rem(me // STRIDE[axis], SIZE[axis])


def peers(me, axis):
    q = coord(me, axis)
    found = []
    for delta in range(1, SIZE[axis]):
        other = lax.rem(q + delta, SIZE[axis])
        found.append((other, me + (other - q) * STRIDE[axis]))
    return found


class Net:
    def __init__(self, me, send_sem, recv_sem):
        self.me, self.send_sem, self.recv_sem, self.used = me, send_sem, recv_sem, 0
        self.started = []

    def send(self, src, dst, device):
        slot = self.used
        self.used += 1
        copy = pltpu.make_async_remote_copy(
            src_ref=src,
            dst_ref=dst,
            send_sem=self.send_sem.at[slot],
            recv_sem=self.recv_sem.at[slot],
            device_id=(device,),
            device_id_type=pl.DeviceIdType.MESH,
        )
        copy.start()
        self.started.append(copy)
        return copy

    def drain(self):
        for copy in self.started:
            copy.wait_send()


def greet(me, axes, extra=()):
    barrier = pltpu.get_barrier_semaphore()
    count = 0
    for axis in axes:
        for _, device in peers(me, axis):
            pl.semaphore_signal(
                barrier, inc=1, device_id=(device,), device_id_type=pl.DeviceIdType.MESH
            )
            count += 1
    for device in extra:
        pl.semaphore_signal(
            barrier, inc=1, device_id=(device,), device_id_type=pl.DeviceIdType.MESH
        )
        count += 1
    return lambda: pl.semaphore_wait(barrier, count)


AXES = ("core", "z", "y", "x")


def merge_stats(parts, rows):
    mean = functools.reduce(jnp.add, [p[0:1] for p in parts]) * (1.0 / len(parts))
    spread = functools.reduce(jnp.add, [p[1:2] for p in parts])
    for p in parts:
        gap = p[0:1] - mean
        spread = spread + rows * gap * gap
    return jnp.concatenate([mean, spread], axis=0)


class DKernel:
    def __init__(self, net, src, core_buf, got_core, got_x, cz, got_z, cy, got_y, full, other):
        self.net = net
        self.src, self.core_buf, self.got_core = src, core_buf, got_core
        self.got_x, self.cz, self.got_z = got_x, cz, got_z
        self.cy, self.got_y, self.full, self.other = cy, got_y, full, other

    def start(self):
        me = self.net.me
        core = coord(me, "core")
        self.c0 = [self.net.send(self.src.at[1 - core], self.got_core, me + 1 - 2 * core)]

    def to_x(self):
        me = self.net.me
        core = coord(me, "core")
        x = coord(me, "x")
        self.c0[0].wait_recv()
        self.core_buf[...] = (self.src[core] + self.got_core[...]).astype(BF16)
        self.cx_c = [
            self.net.send(self.core_buf.at[other], self.got_x.at[i], device)
            for i, (other, device) in enumerate(peers(me, "x"))
        ]

    def to_z(self):
        me = self.net.me
        total = self.core_buf[coord(me, "x")].astype(F32)
        for i, copy in enumerate(self.cx_c):
            copy.wait_recv()
            total = total + self.got_x[i].astype(F32)
        self.cz[...] = total.astype(BF16)
        self.cz_c = [
            self.net.send(self.cz, self.got_z.at[i], device)
            for i, (_, device) in enumerate(peers(me, "z"))
        ]

    def to_y(self):
        me = self.net.me
        total = self.cz[...].astype(F32)
        for i, copy in enumerate(self.cz_c):
            copy.wait_recv()
            total = total + self.got_z[i].astype(F32)
        self.cy[...] = total.astype(BF16)
        self.cy_c = [
            self.net.send(self.cy, self.got_y.at[i], device)
            for i, (_, device) in enumerate(peers(me, "y"))
        ]

    def gather_x(self):
        me = self.net.me
        total = self.cy[...].astype(F32)
        for i, copy in enumerate(self.cy_c):
            copy.wait_recv()
            total = total + self.got_y[i].astype(F32)
        x = coord(me, "x")
        self.full[x] = total.astype(BF16)
        self.gx_c = [
            self.net.send(self.full.at[x], self.full.at[x], device)
            for _, device in peers(me, "x")
        ]

    def gather_core(self):
        me = self.net.me
        core = coord(me, "core")
        for copy in self.gx_c:
            copy.wait_recv()
        self.gc_c = self.net.send(self.full, self.other, me + 1 - 2 * core)

    def finish(self, out):
        core = coord(self.net.me, "core")
        self.gc_c.wait_recv()
        for i in range(4):
            mine = self.full[i].astype(F32)
            theirs = self.other[i].astype(F32)
            out[pl.ds(8 * i, 8), 0:HALF] = jnp.where(core == 0, mine, theirs)
            out[pl.ds(8 * i, 8), HALF:D] = jnp.where(core == 0, theirs, mine)


DK_SCRATCH = [
    pltpu.VMEM((4, 8, HALF), BF16),
    pltpu.VMEM((4, 8, HALF), F32),
    pltpu.VMEM((3, 8, HALF), BF16),
    pltpu.VMEM((8, HALF), BF16),
    pltpu.VMEM((3, 8, HALF), BF16),
    pltpu.VMEM((8, HALF), BF16),
    pltpu.VMEM((3, 8, HALF), BF16),
    pltpu.VMEM((4, 8, HALF), BF16),
    pltpu.VMEM((4, 8, HALF), BF16),
]


def pick(ref, dims, axis, index):
    where = dims.index(axis)
    if where == 0:
        return ref.at[index]
    if where == 1:
        return ref.at[:, index]
    return ref.at[:, :, index]


class Scatter:
    def __init__(self, net, src, got_core, s1, got1, s2, got2, s3, got3, tail, got_tail):
        self.net, self.src, self.got_core = net, src, got_core
        self.s = [s1, s2, s3]
        self.got = [got1, got2, got3]
        self.tail, self.got_tail = tail, got_tail

    def start(self, part):
        me = self.net.me
        core = coord(me, "core")
        return self.net.send(self.src.at[1 - core, part], self.got_core.at[part], me + 1 - 2 * core)

    def dims(self, part, level):
        gone = ORDERS[part][:level]
        return [a for a in ("x", "y", "z") if a not in gone]

    def add_core(self, part, copy):
        core = coord(self.net.me, "core")
        copy.wait_recv()

        def body(i, carry):
            x, y = i // 4, lax.rem(i, 4)
            mine = self.src[core, part, x, y].astype(F32)
            theirs = self.got_core[part, x, y].astype(F32)
            self.s[0][part, x, y] = (mine + theirs).astype(BF16)
            return carry

        lax.fori_loop(0, 16, body, 0, unroll=2)

    def send_level(self, part, level):
        me = self.net.me
        axis = ORDERS[part][level]
        dims = self.dims(part, level)
        return [
            self.net.send(
                pick(self.s[level].at[part], dims, axis, other),
                self.got[level].at[part, i],
                device,
            )
            for i, (other, device) in enumerate(peers(me, axis))
        ]

    def add_level(self, part, level, copies):
        me = self.net.me
        axis = ORDERS[part][level]
        dims = self.dims(part, level)
        own = pick(self.s[level].at[part], dims, axis, coord(me, axis))
        for copy in copies:
            copy.wait_recv()
        got = self.got[level].at[part]
        if level == 2:
            total = own[...].astype(F32)
            for i in range(3):
                total = total + got[i].astype(F32)
            return total
        for a in range(4):
            total = own[a].astype(F32)
            for i in range(3):
                total = total + got[i, a].astype(F32)
            self.s[level + 1][part, a] = total.astype(BF16)

    def exchange(self, totals):
        core = coord(self.net.me, "core")
        self.mine = []
        for part in range(3):
            for half in range(2):
                low = totals[part][half * 24 : half * 24 + 12]
                high = totals[part][half * 24 + 12 : half * 24 + 24]
                self.mine.append(jnp.where(core == 0, low, high))
                self.tail[part * 2 + half] = jnp.where(core == 0, high, low)
        self.copy = self.net.send(self.tail, self.got_tail, self.net.me + 1 - 2 * core)

    def finish(self, out):
        core = coord(self.net.me, "core")
        self.copy.wait_recv()
        for piece in range(6):
            mine = self.mine[piece]
            theirs = self.got_tail[piece]
            out[:, piece * 128 : piece * 128 + 128] = jnp.where(core == 0, mine, theirs)
            out[:, HALF + piece * 128 : HALF + piece * 128 + 128] = jnp.where(core == 0, theirs, mine)


RS_SCRATCH = [
    pltpu.VMEM((3, 4, 4, 4, 48, 128), BF16),
    pltpu.VMEM((3, 4, 4, 4, 48, 128), BF16),
    pltpu.VMEM((3, 3, 4, 4, 48, 128), BF16),
    pltpu.VMEM((3, 4, 4, 48, 128), BF16),
    pltpu.VMEM((3, 3, 4, 48, 128), BF16),
    pltpu.VMEM((3, 4, 48, 128), BF16),
    pltpu.VMEM((3, 3, 48, 128), BF16),
    pltpu.VMEM((6, 12, 128), F32),
    pltpu.VMEM((6, 12, 128), F32),
]


class Reduce:
    def __init__(self, net, merge, cur, got):
        self.net, self.merge, self.cur, self.got = net, merge, cur, got
        self.rows, self.level, self.slot = float(UTT * FRAMES_DEV), 0, 0

    def start(self, value):
        self.value = value
        self.cur[self.level] = value
        self.copies = []
        for _, device in peers(self.net.me, AXES[self.level]):
            self.copies.append(
                (self.net.send(self.cur.at[self.level], self.got.at[self.slot], device), self.slot)
            )
            self.slot += 1

    def take(self):
        parts = [self.value]
        for copy, index in self.copies:
            copy.wait_recv()
            parts.append(self.got[index])
        if self.merge:
            value = merge_stats(parts, self.rows)
        else:
            value = functools.reduce(jnp.add, parts)
        self.rows *= SIZE[AXES[self.level]]
        self.level += 1
        return value

    def step(self):
        self.start(self.take())


ROWS = UTT * FRAMES_DEV
CHUNK = 256
CHUNKS = D // CHUNK
HALO = 16
OWN = HALO * 8


def dot(a, b):
    return jnp.dot(a, b, preferred_element_type=F32)


def dot_t(a, b):
    return lax.dot_general(a, b, (((1,), (1,)), ((), ())), preferred_element_type=F32)


def span(index, size):
    return pl.ds(pl.multiple_of(index * size, size), size)


def frame_of(row):
    return (row & 7) * 32 + (row >> 3)


def fold(x):
    return jnp.sum(x.reshape(x.shape[0] // 8, 8, x.shape[1]), axis=0)


class Halo:
    def __init__(self, me, devices, out, got, send_sem, recv_sem):
        self.out, self.got, self.send_sem, self.recv_sem = out, got, send_sem, recv_sem
        self.right = lax.rem(me + 1, devices)
        self.left = lax.rem(me + devices - 1, devices)

    def copies(self, c):
        return [
            pltpu.make_async_remote_copy(
                src_ref=self.out.at[c, way],
                dst_ref=self.got.at[c, way],
                send_sem=self.send_sem.at[c, way],
                recv_sem=self.recv_sem.at[c, way],
                device_id=(device,),
                device_id_type=pl.DeviceIdType.MESH,
            )
            for way, device in enumerate((self.right, self.left))
        ]

    def push(self, c, select, blocks):
        for u in range(UTT):
            edge = dot(select[...], blocks[u]).astype(BF16)
            self.out[c, 0, u] = edge[0:HALO]
            self.out[c, 1, u] = edge[HALO : 2 * HALO]
        for copy in self.copies(c):
            copy.start()

    def wait(self, c):
        for copy in self.copies(c):
            copy.wait_recv()

    def drain(self):
        for c in range(CHUNKS):
            for copy in self.copies(c):
                copy.wait_send()


def extend(ext, u, cols, low, high, row_id):
    for j in range(HALO):
        below = pltpu.roll(ext[u, OWN + (16 + j) * 8 : OWN + (17 + j) * 8, cols], 1, 0)
        ext[u, j * 8 : j * 8 + 8, cols] = jnp.where(row_id == 0, low[j : j + 1], below)
        above = pltpu.roll(ext[u, OWN + j * 8 : OWN + j * 8 + 8, cols], 7, 0)
        ext[u, (48 + j) * 8 : (49 + j) * 8, cols] = jnp.where(row_id == 7, high[j : j + 1], above)


def convolve(ext, u, cols, taps, offset):
    low, high = taps[0::2], taps[1::2]
    both = [a + b for a, b in zip(low, high)]

    def x(n):
        return ext[u, (n + offset) * 8 : (n + offset) * 8 + 8, cols]

    def product(weights, source, start, first):
        acc = list(start)
        for n in range(first, first + 23):
            value = source(n)
            for p in range(8):
                m = n - first - p
                if 0 <= m < 16:
                    term = weights[m] * value
                    acc[p] = term if acc[p] is None else acc[p] + term
        return acc

    for first in (0, 8):
        shared = product(both, lambda n: x(2 * n + 1), [None] * 8, first)
        even = product(low, lambda n: x(2 * n) - x(2 * n + 1), shared, first)
        odd = product(high, lambda n: x(2 * n + 2) - x(2 * n + 1), shared, first)
        yield 2 * first, [v for pair in zip(even, odd) for v in pair]


def whole_kernel(n_dev, x_hbm, lng_ref, win_hbm, ker_ref, bng_ref, bnb_ref, wout_hbm, cot_hbm,
                 out_hbm, din_hbm, dw_ref, dk_ref, dbn_ref, *scratch):
    s = dict(zip([name for name, _ in SCRATCH], scratch))
    me = lax.axis_index("seq")
    local = s["local_sem"]
    load_x = [pltpu.make_async_copy(x_hbm.at[u], s["x_raw"].at[u], local.at[u]) for u in range(UTT)]
    load_cot = pltpu.make_async_copy(cot_hbm, s["cot_raw"], local.at[2])
    load_out = pltpu.make_async_copy(wout_hbm, s["w_out"], local.at[3])

    def load_in(c):
        found = []
        for side in range(2):
            cols = pl.ds(pl.multiple_of(side * D + c * CHUNK, CHUNK), CHUNK)
            found.append(
                pltpu.make_async_copy(win_hbm.at[:, cols], s["w_in"].at[:, cols], s["win_sem"].at[c, side])
            )
        return found

    for copy in load_x:
        copy.start()
    vec = s["vec"]
    for row, ref in enumerate((lng_ref, bng_ref, bnb_ref)):
        vec[row : row + 1, :] = ref[...].reshape(1, D)
    net = Net(me, s["send_sem"], s["recv_sem"])
    halo1 = Halo(me, n_dev, s["h_out1"], s["h_got1"], s["h_send1"], s["h_recv1"])
    halo2 = Halo(me, n_dev, s["h_out2"], s["h_got2"], s["h_send2"], s["h_recv2"])

    entered = greet(me, AXES, (halo1.left, halo1.right))
    perm, eye, select = s["perm"], s["eye"], s["select"]
    r0 = lax.broadcasted_iota(jnp.int32, (256, 256), 0)
    r1 = lax.broadcasted_iota(jnp.int32, (256, 256), 1)
    perm[...] = jnp.where(frame_of(r0) == r1, 1.0, 0.0).astype(BF16)
    eye[...] = jnp.where(r0 == r1, 1.0, 0.0).astype(BF16)
    q0 = lax.broadcasted_iota(jnp.int32, (32, 256), 0)
    q1 = lax.broadcasted_iota(jnp.int32, (32, 256), 1)
    edge_frame = jnp.where(q0 < HALO, FRAMES_DEV - HALO + q0, q0 - HALO)
    select[...] = jnp.where(frame_of(q1) == edge_frame, 1.0, 0.0).astype(BF16)
    row_id = lax.broadcasted_iota(jnp.int32, (8, 128), 0)

    x_p, normed, mu_ref, rstd_ref = s["x_p"], s["bf"], s["mu"], s["rstd"]
    for copy in load_x:
        copy.wait()
    for c in range(CHUNKS):
        for copy in load_in(c):
            copy.start()

    def permute(c, carry):
        cols = span(c, CHUNK)
        for u in range(UTT):
            x_p[u * 256 : u * 256 + 256, cols] = dot(perm[...], s["x_raw"][u, :, cols]).astype(BF16)
        return carry

    lax.fori_loop(0, CHUNKS, permute, 0, unroll=2)

    def norm_tile(i, carry):
        rows = span(i, 16)
        x = x_p[rows, :].astype(F32)
        mean = jnp.mean(x, axis=-1, keepdims=True)
        gap = x - mean
        rstd = lax.rsqrt(jnp.mean(gap * gap, axis=-1, keepdims=True) + EPSILON)
        mu_ref[rows, :] = mean
        rstd_ref[rows, :] = rstd
        normed[rows, :] = (gap * rstd * vec[0:1, :]).astype(BF16)
        return carry

    lax.fori_loop(0, ROWS // 16, norm_tile, 0, unroll=4)
    entered()
    w_in, val, gs, ext_g, ext_d = s["w_in"], s["val"], s["gs"], s["ext_g"], s["ext_d"]

    def project(c, carry):
        for copy in load_in(c):
            copy.wait()
        project_chunk(c)
        return carry

    def project_chunk(c):
        cols = span(c, CHUNK)
        val[:, cols] = dot(normed[...], w_in[:, cols])
        gate_cols = pl.ds(pl.multiple_of(D + c * CHUNK, CHUNK), CHUNK)
        gs[:, cols] = dot(normed[...], w_in[:, gate_cols])
        blocks = []
        for u in range(UTT):
            rows = pl.ds(u * 256, 256)
            sig = jax.nn.sigmoid(gs[rows, cols])
            gs[rows, cols] = sig
            gated = (val[rows, cols] * sig).astype(BF16)
            ext_g[u, OWN : OWN + 256, cols] = gated.astype(F32)
            blocks.append(gated)
        halo1.push(c, select, blocks)

    lax.fori_loop(0, CHUNKS, project, 0)
    load_cot.start()
    load_out.start()

    def halo_rows(halo, c, u, lane):
        low = halo.got[c, 0, u, :, lane : lane + 128].astype(F32)
        high = halo.got[c, 1, u, :, lane : lane + 128].astype(F32)
        return jnp.where(me == 0, 0.0, low), jnp.where(me == n_dev - 1, 0.0, high)

    conv, stat = s["conv"], s["stat"]

    def taps_of(cols):
        return [jnp.broadcast_to(ker_ref[k : k + 1, cols], (8, 128)) for k in range(K)]

    def conv_only(c, carry):
        halo1.wait(c)
        conv_chunk(c)
        return carry

    def conv_chunk(c):
        for half in range(2):
            cols = pl.ds(pl.multiple_of(c * CHUNK + half * 128, 128), 128)
            taps = taps_of(cols)
            total = jnp.zeros((8, 128), F32)
            for u in range(UTT):
                low, high = halo_rows(halo1, c, u, half * 128)
                extend(ext_g, u, cols, low, high, row_id)
                for base, acc in convolve(ext_g, u, cols, taps, 1):
                    for o in range(16):
                        conv[pl.ds(u * 256 + (base + o) * 8, 8), cols] = acc[o]
                        total = total + acc[o]
            mean = jnp.sum(total, axis=0, keepdims=True) * (1.0 / ROWS)
            gap = conv[:, cols] - mean
            stat[0:1, cols] = mean
            stat[1:2, cols] = jnp.sum(fold(gap * gap), axis=0, keepdims=True)

    wide = (slice(0, HALF), slice(HALF, D))
    ar1 = [Reduce(net, True, s["cur"].at[h], s["got"].at[h]) for h in range(2)]
    ar2 = [Reduce(net, False, s["cur"].at[2 + h], s["got"].at[2 + h]) for h in range(2)]
    lax.fori_loop(0, 3, conv_only, 0)
    ar1[0].start(stat[:, wide[0]])
    lax.fori_loop(3, 4, conv_only, 0)
    ar1[0].step()
    lax.fori_loop(4, CHUNKS, conv_only, 0)
    ar1[0].step()
    ar1[1].start(stat[:, wide[1]])
    load_cot.wait()
    cot_p, cot_t, w_out = s["cot_p"], s["cot_t"], s["w_out"]

    def turn(c, carry):
        cols = span(c, CHUNK)
        for u in range(UTT):
            cot_p[u * 256 : u * 256 + 256, cols] = dot(perm[...], s["cot_raw"][u, :, cols]).astype(BF16)
        cot_t[cols, :] = dot_t(eye[...], cot_p[:, cols]).astype(BF16)
        return carry

    lax.fori_loop(0, CHUNKS, turn, 0, unroll=2)
    ar1[1].step()
    ar1[0].step()
    load_out.wait()

    def act_grad(c, carry):
        cols = span(c, CHUNK)
        res = dot(cot_p[...], w_out[:, cols])
        for u in range(UTT):
            ext_d[u, OWN : OWN + 256, cols] = res[u * 256 : u * 256 + 256]
        return carry

    total_rows = float(ROWS * n_dev)
    coef = s["coef"]

    def use_stats(h):
        stats = ar1[h].take()
        coef[0:1, wide[h]] = stats[0:1]
        coef[1:2, wide[h]] = lax.rsqrt(stats[1:2] * (1.0 / total_rows) + EPSILON)

    lax.fori_loop(0, CHUNKS // 2, act_grad, 0)
    ar1[1].step()
    lax.fori_loop(CHUNKS // 2, CHUNKS, act_grad, 0)
    use_stats(0)
    act = s["bf"]

    def bn_block(cb, carry):
        cols = span(cb, 128)
        mean, rstd = coef[0:1, cols], coef[1:2, cols]
        gain, bias = vec[1:2, cols], vec[2:3, cols]
        sum_bias = jnp.zeros((8, 128), F32)
        sum_gain = jnp.zeros((8, 128), F32)
        for u in range(UTT):
            rows = pl.ds(u * 256, 256)
            xhat = (conv[rows, cols] - mean) * rstd
            bn = xhat * gain + bias
            sig = jax.nn.sigmoid(bn)
            conv[rows, cols] = xhat
            act[rows, cols] = (bn * sig).astype(BF16)
            d_bn = ext_d[u, OWN : OWN + 256, cols] * (sig + bn * sig * (1.0 - sig))
            ext_d[u, OWN : OWN + 256, cols] = d_bn
            sum_bias = sum_bias + fold(d_bn)
            sum_gain = sum_gain + fold(d_bn * xhat)
        stat[0:1, cols] = jnp.sum(sum_gain, axis=0, keepdims=True)
        stat[1:2, cols] = jnp.sum(sum_bias, axis=0, keepdims=True)
        return carry

    core = coord(me, "core")
    part_ref = s["part"]
    rs = Scatter(net, part_ref, *[s[name] for name in RS_NAMES])

    def weight_part(h, p):
        cols = pl.ds(pl.multiple_of(h * HALF + p * CHUNK, CHUNK), CHUNK)

        def weight_tile(m, carry):
            res = dot(cot_t[span(m, 384), :], act[:, cols])
            for j in range(16):
                piece = res[j * 24 : j * 24 + 24]
                piece = jnp.concatenate([piece[:, 0:128], piece[:, 128:256]], axis=0).astype(BF16)
                part_ref[h, p, m, j // 4, j % 4] = piece
            return carry

        lax.fori_loop(0, 4, weight_tile, 0, unroll=2)

    saves = []

    def branch(n, carry):
        cols = span(n, CHUNK)
        res = dot_t(act[...], w_out[cols, :])
        s["out_p"][:, cols] = (x_p[:, cols].astype(F32) + res).astype(BF16)
        return carry

    def use_sums(h):
        sums = ar2[h].take()
        s["dbn_s"][:, wide[h]] = sums
        gain_row = vec[1:2, wide[h]]
        rstd_row = coef[1:2, wide[h]]
        coef[2:3, wide[h]] = rstd_row * gain_row
        coef[3:4, wide[h]] = rstd_row * (gain_row * sums[1:2] * (1.0 / total_rows))
        coef[4:5, wide[h]] = rstd_row * (gain_row * sums[0:1] * (1.0 / total_rows))

    lax.fori_loop(0, 6, bn_block, 0)
    ar1[1].step()
    ar2[0].start(stat[:, wide[0]])
    weight_part(0, 0)
    weight_part(0, 1)
    ar2[0].step()
    weight_part(0, 2)
    use_stats(1)
    lax.fori_loop(6, 12, bn_block, 0)
    ar2[0].step()
    ar2[1].start(stat[:, wide[1]])
    weight_part(1, 0)
    weight_part(1, 1)
    ar2[1].step()
    weight_part(1, 2)
    firsts = {p: rs.start(p) for p in (2, 1, 0)}
    lax.fori_loop(0, CHUNKS // 2, branch, 0)
    ar2[0].step()
    ar2[1].step()
    lax.fori_loop(CHUNKS // 2, CHUNKS, branch, 0)
    copy = pltpu.make_async_copy(s["out_p"], out_hbm, local.at[4])
    copy.start()
    saves.append(copy)
    use_sums(0)

    def conv_grad(c, carry):
        cols = span(c, CHUNK)
        blocks = []
        for u in range(UTT):
            d_bn = ext_d[u, OWN : OWN + 256, cols]
            xhat = conv[u * 256 : u * 256 + 256, cols]
            d_conv = d_bn * coef[2:3, cols] - coef[3:4, cols] - xhat * coef[4:5, cols]
            ext_d[u, OWN : OWN + 256, cols] = d_conv
            blocks.append(d_conv.astype(BF16))
        halo2.push(c, select, blocks)
        return carry

    dk_src = s["dk_src"]

    def kernel_grad(h):
        def tap_sums(n, carry):
            cols = pl.ds(pl.multiple_of(h * HALF + n * 128, 128), 128)
            for u in range(UTT):
                grads = [ext_d[u, OWN + i * 8 : OWN + i * 8 + 8, cols] for i in range(32)]
                for base, acc in convolve(ext_g, u, cols, grads, 1):
                    for part in range(2):
                        row = base // 8 + part
                        folded = jnp.concatenate(
                            [jnp.sum(a, axis=0, keepdims=True) for a in acc[part * 8 : part * 8 + 8]],
                            axis=0,
                        )
                        if u == 0:
                            dk_src[h, row, :, span(n, 128)] = folded
                        else:
                            dk_src[h, row, :, span(n, 128)] += folded
            return carry

        lax.fori_loop(0, HALF // 128, tap_sums, 0)

    lax.fori_loop(0, 3, conv_grad, 0)
    ar2[1].step()
    levels = {}
    for p in (2, 1, 0):
        rs.add_core(p, firsts[p])
        levels[p] = rs.send_level(p, 0)
    kernel_grad(0)
    use_sums(1)
    lax.fori_loop(3, CHUNKS, conv_grad, 0)

    dk = DKernel(net, dk_src, *[s[name] for name in DK_NAMES])
    kernel_grad(1)
    dk.start()
    grads = (s["d_proj0"], s["d_proj1"])

    def input_grad(c, d_proj):
        halo2.wait(c)
        for half in range(2):
            start = pl.multiple_of(c * CHUNK + half * 128, 128)
            cols = pl.ds(start, 128)
            taps = taps_of(cols)[::-1]
            lane = half * 128
            for u in range(UTT):
                low, high = halo_rows(halo2, c, u, lane)
                extend(ext_d, u, cols, low, high, row_id)
                for base, acc in convolve(ext_d, u, cols, taps, 0):
                    rows = pl.ds(u * 256 + base * 8, 128)
                    grad = jnp.concatenate(acc, axis=0)
                    sig = gs[rows, cols]
                    by_sig = grad * sig
                    d_proj[rows, lane : lane + 128] = by_sig.astype(BF16)
                    d_proj[rows, CHUNK + lane : CHUNK + lane + 128] = (
                        by_sig * val[rows, cols] * (1.0 - sig)
                    ).astype(BF16)

    def frame_grad(c, d_proj):
        cols = span(c, CHUNK)
        gate_cols = pl.ds(pl.multiple_of(D + c * CHUNK, CHUNK), CHUNK)
        for n in range(CHUNKS):
            rows = slice(n * CHUNK, n * CHUNK + CHUNK)
            weights = jnp.concatenate([w_in[rows, cols], w_in[rows, gate_cols]], axis=1)
            if c == 0:
                conv[:, rows] = dot_t(d_proj[...], weights)
            else:
                conv[:, rows] += dot_t(d_proj[...], weights)

    def pair(c):
        input_grad(c + 1, grads[1 - c % 2])
        frame_grad(c, grads[c % 2])

    def next_level(level):
        found = {}
        for p in (2, 1, 0):
            rs.add_level(p, level, levels[p])
            found[p] = rs.send_level(p, level + 1)
        return found

    input_grad(0, grads[0])
    dk.to_x()
    pair(0)
    dk.to_z()
    pair(1)
    levels = next_level(0)
    dk.to_y()
    pair(2)
    pair(3)
    dk.gather_x()
    levels = next_level(1)
    input_grad(5, grads[1])
    halo1.drain()
    halo2.drain()
    frame_grad(4, grads[0])
    dk.gather_core()
    frame_grad(5, grads[1])
    rs.exchange([rs.add_level(p, 2, levels[p]) for p in range(3)])

    def leave(src, dst, sem):
        copy = pltpu.make_async_copy(src, dst, local.at[sem])
        copy.start()
        saves.append(copy)

    leave(s["dbn_s"], dbn_ref, 10)

    def norm_grad(u):
        def tile(i, carry):
            rows = pl.ds(pl.multiple_of(u * 128 + i * 16, 16), 16)
            d_hat = conv[rows, :] * vec[0:1, :]
            rstd = rstd_ref[rows, :]
            hat = (x_p[rows, :].astype(F32) - mu_ref[rows, :]) * rstd
            m1 = jnp.mean(d_hat, axis=-1, keepdims=True)
            m2 = jnp.mean(d_hat * hat, axis=-1, keepdims=True)
            grad = rstd * (d_hat - m1 - hat * m2)
            act[rows, :] = (cot_p[rows, :].astype(F32) + grad).astype(BF16)
            return carry

        lax.fori_loop(0, 8, tile, 0, unroll=4)
        rows_u = pl.ds(u * 128, 128)
        copy = pltpu.make_async_copy(act.at[rows_u], din_hbm.at[rows_u], local.at[6 + u])
        copy.start()
        saves.append(copy)

    norm_grad(0)
    norm_grad(1)
    norm_grad(2)
    rs.finish(s["dw_s"])
    leave(s["dw_s"], dw_ref, 5)
    norm_grad(3)
    dk.finish(s["dk_s"])
    leave(s["dk_s"], dk_ref, 11)
    net.drain()
    for copy in saves:
        copy.wait()


RS_NAMES = ["got_core", "s1", "got1", "s2", "got2", "s3", "got3", "tail", "got_tail"]
DK_NAMES = ["dk%d" % i for i in range(len(DK_SCRATCH))]
VM = pltpu.VMEM
SCRATCH = [
    ("x_raw", VM((UTT, 256, D), BF16)),
    ("w_in", VM((D, 2 * D), BF16)),
    ("cot_raw", VM((UTT, 256, D), BF16)),
    ("w_out", VM((D, D), BF16)),
    ("perm", VM((256, 256), BF16)),
    ("win_sem", pltpu.SemaphoreType.DMA((CHUNKS, 2))),
    ("vec", VM((3, D), F32)),
    ("out_p", VM((ROWS, D), BF16)),
    ("eye", VM((256, 256), BF16)),
    ("select", VM((32, 256), BF16)),
    ("x_p", VM((ROWS, D), BF16)),
    ("bf", VM((ROWS, D), BF16)),
    ("mu", VM((ROWS, 1), F32)),
    ("rstd", VM((ROWS, 1), F32)),
    ("val", VM((ROWS, D), F32)),
    ("gs", VM((ROWS, D), F32)),
    ("ext_g", VM((UTT, 512, D), F32)),
    ("ext_d", VM((UTT, 512, D), F32)),
    ("conv", VM((ROWS, D), F32)),
    ("dbn_s", VM((2, D), F32)),
    ("dk_s", VM((K, D), F32)),
    ("dw_s", VM((D // 128, D), F32)),
    ("stat", VM((2, D), F32)),
    ("coef", VM((8, D), F32)),
    ("cot_p", VM((ROWS, D), BF16)),
    ("cot_t", VM((D, ROWS), BF16)),
    ("d_proj0", VM((ROWS, 2 * CHUNK), BF16)),
    ("d_proj1", VM((ROWS, 2 * CHUNK), BF16)),
    ("part", VM((2, 3, 4, 4, 4, 48, 128), BF16)),
    ("h_out1", VM((CHUNKS, 2, UTT, HALO, CHUNK), BF16)),
    ("h_got1", VM((CHUNKS, 2, UTT, HALO, CHUNK), BF16)),
    ("h_out2", VM((CHUNKS, 2, UTT, HALO, CHUNK), BF16)),
    ("h_got2", VM((CHUNKS, 2, UTT, HALO, CHUNK), BF16)),
    ("cur", VM((4, 4, 2, HALF), F32)),
    ("got", VM((4, 10, 2, HALF), F32)),
    ("dk_src", VM((2, 4, 8, HALF), F32)),
]
SCRATCH += list(zip(RS_NAMES, RS_SCRATCH)) + list(zip(DK_NAMES, DK_SCRATCH))
SCRATCH += [
    ("local_sem", pltpu.SemaphoreType.DMA((12,))),
    ("send_sem", pltpu.SemaphoreType.DMA((88,))),
    ("recv_sem", pltpu.SemaphoreType.DMA((88,))),
    ("h_send1", pltpu.SemaphoreType.DMA((CHUNKS, 2))),
    ("h_recv1", pltpu.SemaphoreType.DMA((CHUNKS, 2))),
    ("h_send2", pltpu.SemaphoreType.DMA((CHUNKS, 2))),
    ("h_recv2", pltpu.SemaphoreType.DMA((CHUNKS, 2))),
]


def finish_kernel(out_p, din_p, dw, dk, dbn, out_ref, din_ref, dw_out, dk_out, gain_out, bias_out, perm_t):
    @pl.when((pl.program_id(0) == 0) & (pl.program_id(1) == 0))
    def _():
        r0 = lax.broadcasted_iota(jnp.int32, (256, 256), 0)
        r1 = lax.broadcasted_iota(jnp.int32, (256, 256), 1)
        perm_t[...] = jnp.where(frame_of(r1) == r0, 1.0, 0.0).astype(BF16)
        dw_out[...] = dw[...]
        dk_out[...] = dk[...]
        gain_out[...] = dbn[0:1, :].reshape(D)
        bias_out[...] = dbn[1:2, :].reshape(D)

    out_ref[0] = dot(perm_t[...], out_p[...]).astype(BF16)
    din_ref[0] = dot(perm_t[...], din_p[...]).astype(BF16)


def on_device(inputs, ln_gain, w_in, kernel, bn_gain, bn_bias, w_out, cotangent):
    any_spec = pl.BlockSpec(memory_space=pl.ANY)
    vmem_spec = pl.BlockSpec(memory_space=pltpu.VMEM)
    flat = jax.ShapeDtypeStruct((ROWS, D), BF16)
    out_p, din_p, dw, dk, dbn = pl.pallas_call(
        functools.partial(whole_kernel, lax.axis_size("seq")),
        out_shape=(
            flat,
            flat,
            jax.ShapeDtypeStruct((D // 128, D), F32),
            jax.ShapeDtypeStruct((K, D), F32),
            jax.ShapeDtypeStruct((2, D), F32),
        ),
        in_specs=[any_spec, vmem_spec, any_spec, vmem_spec, vmem_spec, vmem_spec, any_spec, any_spec],
        out_specs=[any_spec] * 5,
        scratch_shapes=[spec for _, spec in SCRATCH],
        compiler_params=pltpu.CompilerParams(
            collective_id=0, has_side_effects=True, vmem_limit_bytes=67043328
        ),
    )(inputs, ln_gain, w_in, kernel, bn_gain, bn_bias, w_out, cotangent)

    def whole(shape):
        return pl.BlockSpec(shape, lambda u, c: (0,) * len(shape))

    wide = D // 2
    rows_spec = pl.BlockSpec((256, wide), lambda u, c: (u, c))
    block_spec = pl.BlockSpec((1, 256, wide), lambda u, c: (u, 0, c))
    full = jax.ShapeDtypeStruct((UTT, FRAMES_DEV, D), BF16)
    return pl.pallas_call(
        finish_kernel,
        grid=(UTT, 2),
        out_shape=(
            full,
            full,
            jax.ShapeDtypeStruct((D // 128, D), F32),
            jax.ShapeDtypeStruct((K, D), F32),
            jax.ShapeDtypeStruct((D,), F32),
            jax.ShapeDtypeStruct((D,), F32),
        ),
        in_specs=[rows_spec, rows_spec, whole((D // 128, D)), whole((K, D)), whole((2, D))],
        out_specs=[block_spec, block_spec, whole((D // 128, D)), whole((K, D)), whole((D,)), whole((D,))],
        scratch_shapes=[pltpu.VMEM((256, 256), BF16)],
    )(out_p, din_p, dw, dk, dbn)


def solution(mesh):
    return jax.shard_map(
        on_device,
        mesh=mesh,
        in_specs=(P(None, "seq", None), P(), P(), P(), P(), P(), P(), P(None, "seq", None)),
        out_specs=(P(None, "seq", None), P(None, "seq", None), P("seq", None), P(), P(), P()),
        check_vma=False,
    )
```
